32 devices in a mesh: dp: 8 (over z, y), tensor: 4 (over x, core).
Axes of the slice: x: 2, y: 2, z: 4, core: 2. Of those that a mesh axis runs over, the one named last changes fastest.
Arguments:
- inputs: bfloat16 [8, 1024, 1024], P('dp'), may hold values from -6 to 6
- memory: bfloat16 [8, 1024, 1024], P('dp'), may hold values from -6 to 6
- memory_positions: int32 [8, 1024], P('dp'), may hold values from -2048 to -1, as said below
- value_routes: int32 [8, 2048, 4, 2], P('dp', None, 'tensor'), may hold values from 0 to 4, all different within a row
- output_routes: int32 [8, 1024, 4, 2], P('dp', None, 'tensor'), may hold values from 0 to 4, all different within a row
- norm_gains: float32 [2, 1024], replicated, may hold values from 0.5 to 1.5
- norm_biases: float32 [2, 1024], replicated, may hold values from -1.75 to 1.75
- query_weight: bfloat16 [1024, 448], P(None, 'tensor'), may hold values from -0.1875 to 0.1875
- key_weight: bfloat16 [1024, 448], P(None, 'tensor'), may hold values from -0.1875 to 0.1875
- value_weight: bfloat16 [1024, 2240], P(None, 'tensor'), may hold values from -0.1875 to 0.1875
- value_router: bfloat16 [1024, 20], P(None, 'tensor'), may hold values from -0.125 to 0.125
- output_router: bfloat16 [1024, 20], P(None, 'tensor'), may hold values from -0.125 to 0.125
- output_weight: bfloat16 [2240, 1024], P('tensor'), may hold values from -8 to 8
- position_weight: bfloat16 [1024, 448], P(None, 'tensor'), may hold values from -0.1875 to 0.1875
- content_bias: float32 [448], P('tensor'), may hold values from -3 to 3
- position_bias: float32 [448], P('tensor'), may hold values from -3 to 3
- up_weight: bfloat16 [1024, 4096], P(None, 'tensor'), may hold values from -0.1875 to 0.1875
- down_weight: bfloat16 [4096, 1024], P('tensor'), may hold values from -0.09375 to 0.09375
- cotangent: bfloat16 [8, 1024, 1024], P('dp'), may hold values from -6 to 6
Outputs:
- output: bfloat16 [8, 1024, 1024], P('dp')
- grad_inputs: bfloat16 [8, 1024, 1024], P('dp')
- grad_norm_gains: float32 [2, 1024], P(None, 'tensor')
- grad_norm_biases: float32 [2, 1024], P(None, 'tensor')
- grad_query_weight: float32 [1024, 448], P(None, 'tensor')
- grad_key_weight: float32 [1024, 448], P(None, 'tensor')
- grad_value_weight: float32 [1024, 2240], P(None, 'tensor')
- grad_value_router: float32 [1024, 20], P(None, 'tensor')
- grad_output_router: float32 [1024, 20], P(None, 'tensor')
- grad_output_weight: float32 [2240, 1024], P('tensor')
- grad_position_weight: float32 [1024, 448], P(None, 'tensor')
- grad_content_bias: float32 [448], P('tensor')
- grad_position_bias: float32 [448], P('tensor')
- grad_up_weight: float32 [1024, 4096], P(None, 'tensor')
- grad_down_weight: float32 [4096, 1024], P('tensor')
- expert_counts: int32 [2, 20], P(None, 'tensor')
The draws below stay inside these ranges and needn't reach their ends.
Inputs may be any that keep to these rules, and one draw needn't show every extreme that they name: `memory_positions`: strictly increasing in every sequence; the first is -2048 and the last is -1. `value_routes`: each row names two different experts of its head. `output_routes`: each token names two different experts of its head.
All inputs are finite; a program needn't handle non-finite values.
Results may differ from the reference program's by a relative error of at most 0.014.
The reference program's roundings to bfloat16 on the way count: a program that leaves them out, or rounds other values in their place, can miss the bound.
Values may be sent and summed in bfloat16 or wider, within the bound.
No kernel may reach another device: no remote copies, remote signals or barrier semaphores. Data moves between devices by JAX's collectives and lax.ppermute only.
A program may use at most 192 MiB of HBM per device.

```python
import math
import jax
import jax.numpy as jnp
from jax import lax

D = 1024
HEADS = 4
DH = 112
EXP = 5
FF = 4096
LEN = 1024
MEM = 1024
QBLOCK = 512
SEQS = 8
PD = 1024


def draw_memory_positions(key, part):

    def one_sequence(seq_key):
        chosen = jax.random.permutation(seq_key, 2 * MEM - 2)[:MEM - 2]
        middle = jnp.sort(chosen).astype(jnp.int32) - (2 * MEM - 1)
        return jnp.concatenate([jnp.full((1,), -2 * MEM, jnp.int32), middle, jnp.full((1,), -1, jnp.int32)])
    return jax.vmap(one_sequence)(jax.random.split(key, SEQS))


def steps_of(rng, dims, pieces, smallest, largest):
    factor_of, own = 1.0, jax.random.fold_in(rng, 6)
    for position, parts in pieces:
        steps = jnp.exp(jax.random.uniform(jax.random.fold_in(own, position), (parts,), jnp.float32, smallest / len(pieces), largest / len(pieces)))
        factor_of = factor_of * jnp.repeat(steps, dims[position] // parts).reshape([-1 if axis == position else 1 for axis in range(len(dims))])
    return factor_of


def picks_of(own_key, rows, amount, top, lift):
    order = jax.random.permutation(jax.random.fold_in(own_key, 1), amount)
    boost = order
    for power in range(3):
        boost = boost * boost // amount
    boost = boost * lift // amount
    chance = jax.random.randint(jax.random.fold_in(own_key, 2), (rows, amount), 0, 4096) + boost
    holders = jax.random.permutation(jax.random.fold_in(own_key, 3), rows)[jnp.arange(amount) % rows]
    chance = jnp.where(jnp.arange(rows)[:, None] == holders[None, :], 1 << 14, chance)
    priority = chance * amount + jnp.arange(amount)
    return lax.top_k(priority.astype(jnp.int32), top)[1].astype(jnp.int32)


def scatter_about(stream_key, extent, scale, limit, shards=(), kind=jnp.bfloat16):
    entries = jax.random.normal(stream_key, extent, jnp.float32) * scale
    if len(shards) > 0:
        entries = steps_of(stream_key, extent, shards, -0.22, 0.18) * entries
    return jnp.clip(entries, min=-limit, max=limit).astype(kind)


def setup_inputs(seed: int = 0) -> dict:
    keys = jax.random.split(jax.random.key(seed), 20)
    return {
        "inputs": scatter_about(keys[0], (SEQS, LEN, D), 1.0, 6.0, ((0, 8),)),
        "memory": scatter_about(keys[1], (SEQS, MEM, D), 1.0, 6.0, ((0, 8),)),
        "memory_positions": draw_memory_positions(jax.random.fold_in(keys[19], 71), 0),
        "value_routes": picks_of(keys[3], SEQS * (MEM + LEN) * HEADS, EXP, 2, 3276).reshape((SEQS, MEM + LEN, HEADS, 2)),
        "output_routes": picks_of(keys[4], SEQS * LEN * HEADS, EXP, 2, 3276).reshape((SEQS, LEN, HEADS, 2)),
        "norm_gains": jnp.clip(1.0 + 0.1 * jax.random.normal(keys[5], (2, D), jnp.float32), 0.5, 1.5),
        "norm_biases": scatter_about(keys[6], (2, D), 0.3, 1.75, (), jnp.float32),
        "query_weight": scatter_about(keys[7], (D, HEADS * DH), D ** -0.5, 0.1875, ((1, 4),)),
        "key_weight": scatter_about(keys[8], (D, HEADS * DH), D ** -0.5, 0.1875, ((1, 4),)),
        "value_weight": scatter_about(keys[9], (D, HEADS * EXP * DH), D ** -0.5, 0.1875, ((1, 4),)),
        "value_router": scatter_about(keys[10], (D, HEADS * EXP), (2 * D) ** -0.5, 0.125, ((1, 4),)),
        "output_router": scatter_about(keys[11], (D, HEADS * EXP), (2 * D) ** -0.5, 0.125, ((1, 4),)),
        "output_weight": scatter_about(keys[12], (HEADS * EXP * DH, D), 1.5, 8.0, ((0, 4),)),
        "position_weight": scatter_about(keys[13], (PD, HEADS * DH), PD ** -0.5, 0.1875, ((1, 4),)),
        "content_bias": scatter_about(keys[14], (HEADS * DH,), 0.5, 3.0, ((0, 4),), jnp.float32),
        "position_bias": scatter_about(keys[15], (HEADS * DH,), 0.5, 3.0, ((0, 4),), jnp.float32),
        "up_weight": scatter_about(keys[16], (D, FF), D ** -0.5, 0.1875, ((1, 4),)),
        "down_weight": scatter_about(keys[17], (FF, D), FF ** -0.5, 0.09375, ((0, 4),)),
        "cotangent": scatter_about(keys[18], (SEQS, LEN, D), 1.0, 6.0, ((0, 8),)),
    }


NORM_EPSILON = 1e-05
GELU_SCALE = 0.7978845608028654
GELU_CUBIC = 0.044715
HIGH = lax.Precision.HIGHEST

@jax.custom_vjp
def low(v):
    return lax.optimization_barrier(v.astype(jnp.bfloat16)).astype(jnp.float32)

@jax.custom_vjp
def low_back(v):
    return v

def low_keep(v):
    return (low(v), None)

def low_pass(kept, grad):
    return (grad,)

def back_keep(v):
    return (v, None)

def back_low(kept, grad):
    return (low(grad),)
low.defvjp(low_keep, low_pass)
low_back.defvjp(back_keep, back_low)

def matmul(left, right):
    return jnp.dot(left, right, precision=HIGH, preferred_element_type=jnp.float32)

def layer_norm(values, gain, bias):
    average = lax.optimization_barrier(jnp.mean(values, axis=-1, keepdims=True))
    centered = values - average
    spread = lax.optimization_barrier(jnp.mean(centered * centered, axis=-1, keepdims=True))
    return centered * lax.rsqrt(spread + NORM_EPSILON) * gain + bias

def gelu_value(values):
    argument = GELU_SCALE * (values + GELU_CUBIC * values * values * values)
    return 0.5 * values * (1.0 + jnp.tanh(argument))

def choose_mask(routes):
    expert_ids = jnp.arange(EXP, dtype=jnp.int32)
    return lax.optimization_barrier(jnp.sum((routes[..., None] == expert_ids).astype(jnp.float32), axis=-2))

def frequencies():
    return jnp.exp(jnp.arange(PD // 2, dtype=jnp.float32) * (-2.0 * math.log(10000.0) / PD))

def attend_block(content_piece, position_piece, first_row, keys_low, pos_keys, values_low):
    scores = jnp.einsum('ihd,jhd->hij', content_piece, keys_low, precision=HIGH)
    scores = scores + jnp.einsum('ihp,jp->hij', position_piece, pos_keys, precision=HIGH)
    scores = low_back(scores * DH ** (-0.5))
    row_index = first_row + jnp.arange(QBLOCK, dtype=jnp.int32)[:, None]
    col_index = jnp.arange(MEM + LEN, dtype=jnp.int32)[None, :]
    visible = (col_index < MEM) | (col_index - MEM <= row_index)
    scores = jnp.where(visible[None], scores, -jnp.inf)
    weights = low(jax.nn.softmax(scores, axis=-1))
    return jnp.einsum('hij,jhd->ihd', weights, values_low, precision=HIGH)

def forward(tokens, params, remembered, positions, value_picks, output_picks):
    norm_gains, norm_biases, query_weight, key_weight, value_weight, value_router, output_router, output_weight, position_weight, content_bias, position_bias, up_weight, down_weight = params
    all_rows = jnp.concatenate([remembered, tokens], axis=0)
    normed = low(layer_norm(all_rows, norm_gains[0], norm_biases[0]))
    current = normed[MEM:]
    query = low_back(matmul(current, query_weight)).reshape(LEN, HEADS, DH)
    keys_low = low(low_back(matmul(normed, key_weight))).reshape(MEM + LEN, HEADS, DH)
    expert_values = low_back(matmul(normed, value_weight)).reshape(MEM + LEN, HEADS, EXP, DH)
    value_logit = low_back(matmul(normed, value_router)).reshape(MEM + LEN, HEADS, EXP)
    value_gate = jax.nn.sigmoid(value_logit) * choose_mask(value_picks)
    values_low = low(lax.optimization_barrier(jnp.sum(value_gate[..., None] * expert_values, axis=2)))
    content_query = low(query + content_bias.reshape(HEADS, DH))
    bias_query = low(query + position_bias.reshape(HEADS, DH))
    relative = low_back(jnp.einsum('thd,phd->thp', bias_query, position_weight.reshape(PD, HEADS, DH), precision=HIGH))
    omega = frequencies()
    query_angle = jnp.arange(LEN, dtype=jnp.float32)[:, None] * omega
    query_sin = jnp.sin(query_angle)[:, None, :]
    query_cos = jnp.cos(query_angle)[:, None, :]
    rel_sin = relative[..., :PD // 2]
    rel_cos = relative[..., PD // 2:]
    pos_query = low(jnp.concatenate([rel_sin * query_sin + rel_cos * query_cos, rel_cos * query_sin - rel_sin * query_cos], axis=-1))
    key_angle = jnp.concatenate([positions.astype(jnp.float32), jnp.arange(LEN, dtype=jnp.float32)])[:, None] * omega
    pos_keys = low(jnp.concatenate([jnp.cos(key_angle), jnp.sin(key_angle)], axis=-1))
    nblocks = LEN // QBLOCK
    firsts = jnp.arange(nblocks, dtype=jnp.int32) * QBLOCK
    block_call = jax.checkpoint(attend_block)
    attended = lax.map(lambda element: block_call(element[0], element[1], element[2], keys_low, pos_keys, values_low), (content_query.reshape(nblocks, QBLOCK, HEADS, DH), pos_query.reshape(nblocks, QBLOCK, HEADS, PD), firsts))
    attended = low(low_back(attended.reshape(LEN, HEADS, DH)))
    output_logit = low_back(matmul(current, output_router)).reshape(LEN, HEADS, EXP)
    output_gate = jax.nn.sigmoid(output_logit) * choose_mask(output_picks)
    mixed = low(output_gate[..., None] * attended[:, :, None, :]).reshape(LEN, HEADS * EXP * DH)
    resid = tokens + low_back(matmul(mixed, output_weight))
    normed_two = low(layer_norm(resid, norm_gains[1], norm_biases[1]))
    upper = low_back(matmul(normed_two, up_weight))
    return resid + matmul(low(gelu_value(upper)), down_weight)

def reference(inputs, memory, memory_positions, value_routes, output_routes, norm_gains, norm_biases, query_weight, key_weight, value_weight, value_router, output_router, output_weight, position_weight, content_bias, position_bias, up_weight, down_weight, cotangent):
    params = tuple((weight.astype(jnp.float32) for weight in (norm_gains, norm_biases, query_weight, key_weight, value_weight, value_router, output_router, output_weight, position_weight, content_bias, position_bias, up_weight, down_weight)))

    def per_sequence(totals, element):
        sequence, remembered, positions, value_picks, output_picks, upstream = element

        def closure(tokens, weights):
            return forward(tokens, weights, remembered.astype(jnp.float32), positions, value_picks, output_picks)
        result, pullback = jax.vjp(closure, sequence.astype(jnp.float32), params)
        grad_tokens, grad_weights = pullback(upstream.astype(jnp.float32))
        totals = jax.tree.map(jnp.add, totals, grad_weights)
        return (totals, (result.astype(jnp.bfloat16), grad_tokens.astype(jnp.bfloat16)))
    zero_init = tuple((jnp.zeros_like(weight) for weight in params))
    grads, (results, grad_tokens) = lax.scan(per_sequence, zero_init, (inputs, memory, memory_positions, value_routes, output_routes, cotangent))
    expert_ids = jnp.arange(EXP, dtype=jnp.int32)
    value_count = lax.optimization_barrier(jnp.sum((value_routes[:, MEM:, :, :, None] == expert_ids).astype(jnp.int32), axis=(0, 1, 3)))
    output_count = lax.optimization_barrier(jnp.sum((output_routes[..., None] == expert_ids).astype(jnp.int32), axis=(0, 1, 3)))
    expert_counts = jnp.stack([value_count.reshape(-1), output_count.reshape(-1)])
    return (results, grad_tokens, grads[0], grads[1], grads[2], grads[3], grads[4], grads[5], grads[6], grads[7], grads[8], grads[9], grads[10], grads[11], grads[12], expert_counts)
```

```python
import math

import jax
import jax.numpy as jnp
from jax import lax
from jax.experimental import pallas as pl
from jax.experimental.pallas import tpu as pltpu
from jax.sharding import PartitionSpec as P

QBLOCK = 512


NORM_EPSILON = 1e-05
GELU_SCALE = 0.7978845608028654
GELU_CUBIC = 0.044715


def dot_first(left, right):
    return lax.dot_general(
        left, right, (((0,), (0,)), ((), ())), preferred_element_type=jnp.float32
    )


def dot_last(left, right):
    return lax.dot_general(
        left, right, (((1,), (1,)), ((), ())), preferred_element_type=jnp.float32
    )


def dot_plain(left, right):
    return jnp.dot(left, right, preferred_element_type=jnp.float32)


def norm_forward(values, gain, bias):
    average = jnp.mean(values, axis=-1, keepdims=True)
    centered = values - average
    spread = jnp.mean(centered * centered, axis=-1, keepdims=True)
    inverse = lax.rsqrt(spread + NORM_EPSILON)
    unit = centered * inverse
    return (unit * gain + bias, unit, inverse)


def norm_backward(upstream, unit, inverse, gain):
    grad_unit = upstream * gain
    return inverse * (
        grad_unit
        - jnp.mean(grad_unit, axis=-1, keepdims=True)
        - unit * jnp.mean(grad_unit * unit, axis=-1, keepdims=True)
    )


def gelu_value(values):
    argument = GELU_SCALE * (values + GELU_CUBIC * values * values * values)
    return 0.5 * values * (1.0 + jnp.tanh(argument))


def gelu_slope(values):
    tangent = jnp.tanh(GELU_SCALE * (values + GELU_CUBIC * values * values * values))
    return 0.5 * (1.0 + tangent) + 0.5 * values * (1.0 - tangent * tangent) * GELU_SCALE * (
        1.0 + 3.0 * GELU_CUBIC * values * values
    )


def selection(routes, experts):
    expert_ids = jnp.arange(experts, dtype=jnp.int32)
    return jnp.sum((routes[:, :, None] == expert_ids).astype(jnp.float32), axis=1)


def allowed(first_row, query_block, key_count, mem_count):
    row_index = first_row + jnp.arange(query_block, dtype=jnp.int32)[:, None]
    col_index = jnp.arange(key_count, dtype=jnp.int32)[None, :]
    return (col_index < mem_count) | (col_index - mem_count <= row_index)


def attend(query_cat, key_cat, values, query_block):
    length = query_cat.shape[0]
    key_count = key_cat.shape[0]
    score_scale = values.shape[1] ** (-0.5)
    nblocks = length // query_block
    firsts = jnp.arange(nblocks, dtype=jnp.int32) * query_block

    def one_block(element):
        query_piece, first_row = element
        scores = dot_last(query_piece, key_cat) * score_scale
        visible = allowed(first_row, query_block, key_count, key_count - length)
        scores = jnp.where(visible, scores, -jnp.inf)
        row_max = jnp.max(scores, axis=1, keepdims=True)
        raised = jnp.exp(scores - row_max)
        row_total = jnp.sum(raised, axis=1, keepdims=True)
        weights = (raised / row_total).astype(jnp.bfloat16)
        return (dot_plain(weights, values), row_max[:, 0] + jnp.log(row_total[:, 0]))

    result, logsum = lax.map(one_block, (query_cat.reshape(nblocks, query_block, -1), firsts))
    return (result.reshape(length, -1), logsum.reshape(length))


def attend_back(query_cat, key_cat, values, logsum, upstream, query_block):
    length = query_cat.shape[0]
    key_count = key_cat.shape[0]
    head_size = values.shape[1]
    score_scale = head_size ** (-0.5)
    nblocks = length // query_block
    firsts = jnp.arange(nblocks, dtype=jnp.int32) * query_block

    def block_step(state_pair, element):
        grad_keys, grad_values = state_pair
        query_piece, logsum_piece, upstream_piece, first_row = element
        scores = dot_last(query_piece, key_cat) * score_scale
        visible = allowed(first_row, query_block, key_count, key_count - length)
        weights = jnp.where(visible, jnp.exp(scores - logsum_piece[:, None]), 0.0)
        grad_weights = dot_last(upstream_piece, values)
        grad_values = grad_values + dot_first(weights.astype(jnp.bfloat16), upstream_piece)
        row_inner = jnp.sum(grad_weights * weights, axis=1, keepdims=True)
        grad_scores = (weights * (grad_weights - row_inner)).astype(jnp.bfloat16)
        grad_query = dot_plain(grad_scores, key_cat) * score_scale
        grad_keys = grad_keys + dot_first(grad_scores, query_piece[:, :head_size]) * score_scale
        return ((grad_keys, grad_values), grad_query)

    zero_init = jnp.zeros((key_count, head_size), jnp.float32)
    (grad_keys, grad_values), grad_query = lax.scan(
        block_step,
        (zero_init, zero_init),
        (
            query_cat.reshape(nblocks, query_block, -1),
            logsum.reshape(nblocks, query_block),
            upstream.reshape(nblocks, query_block, head_size),
            firsts,
        ),
    )
    return (grad_keys, grad_values, grad_query.reshape(length, -1))


def dp_bits():
    count = lax.axis_size("dp")
    bits = []
    bit = 1
    while bit < count:
        bits.append(bit)
        bit = bit * 2
    return bits


def relative_chunks(bits):
    count = 2 ** len(bits)
    order = []
    for place in range(count):
        value = 0
        for depth, bit in enumerate(bits):
            if place & (count >> (depth + 1)):
                value = value | bit
        order.append(value)
    return order


def move_chunks(source, order, me, dtype, gather):
    count = len(order)
    rows = source.shape[0] // count
    width = source.shape[1]
    table = jnp.bitwise_xor(jnp.array(order, jnp.int32), me)

    def body(table_ref, source_ref, out_ref):
        out_ref[...] = source_ref[...].astype(dtype)

    moved = lambda i, table_ref: (table_ref[i], 0)
    plain = lambda i, table_ref: (i, 0)
    return pl.pallas_call(
        body,
        out_shape=jax.ShapeDtypeStruct(source.shape, dtype),
        grid_spec=pltpu.PrefetchScalarGridSpec(
            num_scalar_prefetch=1,
            grid=(count,),
            in_specs=[pl.BlockSpec((rows, width), moved if gather else plain)],
            out_specs=pl.BlockSpec((rows, width), plain if gather else moved),
        ),
    )(table, source)


def dp_partner(bit):
    return [(i, i ^ bit) for i in range(lax.axis_size("dp"))]


def dp_sum(source, bits):
    me = lax.axis_index("dp")
    order = relative_chunks(bits)
    held = move_chunks(source, order, me, jnp.bfloat16, True)
    for bit in bits:
        half = held.shape[0] // 2
        got = lax.ppermute(held[half:], "dp", dp_partner(bit))
        held = (held[:half].astype(jnp.float32) + got.astype(jnp.float32)).astype(jnp.bfloat16)
    for bit in reversed(bits):
        got = lax.ppermute(held, "dp", dp_partner(bit))
        held = jnp.concatenate([held, got], axis=0)
    return move_chunks(held, order, me, jnp.float32, False)


def dp_sum_small(source):
    total = source
    for bit in dp_bits():
        total = total + lax.ppermute(total, "dp", dp_partner(bit))
    return total


def on_device(
    inputs,
    memory,
    memory_positions,
    value_routes,
    output_routes,
    norm_gains,
    norm_biases,
    query_weight,
    key_weight,
    value_weight,
    value_router,
    output_router,
    output_weight,
    position_weight,
    content_bias,
    position_bias,
    up_weight,
    down_weight,
    cotangent,
):
    count_seq, length, width = inputs.shape
    mem_count = memory.shape[1]
    key_count = mem_count + length
    head_size = query_weight.shape[1]
    experts = value_router.shape[1]
    pos_width = position_weight.shape[0]
    freq_count = pos_width // 2
    query_rows = count_seq * length
    share_rows = query_rows // lax.axis_size("tensor")
    row_start = lax.axis_index("tensor") * share_rows
    expert_ids = jnp.arange(experts, dtype=jnp.int32)
    value_picks = jnp.sum(
        (value_routes[:, mem_count:].reshape(-1)[:, None] == expert_ids).astype(jnp.int32), axis=0
    )
    output_picks = jnp.sum(
        (output_routes.reshape(-1)[:, None] == expert_ids).astype(jnp.int32), axis=0
    )
    local_counts = jnp.stack([value_picks, output_picks])
    all_rows = (
        jnp.concatenate([memory, inputs], axis=1)
        .astype(jnp.float32)
        .reshape(count_seq * key_count, width)
    )
    normed_full, unit_one, inverse_one = norm_forward(all_rows, norm_gains[0], norm_biases[0])
    normed = normed_full.astype(jnp.bfloat16)
    current = normed.reshape(count_seq, key_count, width)[:, mem_count:].reshape(query_rows, width)
    query = dot_plain(current, query_weight)
    content_query = (query + content_bias).astype(jnp.bfloat16)
    bias_query = (query + position_bias).astype(jnp.bfloat16)
    relative = dot_last(bias_query, position_weight).reshape(count_seq, length, pos_width)
    omega = jnp.exp(
        jnp.arange(freq_count, dtype=jnp.float32) * (-2.0 * math.log(10000.0) / pos_width)
    )
    current_pos = jnp.arange(length, dtype=jnp.float32)
    query_angle = current_pos[:, None] * omega
    query_sin = jnp.sin(query_angle)
    query_cos = jnp.cos(query_angle)
    rel_sin = relative[:, :, :freq_count]
    rel_cos = relative[:, :, freq_count:]
    pos_query = jnp.concatenate(
        [rel_sin * query_sin + rel_cos * query_cos, rel_cos * query_sin - rel_sin * query_cos],
        axis=2,
    ).astype(jnp.bfloat16)
    key_pos = jnp.concatenate(
        [memory_positions.astype(jnp.float32), jnp.broadcast_to(current_pos, (count_seq, length))],
        axis=1,
    )
    key_angle = key_pos[:, :, None] * omega
    pos_keys = jnp.concatenate([jnp.cos(key_angle), jnp.sin(key_angle)], axis=2).astype(
        jnp.bfloat16
    )
    keys_low = dot_plain(normed, key_weight).astype(jnp.bfloat16)
    expert_values = dot_plain(normed, value_weight).reshape(-1, experts, head_size)
    value_logit = dot_plain(normed, value_router)
    value_select = selection(value_routes.reshape(count_seq * key_count, -1), experts)
    value_sigmoid = jax.nn.sigmoid(value_logit)
    value_gate = value_sigmoid * value_select
    values_low = jnp.sum(value_gate[:, :, None] * expert_values, axis=1).astype(jnp.bfloat16)
    query_cat = jnp.concatenate(
        [content_query.reshape(count_seq, length, head_size), pos_query], axis=2
    )
    key_cat = jnp.concatenate([keys_low.reshape(count_seq, key_count, head_size), pos_keys], axis=2)
    values_seq = values_low.reshape(count_seq, key_count, head_size)
    attended, logsums = lax.map(
        lambda element: attend(element[0], element[1], element[2], QBLOCK),
        (query_cat, key_cat, values_seq),
    )
    attended_low = attended.reshape(query_rows, head_size).astype(jnp.bfloat16)
    attended_full = attended_low.astype(jnp.float32)
    output_logit = dot_plain(current, output_router)
    output_select = selection(output_routes.reshape(query_rows, -1), experts)
    output_sigmoid = jax.nn.sigmoid(output_logit)
    output_gate = output_sigmoid * output_select
    mixed = (
        (output_gate[:, :, None] * attended_full[:, None, :])
        .reshape(query_rows, experts * head_size)
        .astype(jnp.bfloat16)
    )
    attention_share = lax.psum_scatter(
        dot_plain(mixed, output_weight), "tensor", scatter_dimension=0, tiled=True
    )
    input_rows = inputs.reshape(query_rows, width)
    resid_share = (
        lax.dynamic_slice_in_dim(input_rows, row_start, share_rows, 0).astype(jnp.float32)
        + attention_share
    )
    normed_two_share, unit_two, inverse_two = norm_forward(
        resid_share, norm_gains[1], norm_biases[1]
    )
    normed_two = lax.all_gather(normed_two_share.astype(jnp.bfloat16), "tensor", axis=0, tiled=True)
    upper = dot_plain(normed_two, up_weight)
    activated = gelu_value(upper).astype(jnp.bfloat16)
    ffn_share = lax.psum_scatter(
        dot_plain(activated, down_weight).astype(jnp.bfloat16),
        "tensor",
        scatter_dimension=0,
        tiled=True,
    ).astype(jnp.float32)
    output_share = (resid_share + ffn_share).astype(jnp.bfloat16)
    output = lax.all_gather(output_share, "tensor", axis=0, tiled=True).reshape(
        count_seq, length, width
    )
    upstream = cotangent.reshape(query_rows, width)
    grad_down_local = dot_first(activated, upstream)
    grad_activated = dot_last(upstream, down_weight)
    grad_upper = (grad_activated * gelu_slope(upper)).astype(jnp.bfloat16)
    grad_up_local = dot_first(normed_two, grad_upper)
    grad_normed_two = lax.psum_scatter(
        dot_last(grad_upper, up_weight), "tensor", scatter_dimension=0, tiled=True
    )
    gain_two = jnp.sum(grad_normed_two * unit_two, axis=0)
    bias_two = jnp.sum(grad_normed_two, axis=0)
    upstream_share = lax.dynamic_slice_in_dim(upstream, row_start, share_rows, 0).astype(
        jnp.float32
    )
    grad_resid_share = upstream_share + norm_backward(
        grad_normed_two, unit_two, inverse_two, norm_gains[1]
    )
    grad_resid_low = lax.all_gather(
        grad_resid_share.astype(jnp.bfloat16), "tensor", axis=0, tiled=True
    )
    grad_output_weight = dot_first(mixed, grad_resid_low)
    grad_mixed = dot_last(grad_resid_low, output_weight).reshape(query_rows, experts, head_size)
    grad_attended = jnp.sum(output_gate[:, :, None] * grad_mixed, axis=1).astype(jnp.bfloat16)
    grad_output_gate = jnp.sum(grad_mixed * attended_full[:, None, :], axis=2)
    grad_output_logit = (
        grad_output_gate * output_select * output_sigmoid * (1.0 - output_sigmoid)
    ).astype(jnp.bfloat16)
    grad_output_router = dot_first(current, grad_output_logit)
    grad_keys, grad_values, grad_query_cat = lax.map(
        lambda element: attend_back(
            element[0], element[1], element[2], element[3], element[4], QBLOCK
        ),
        (
            query_cat,
            key_cat,
            values_seq,
            logsums,
            grad_attended.reshape(count_seq, length, head_size),
        ),
    )
    grad_content_query = grad_query_cat[:, :, :head_size].reshape(query_rows, head_size)
    grad_pos_sin = grad_query_cat[:, :, head_size : head_size + freq_count]
    grad_pos_cos = grad_query_cat[:, :, head_size + freq_count :]
    grad_relative = (
        jnp.concatenate(
            [
                grad_pos_sin * query_sin - grad_pos_cos * query_cos,
                grad_pos_sin * query_cos + grad_pos_cos * query_sin,
            ],
            axis=2,
        )
        .reshape(query_rows, pos_width)
        .astype(jnp.bfloat16)
    )
    grad_position_weight = dot_first(grad_relative, bias_query)
    grad_bias_query = dot_plain(grad_relative, position_weight)
    grad_content_bias = jnp.sum(grad_content_query, axis=0)
    grad_position_bias = jnp.sum(grad_bias_query, axis=0)
    grad_query = (grad_content_query + grad_bias_query).astype(jnp.bfloat16)
    grad_query_weight = dot_first(current, grad_query)
    grad_current = dot_last(grad_query, query_weight) + dot_last(grad_output_logit, output_router)
    grad_keys_low = grad_keys.reshape(-1, head_size).astype(jnp.bfloat16)
    grad_values_full = grad_values.reshape(-1, head_size)
    grad_expert = (
        (value_gate[:, :, None] * grad_values_full[:, None, :])
        .reshape(-1, experts * head_size)
        .astype(jnp.bfloat16)
    )
    grad_value_gate = jnp.sum(expert_values * grad_values_full[:, None, :], axis=2)
    grad_value_logit = (
        grad_value_gate * value_select * value_sigmoid * (1.0 - value_sigmoid)
    ).astype(jnp.bfloat16)
    grad_key_weight = dot_first(normed, grad_keys_low)
    grad_value_weight = dot_first(normed, grad_expert)
    grad_value_router = dot_first(normed, grad_value_logit)
    grad_all = (
        dot_last(grad_keys_low, key_weight)
        + dot_last(grad_expert, value_weight)
        + dot_last(grad_value_logit, value_router)
    ).reshape(count_seq, key_count, width)
    grad_memory_rows = grad_all[:, :mem_count]
    grad_current_rows = grad_all[:, mem_count:] + grad_current.reshape(count_seq, length, width)
    unit_rows = unit_one.reshape(count_seq, key_count, width)
    inverse_rows = inverse_one.reshape(count_seq, key_count, 1)
    gain_one = jnp.sum(grad_memory_rows * unit_rows[:, :mem_count], axis=(0, 1)) + jnp.sum(
        grad_current_rows * unit_rows[:, mem_count:], axis=(0, 1)
    )
    bias_one = jnp.sum(grad_memory_rows, axis=(0, 1)) + jnp.sum(grad_current_rows, axis=(0, 1))
    grad_normed_one = lax.psum_scatter(
        grad_current_rows.reshape(query_rows, width), "tensor", scatter_dimension=0, tiled=True
    )
    unit_current = lax.dynamic_slice_in_dim(
        unit_rows[:, mem_count:].reshape(query_rows, width), row_start, share_rows, 0
    )
    inverse_current = lax.dynamic_slice_in_dim(
        inverse_rows[:, mem_count:].reshape(query_rows, 1), row_start, share_rows, 0
    )
    grad_inputs_share = (
        grad_resid_share
        + norm_backward(grad_normed_one, unit_current, inverse_current, norm_gains[0])
    ).astype(jnp.bfloat16)
    grad_inputs = lax.all_gather(grad_inputs_share, "tensor", axis=0, tiled=True).reshape(
        count_seq, length, width
    )
    gain_full = jnp.stack([gain_one, gain_two])
    bias_full = jnp.stack([bias_one, bias_two])
    gain_shard, bias_shard = (
        lax.psum_scatter(gain_full, "tensor", scatter_dimension=1, tiled=True),
        lax.psum_scatter(bias_full, "tensor", scatter_dimension=1, tiled=True),
    )
    bits = dp_bits()
    grad_up = dp_sum(grad_up_local, bits)
    grad_down = dp_sum(grad_down_local, bits)
    out_rows = grad_output_weight.shape[0]
    out_pad = -out_rows % (8 * 2 ** len(bits))
    grad_out = dp_sum(jnp.pad(grad_output_weight, ((0, out_pad), (0, 0))), bits)[:out_rows]
    late = [
        grad_value_weight,
        grad_key_weight,
        grad_query_weight,
        grad_position_weight,
        grad_value_router,
        grad_output_router,
    ]
    widths = [piece.shape[1] for piece in late]
    late_pad = -sum(widths) % 128
    late_sum = dp_sum(
        jnp.concatenate(late + [jnp.zeros((width, late_pad), jnp.float32)], axis=1), bits
    )
    cut = []
    offset = 0
    for size in widths:
        cut.append(late_sum[:, offset : offset + size])
        offset = offset + size
    small = jnp.concatenate(
        [
            gain_shard.reshape(-1),
            bias_shard.reshape(-1),
            grad_content_bias,
            grad_position_bias,
            local_counts.astype(jnp.float32).reshape(-1),
        ]
    )
    small_size = small.shape[0]
    small = jnp.pad(small, (0, -small_size % 1024)).reshape(-1, 128)
    small = dp_sum_small(small).reshape(-1)
    share = gain_shard.size
    grad_gains = small[:share].reshape(gain_shard.shape)
    grad_biases = small[share : 2 * share].reshape(bias_shard.shape)
    offset = 2 * share
    content_sum = small[offset : offset + head_size]
    position_sum = small[offset + head_size : offset + 2 * head_size]
    offset = offset + 2 * head_size
    expert_counts = (
        small[offset : offset + 2 * experts].reshape(2, experts).astype(jnp.int32)
    )
    return (
        output,
        grad_inputs,
        grad_gains,
        grad_biases,
        cut[2],
        cut[1],
        cut[0],
        cut[4],
        cut[5],
        grad_out,
        cut[3],
        content_sum,
        position_sum,
        grad_up,
        grad_down,
        expert_counts,
    )


def solution(mesh):
    placed = (
        P("dp", None, None),
        P("dp", None, None),
        P("dp", None),
        P("dp", None, "tensor", None),
        P("dp", None, "tensor", None),
        P(),
        P(),
        P(None, "tensor"),
        P(None, "tensor"),
        P(None, "tensor"),
        P(None, "tensor"),
        P(None, "tensor"),
        P("tensor", None),
        P(None, "tensor"),
        P("tensor"),
        P("tensor"),
        P(None, "tensor"),
        P("tensor", None),
        P("dp", None, None),
    )
    return jax.shard_map(
        on_device,
        mesh=mesh,
        in_specs=placed,
        out_specs=(
            P("dp", None, None),
            P("dp", None, None),
            P(None, "tensor"),
            P(None, "tensor"),
            P(None, "tensor"),
            P(None, "tensor"),
            P(None, "tensor"),
            P(None, "tensor"),
            P(None, "tensor"),
            P("tensor", None),
            P(None, "tensor"),
            P("tensor"),
            P("tensor"),
            P(None, "tensor"),
            P("tensor", None),
            P(None, "tensor"),
        ),
        check_vma=False,
    )
```

```python
import functools
import math

import jax
import jax.numpy as jnp
from jax import lax
from jax.experimental import pallas as pl
from jax.experimental.pallas import tpu as pltpu
from jax.sharding import PartitionSpec as P

NORM_EPSILON = 1e-05
GELU_SCALE = 0.7978845608028654
GELU_CUBIC = 0.044715
LANES = 128
ROWS = 256
FINE = 32
SPLITS = 3
VMEM = 56 * 1024 * 1024
BF16 = jnp.bfloat16
F32 = jnp.float32


def dot_first(left, right):
    return lax.dot_general(left, right, (((0,), (0,)), ((), ())), preferred_element_type=F32)


def dot_last(left, right):
    return lax.dot_general(left, right, (((1,), (1,)), ((), ())), preferred_element_type=F32)


def dot_plain(left, right):
    return jnp.dot(left, right, preferred_element_type=F32)


def gelu_parts(values):
    square = values * values
    tangent = jnp.tanh(GELU_SCALE * (values + GELU_CUBIC * values * square))
    half = 0.5 * (1.0 + tangent)
    slope = half + 0.5 * values * (1.0 - tangent * tangent) * (
        GELU_SCALE * (1.0 + 3.0 * GELU_CUBIC * square)
    )
    return (values * half, slope)


def unit_rows(values):
    average = jnp.mean(values, axis=-1, keepdims=True)
    centered = values - average
    spread = jnp.mean(centered * centered, axis=-1, keepdims=True)
    inverse = lax.rsqrt(spread + NORM_EPSILON)
    return (centered * inverse, inverse)


def norm_backward(upstream, unit, inverse, gain):
    grad_unit = upstream * gain
    return inverse * (
        grad_unit
        - jnp.mean(grad_unit, axis=-1, keepdims=True)
        - unit * jnp.mean(grad_unit * unit, axis=-1, keepdims=True)
    )


def lane_index(rows):
    return lax.broadcasted_iota(jnp.int32, (rows, LANES), 1)


def whole(array):
    rank = array.ndim
    return pl.BlockSpec(
        array.shape, lambda *_: (0,) * rank, pipeline_mode=pl.Buffered(1)
    )


def fixed(shape):
    return pl.BlockSpec(shape, lambda *_: (0,) * len(shape))


def params():
    return pltpu.CompilerParams(vmem_limit_bytes=VMEM)


def cost(flops, moved, special=0):
    return pl.CostEstimate(flops=int(flops), bytes_accessed=int(moved), transcendentals=int(special))


def axis_bits(name):
    count = lax.axis_size(name)
    bits = []
    bit = 1
    while bit < count:
        bits.append(bit)
        bit = bit * 2
    return bits


def relative_order(bits):
    count = 2 ** len(bits)
    order = []
    for place in range(count):
        value = 0
        for depth, bit in enumerate(bits):
            if place & (count >> (depth + 1)):
                value = value | bit
        order.append(value)
    return order


def swap(piece, name, bit):
    return lax.ppermute(piece, name, [(i, i ^ bit) for i in range(lax.axis_size(name))])


def add_pieces(left, right):
    return (left.astype(F32) + right.astype(F32)).astype(BF16)


def sum_scatter(held, name, bits):
    for bit in bits:
        half = held.shape[0] // 2
        got = swap(held[half:], name, bit)
        held = add_pieces(held[:half], got)
    return held


def gather_chunks(held, name, bits):
    for bit in reversed(bits):
        held = jnp.concatenate([held, swap(held, name, bit)], axis=0)
    return held


def dp_sum(held, bits):
    held = sum_scatter(held, "dp", bits)
    for bit in axis_bits("dp"):
        if bit not in bits:
            held = add_pieces(held, swap(held, "dp", bit))
    return gather_chunks(held, "dp", bits)


def chunk_table(bits, name):
    place = jnp.bitwise_and(lax.axis_index(name), 2 ** len(bits) - 1)
    return jnp.bitwise_xor(jnp.array(relative_order(bits), jnp.int32), place)


def place_chunks(held, table, dtype):
    count, rows, width = held.shape

    def body(table_ref, held_ref, out_ref):
        out_ref[...] = held_ref[0].astype(dtype)

    return pl.pallas_call(
        body,
        out_shape=jax.ShapeDtypeStruct((count * rows, width), dtype),
        grid_spec=pltpu.PrefetchScalarGridSpec(
            num_scalar_prefetch=1,
            grid=(count,),
            in_specs=[pl.BlockSpec((1, rows, width), lambda i, table_ref: (i, 0, 0))],
            out_specs=pl.BlockSpec((rows, width), lambda i, table_ref: (table_ref[i], 0)),
        ),
        name="place_chunks",
    )(table, held)


def project_body(
    head,
    experts,
    mem_blocks,
    shift,
    memory_ref,
    inputs_ref,
    gains_ref,
    biases_ref,
    key_ref,
    value_ref,
    value_router_ref,
    query_ref,
    output_router_ref,
    content_ref,
    position_ref,
    value_route_ref,
    output_route_ref,
    place_ref,
    coarse_ref,
    fine_ref,
    normed_ref,
    key_cat_ref,
    values_ref,
    expert_ref,
    gate_ref,
    content_query_ref,
    bias_query_ref,
    out_gate_ref,
    trig_ref,
    weight_ref,
    count_ref,
    bias_scratch,
):
    step = pl.program_id(0)
    split = LANES * (1 + experts)

    @pl.when(step == 0)
    def _():
        weight_ref[...] = jnp.zeros_like(weight_ref)
        bias_scratch[...] = jnp.zeros_like(bias_scratch)
        count_ref[...] = jnp.zeros_like(count_ref)
        weight_ref[:, 0:head] = key_ref[...]
        weight_ref[:, head : head + experts] = value_router_ref[...]
        for e in range(experts):
            start = LANES * (e + 1)
            weight_ref[:, start : start + head] = value_ref[:, e * head : (e + 1) * head]
        weight_ref[:, split : split + head] = query_ref[...]
        weight_ref[:, split + head : split + head + experts] = output_router_ref[...]
        bias_scratch[0:1, 0:head] = content_ref[...]
        bias_scratch[1:2, 0:head] = position_ref[...]

    old = step < mem_blocks
    rows = jnp.where(old, memory_ref[...], inputs_ref[...]).astype(F32)
    unit, _ = unit_rows(rows)
    normed = (unit * gains_ref[0:1, :] + biases_ref[0:1, :]).astype(BF16)
    normed_ref[...] = normed
    product = dot_plain(normed, weight_ref[:, 0:split])
    lane = lane_index(ROWS)
    first = product[:, 0:LANES]
    key_cat_ref[:, 0:LANES] = jnp.where(lane < head, first, 0.0).astype(BF16)

    def picks(route):
        return (route[:, 0:1] == lane - head).astype(F32) + (route[:, 1:2] == lane - head).astype(
            F32
        )

    chosen = picks(value_route_ref[...])
    gate = jax.nn.sigmoid(first) * chosen
    gate_ref[...] = gate
    expert_ref[...] = product[:, LANES:split]
    total = jnp.zeros((ROWS, LANES), F32)
    for e in range(experts):
        start = LANES * (e + 1)
        total = total + gate[:, head + e : head + e + 1] * product[:, start : start + LANES]
    values_ref[...] = total.astype(BF16)
    freq = coarse_ref.shape[1] // 2
    current_place = lax.broadcasted_iota(jnp.int32, (1, ROWS), 1) + (step - mem_blocks) * ROWS
    place = jnp.where(old, place_ref[...], current_place) + shift
    coarse_rows = lax.broadcasted_iota(jnp.int32, (coarse_ref.shape[0] // 2, ROWS), 0)
    fine_rows = lax.broadcasted_iota(jnp.int32, (FINE, ROWS), 0)
    coarse_hit = (coarse_rows == place // FINE).astype(BF16)
    fine_hit = (fine_rows == lax.rem(place, FINE)).astype(BF16)
    slots = coarse_ref.shape[0] // 2
    big = dot_first(coarse_hit, coarse_ref[0:slots, :]) + dot_first(
        coarse_hit, coarse_ref[slots:, :]
    )
    small = dot_first(fine_hit, fine_ref[0:FINE, :]) + dot_first(fine_hit, fine_ref[FINE:, :])
    cosine = big[:, 0:freq] * small[:, 0:freq] - big[:, freq:] * small[:, freq:]
    sine = big[:, freq:] * small[:, 0:freq] + big[:, 0:freq] * small[:, freq:]
    key_cat_ref[:, LANES : LANES + freq] = cosine.astype(BF16)
    key_cat_ref[:, LANES + freq :] = sine.astype(BF16)

    @pl.when(step >= mem_blocks)
    def _():
        last = dot_plain(normed, weight_ref[:, split : split + LANES])
        query = jnp.where(lane < head, last, 0.0)
        content_query_ref[...] = (query + bias_scratch[0:1, :]).astype(BF16)
        bias_query_ref[...] = (query + bias_scratch[1:2, :]).astype(BF16)
        out_chosen = picks(output_route_ref[...])
        out_gate_ref[...] = jax.nn.sigmoid(last) * out_chosen
        trig_ref[:, 0:freq] = cosine
        trig_ref[:, freq:] = sine
        count_ref[0:1, :] += jnp.sum(chosen, axis=0, keepdims=True)
        count_ref[1:2, :] += jnp.sum(out_chosen, axis=0, keepdims=True)


def project(
    memory,
    inputs,
    gains,
    biases,
    key_weight,
    value_weight,
    value_router,
    query_weight,
    output_router,
    content_bias,
    position_bias,
    value_routes,
    output_routes,
    places,
    coarse,
    fine,
):
    mem_count, width = memory.shape
    length = inputs.shape[0]
    head = key_weight.shape[1]
    experts = value_router.shape[1]
    pos_width = coarse.shape[1]
    keys = mem_count + length
    mem_blocks = mem_count // ROWS
    blocks = keys // ROWS
    wide = LANES * (2 + experts)
    old = lambda i: (jnp.minimum(i, mem_blocks - 1), 0)
    new = lambda i: (jnp.maximum(i - mem_blocks, 0), 0)
    every = lambda i: (i, 0)
    row = lambda size, index: pl.BlockSpec((ROWS, size), index)
    return pl.pallas_call(
        functools.partial(project_body, head, experts, mem_blocks, 2 * mem_count),
        out_shape=(
            jax.ShapeDtypeStruct((keys, width), BF16),
            jax.ShapeDtypeStruct((keys, LANES + pos_width), BF16),
            jax.ShapeDtypeStruct((keys, LANES), BF16),
            jax.ShapeDtypeStruct((keys, LANES * experts), F32),
            jax.ShapeDtypeStruct((keys, LANES), F32),
            jax.ShapeDtypeStruct((length, LANES), BF16),
            jax.ShapeDtypeStruct((length, LANES), BF16),
            jax.ShapeDtypeStruct((length, LANES), F32),
            jax.ShapeDtypeStruct((length, pos_width), F32),
            jax.ShapeDtypeStruct((width, wide), BF16),
            jax.ShapeDtypeStruct((8, LANES), F32),
        ),
        grid=(blocks,),
        in_specs=[
            row(width, old),
            row(width, new),
            whole(gains),
            whole(biases),
            whole(key_weight),
            whole(value_weight),
            whole(value_router),
            whole(query_weight),
            whole(output_router),
            whole(content_bias),
            whole(position_bias),
            row(value_routes.shape[1], every),
            row(output_routes.shape[1], new),
            pl.BlockSpec((1, ROWS), lambda i: (0, jnp.minimum(i, mem_blocks - 1))),
            whole(coarse),
            whole(fine),
        ],
        out_specs=(
            row(width, every),
            row(LANES + pos_width, every),
            row(LANES, every),
            row(LANES * experts, every),
            row(LANES, every),
            row(LANES, new),
            row(LANES, new),
            row(LANES, new),
            row(pos_width, new),
            fixed((width, wide)),
            fixed((8, LANES)),
        ),
        scratch_shapes=[pltpu.VMEM((8, LANES), F32)],
        compiler_params=params(),
        cost_estimate=cost(2 * keys * width * wide, 20e6),
        name="project",
    )(
        memory,
        inputs,
        gains,
        biases,
        key_weight,
        value_weight,
        value_router,
        query_weight,
        output_router,
        content_bias,
        position_bias,
        value_routes,
        output_routes,
        places,
        coarse,
        fine,
    )


def trig_tables(first, count, step, pos_width):
    freq = pos_width // 2
    omega = jnp.exp(jnp.arange(freq, dtype=F32) * (-2.0 * math.log(10000.0) / pos_width))
    angle = (jnp.arange(count, dtype=F32) * step + first)[:, None] * omega
    table = jnp.concatenate([jnp.cos(angle), jnp.sin(angle)], axis=1)
    lead = lax.reduce_precision(table, 8, 7)
    return jnp.concatenate([lead, table - lead], axis=0).astype(BF16)


def attend_body(
    head,
    experts,
    content_ref,
    bias_ref,
    trig_ref,
    position_ref,
    key_cat_ref,
    values_ref,
    gate_ref,
    probs_ref,
    out_ref,
    query_scratch,
):
    step = pl.program_id(0)
    length = pl.num_programs(0) * ROWS
    keys = key_cat_ref.shape[0]
    freq = trig_ref.shape[1] // 2
    relative = dot_last(bias_ref[:, 0:head], position_ref[...])
    rel_sin = relative[:, 0:freq]
    rel_cos = relative[:, freq:]
    cosine = trig_ref[:, 0:freq]
    sine = trig_ref[:, freq:]
    query_scratch[:, 0:LANES] = content_ref[...]
    query_scratch[:, LANES : LANES + freq] = (rel_sin * sine + rel_cos * cosine).astype(BF16)
    query_scratch[:, LANES + freq :] = (rel_cos * sine - rel_sin * cosine).astype(BF16)
    lane = lane_index(ROWS)
    gate = jnp.where((lane >= head) & (lane < head + experts), gate_ref[...], 0.0)
    rest = gate - gate.astype(BF16).astype(F32)
    extra = gate + pltpu.roll(rest, experts, 1)
    scale = head ** (-0.5)

    length_static = gate_length(keys)

    def variant(block):
        def run():
            seen = keys - length_static + (block + 1) * ROWS
            scores = dot_last(query_scratch[...], key_cat_ref[0:seen, :]) * scale
            row = lax.broadcasted_iota(jnp.int32, (ROWS, ROWS), 0)
            col = lax.broadcasted_iota(jnp.int32, (ROWS, ROWS), 1)
            tail = jnp.where(col <= row, scores[:, seen - ROWS :], -jnp.inf)
            body = scores[:, 0 : seen - ROWS]
            top = jnp.maximum(
                jnp.max(body, axis=1, keepdims=True), jnp.max(tail, axis=1, keepdims=True)
            )
            body = jnp.exp(body - top)
            tail = jnp.exp(tail - top)
            total = jnp.sum(body, axis=1, keepdims=True) + jnp.sum(tail, axis=1, keepdims=True)
            share = 1.0 / total
            body = (body * share).astype(BF16)
            tail = (tail * share).astype(BF16)
            probs_ref[:, 0 : seen - ROWS] = body
            probs_ref[:, seen - ROWS : seen] = tail
            result = dot_plain(body, values_ref[0 : seen - ROWS, :]) + dot_plain(
                tail, values_ref[seen - ROWS : seen, :]
            )
            out_ref[...] = jnp.where(lane < head, result, extra).astype(BF16)

        return run

    for block in range(length_static // ROWS):
        pl.when(step == block)(variant(block))


def gate_length(keys):
    return keys // 2


def attend(content_query, bias_query, trig, position_weight, key_cat, values, out_gate, experts):
    length = content_query.shape[0]
    keys = key_cat.shape[0]
    head = position_weight.shape[1]
    pos_width = trig.shape[1]
    every = lambda i: (i, 0)
    row = lambda size: pl.BlockSpec((ROWS, size), every)
    return pl.pallas_call(
        functools.partial(attend_body, head, experts),
        out_shape=(
            jax.ShapeDtypeStruct((length, keys), BF16),
            jax.ShapeDtypeStruct((length, LANES), BF16),
        ),
        grid=(length // ROWS,),
        in_specs=[
            row(LANES),
            row(LANES),
            row(pos_width),
            whole(position_weight),
            whole(key_cat),
            whole(values),
            row(LANES),
        ],
        out_specs=(row(keys), row(LANES)),
        scratch_shapes=[pltpu.VMEM((ROWS, LANES + pos_width), BF16)],
        compiler_params=params(),
        cost_estimate=cost(2 * length * keys * (pos_width + 2 * LANES), 18e6, length * keys),
        name="attend",
    )(content_query, bias_query, trig, position_weight, key_cat, values, out_gate)


def attend_back_body(
    head,
    me_ref,
    probs_ref,
    grad_ref,
    key_cat_ref,
    values_ref,
    content_ref,
    bias_ref,
    trig_ref,
    position_ref,
    normed_ref,
    grad_keys_ref,
    grad_values_ref,
    grad_query_ref,
    weight_ref,
    sums_ref,
    position_scratch,
    relative_scratch,
):
    step = pl.program_id(0)
    keys = key_cat_ref.shape[0]
    length = gate_length(keys)
    freq = trig_ref.shape[1] // 2
    scale = head ** (-0.5)

    @pl.when(step == 0)
    def _():
        grad_keys_ref[...] = jnp.zeros_like(grad_keys_ref)
        grad_values_ref[...] = jnp.zeros_like(grad_values_ref)
        weight_ref[...] = jnp.zeros_like(weight_ref)
        sums_ref[...] = jnp.zeros_like(sums_ref)
        position_scratch[...] = jnp.zeros_like(position_scratch)
        position_scratch[:, 0:head] = position_ref[...]

    lane = lane_index(ROWS)
    packed = grad_ref[0]
    upstream = jnp.where(lane < head, packed, jnp.zeros_like(packed))
    cosine = trig_ref[:, 0:freq]
    sine = trig_ref[:, freq:]

    def variant(block):
        def run():
            seen = keys - length + (block + 1) * ROWS
            weights_low = probs_ref[:, 0:seen]
            weights = weights_low.astype(F32)
            grad_weights = dot_last(upstream, values_ref[0:seen, :])
            inner = jnp.sum(grad_weights * weights, axis=1, keepdims=True)
            grad_scores = (weights * (grad_weights - inner)).astype(BF16)
            grad_values_ref[0:seen, :] += dot_first(weights_low, upstream)
            grad_keys_ref[0:seen, :] += dot_first(grad_scores, content_ref[...]) * scale
            grad_query = dot_plain(grad_scores, key_cat_ref[0:seen, :]) * scale
            grad_content = grad_query[:, 0:LANES]
            grad_sin = grad_query[:, LANES : LANES + freq]
            grad_cos = grad_query[:, LANES + freq :]
            relative_scratch[:, 0:freq] = (grad_sin * sine - grad_cos * cosine).astype(BF16)
            relative_scratch[:, freq:] = (grad_sin * cosine + grad_cos * sine).astype(BF16)
            relative = relative_scratch[...]
            grad_bias = dot_plain(relative, position_scratch[...])
            weight_ref[:, LANES:] += dot_first(relative, bias_ref[...])
            sums_ref[0:1, :] += jnp.sum(grad_content, axis=0, keepdims=True)
            sums_ref[1:2, :] += jnp.sum(grad_bias, axis=0, keepdims=True)
            both = jnp.where(lane < head, (grad_content + grad_bias).astype(BF16), packed)
            grad_query_ref[...] = both
            weight_ref[:, 0:LANES] += dot_first(normed_ref[...], both)

        return run

    for block in range(length // ROWS):
        pl.when(step == block)(variant(block))


def attend_back(
    me, probs, grads, key_cat, values, content_query, bias_query, trig, position_weight, normed
):
    length, keys = probs.shape
    head = position_weight.shape[1]
    pos_width = trig.shape[1]
    width = normed.shape[1]
    mem_blocks = (keys - length) // ROWS
    every = lambda i, me_ref: (i, 0)
    row = lambda size: pl.BlockSpec((ROWS, size), every)
    return pl.pallas_call(
        functools.partial(attend_back_body, head),
        out_shape=(
            jax.ShapeDtypeStruct((keys, LANES), F32),
            jax.ShapeDtypeStruct((keys, LANES), F32),
            jax.ShapeDtypeStruct((length, LANES), BF16),
            jax.ShapeDtypeStruct((width, 2 * LANES), F32),
            jax.ShapeDtypeStruct((8, LANES), F32),
        ),
        grid_spec=pltpu.PrefetchScalarGridSpec(
            num_scalar_prefetch=1,
            grid=(length // ROWS,),
            in_specs=[
                row(keys),
                pl.BlockSpec((1, ROWS, LANES), lambda i, me_ref: (i ^ me_ref[0], 0, 0)),
                whole(key_cat),
                whole(values),
                row(LANES),
                row(LANES),
                row(pos_width),
                whole(position_weight),
                pl.BlockSpec((ROWS, width), lambda i, me_ref: (i + mem_blocks, 0)),
            ],
            out_specs=(
                fixed((keys, LANES)),
                fixed((keys, LANES)),
                row(LANES),
                fixed((width, 2 * LANES)),
                fixed((8, LANES)),
            ),
            scratch_shapes=[
                pltpu.VMEM((pos_width, LANES), BF16),
                pltpu.VMEM((ROWS, pos_width), BF16),
            ],
        ),
        compiler_params=params(),
        cost_estimate=cost(2 * length * keys * (pos_width + 4 * LANES), 25e6),
        name="attend_back",
    )(me, probs, grads, key_cat, values, content_query, bias_query, trig, position_weight, normed)


def spread_weights(head, experts, weight_refs, scratch):
    scratch[...] = jnp.zeros_like(scratch)
    for j, weight_ref in enumerate(weight_refs):
        for e in range(experts):
            start = LANES * (experts * j + e)
            scratch[start : start + head, :] = weight_ref[e * head : (e + 1) * head, :]


def gate_columns(head, experts, packed):
    return [
        packed[:, head + e : head + e + 1] + packed[:, head + experts + e : head + experts + e + 1]
        for e in range(experts)
    ]


def forward_body(
    head,
    experts,
    heads,
    table_ref,
    *refs,
):
    attended_refs = refs[0:heads]
    weight_refs = refs[heads : 2 * heads]
    (
        inputs_ref,
        cotangent_ref,
        up_ref,
        down_ref,
        gains_ref,
        biases_ref,
        resid_ref,
        normed_ref,
        active_ref,
        grad_upper_ref,
        grad_normed_ref,
        share_ref,
        weight_scratch,
        mixed_scratch,
    ) = refs[2 * heads :]

    @pl.when(pl.program_id(0) == 0)
    def _():
        spread_weights(head, experts, weight_refs, weight_scratch)

    lane = lane_index(ROWS)
    for j, attended_ref in enumerate(attended_refs):
        packed = attended_ref[...].astype(F32)
        attended = jnp.where(lane < head, packed, 0.0)
        for e, gate in enumerate(gate_columns(head, experts, packed)):
            start = LANES * (experts * j + e)
            mixed_scratch[:, start : start + LANES] = (attended * gate).astype(BF16)
    resid = inputs_ref[...].astype(F32) + dot_plain(mixed_scratch[...], weight_scratch[...])
    resid_ref[...] = resid
    unit, _ = unit_rows(resid)
    normed = (unit * gains_ref[1:2, :] + biases_ref[1:2, :]).astype(BF16)
    normed_ref[...] = normed
    upper = dot_plain(normed, up_ref[...])
    active, slope = gelu_parts(upper)
    active = active.astype(BF16)
    active_ref[...] = active
    grad_upper = (dot_last(cotangent_ref[...], down_ref[...]) * slope).astype(BF16)
    grad_upper_ref[...] = grad_upper
    grad_normed_ref[0] = dot_last(grad_upper, up_ref[...]).astype(BF16)
    share_ref[0] = dot_plain(active, down_ref[...]).astype(BF16)


def forward_ffn(table, attended, weights, inputs, cotangent, up, down, gains, biases, experts):
    heads = len(attended)
    length, width = inputs.shape
    head = weights[0].shape[0] // experts
    hidden = up.shape[1]
    blocks = length // ROWS
    absolute = lambda i, table_ref: (table_ref[i], 0)
    relative = lambda i, table_ref: (blocks - 1 - i, 0, 0)
    row = lambda size: pl.BlockSpec((ROWS, size), absolute)
    return pl.pallas_call(
        functools.partial(forward_body, head, experts, heads),
        out_shape=(
            jax.ShapeDtypeStruct((length, width), F32),
            jax.ShapeDtypeStruct((length, width), BF16),
            jax.ShapeDtypeStruct((length, hidden), BF16),
            jax.ShapeDtypeStruct((length, hidden), BF16),
            jax.ShapeDtypeStruct((blocks, ROWS, width), BF16),
            jax.ShapeDtypeStruct((blocks, ROWS, width), BF16),
        ),
        grid_spec=pltpu.PrefetchScalarGridSpec(
            num_scalar_prefetch=1,
            grid=(blocks,),
            in_specs=[row(LANES) for _ in attended]
            + [whole(weight) for weight in weights]
            + [row(width), row(width), whole(up), whole(down), whole(gains), whole(biases)],
            out_specs=(
                row(width),
                row(width),
                row(hidden),
                row(hidden),
                pl.BlockSpec((1, ROWS, width), relative),
                pl.BlockSpec((1, ROWS, width), relative),
            ),
            scratch_shapes=[
                pltpu.VMEM((heads * experts * LANES, width), BF16),
                pltpu.VMEM((ROWS, heads * experts * LANES), BF16),
            ],
        ),
        compiler_params=params(),
        cost_estimate=cost(
            2 * length * width * (heads * experts * LANES + 4 * hidden), 34e6, length * hidden
        ),
        name="forward_ffn",
    )(table, *attended, *weights, inputs, cotangent, up, down, gains, biases)


def second_norm_back_body(head, experts, heads, me_ref, *refs):
    attended_refs = refs[0:heads]
    weight_refs = refs[heads : 2 * heads]
    (
        left_ref,
        right_ref,
        resid_ref,
        cotangent_ref,
        gains_ref,
        grad_resid_ref,
        low_ref,
        packed_ref,
        sums_ref,
        weight_scratch,
    ) = refs[2 * heads :]
    spread_weights(head, experts, weight_refs, weight_scratch)
    unit, inverse = unit_rows(resid_ref[...])
    grad = left_ref[0].astype(F32) + right_ref[0].astype(F32)
    sums_ref[...] = jnp.zeros_like(sums_ref)
    sums_ref[0:1, :] = jnp.sum(grad * unit, axis=0, keepdims=True)
    sums_ref[1:2, :] = jnp.sum(grad, axis=0, keepdims=True)
    grad_resid = cotangent_ref[...].astype(F32) + norm_backward(
        grad, unit, inverse, gains_ref[1:2, :]
    )
    grad_resid_ref[...] = grad_resid
    low = grad_resid.astype(BF16)
    low_ref[0] = low
    grad_mixed = dot_last(low, weight_scratch[...])
    lane = lane_index(ROWS)
    for j, attended_ref in enumerate(attended_refs):
        packed = attended_ref[...].astype(F32)
        attended = jnp.where(lane < head, packed, 0.0)
        total = jnp.zeros((ROWS, LANES), F32)
        for e, gate in enumerate(gate_columns(head, experts, packed)):
            start = LANES * (experts * j + e)
            piece = grad_mixed[:, start : start + LANES]
            total = total + gate * piece
            logit = jnp.sum(piece * attended, axis=1, keepdims=True) * (gate * (1.0 - gate))
            total = jnp.where(lane == head + e, logit, total)
        packed_ref[j] = total.astype(BF16)


def second_norm_back(me, attended, weights, left, right, resid, cotangent, gains, experts):
    heads = len(attended)
    width = resid.shape[1]
    head = weights[0].shape[0] // experts
    own = lambda i, me_ref: (me_ref[0], 0)
    row = lambda size: pl.BlockSpec((ROWS, size), own)
    return pl.pallas_call(
        functools.partial(second_norm_back_body, head, experts, heads),
        out_shape=(
            jax.ShapeDtypeStruct((ROWS, width), F32),
            jax.ShapeDtypeStruct((1, ROWS, width), BF16),
            jax.ShapeDtypeStruct((heads, ROWS, LANES), BF16),
            jax.ShapeDtypeStruct((8, width), F32),
        ),
        grid_spec=pltpu.PrefetchScalarGridSpec(
            num_scalar_prefetch=1,
            grid=(1,),
            in_specs=[row(LANES) for _ in attended]
            + [whole(weight) for weight in weights]
            + [whole(left), whole(right), row(width), row(width), whole(gains)],
            out_specs=(
                fixed((ROWS, width)),
                fixed((1, ROWS, width)),
                fixed((heads, ROWS, LANES)),
                fixed((8, width)),
            ),
            scratch_shapes=[pltpu.VMEM((heads * experts * LANES, width), BF16)],
        ),
        compiler_params=params(),
        cost_estimate=cost(2 * ROWS * width * heads * experts * LANES, 12e6),
        name="second_norm_back",
    )(me, *attended, *weights, left, right, resid, cotangent, gains)


def grad_chunks(table, left, right):
    count = table.shape[0]
    length, rows = left.shape
    width = right.shape[1]
    chunk = rows // count

    def body(table_ref, left_ref, right_ref, out_ref):
        out_ref[0] = dot_first(left_ref[...], right_ref[...]).astype(BF16)

    return pl.pallas_call(
        body,
        out_shape=jax.ShapeDtypeStruct((count, chunk, width), BF16),
        grid_spec=pltpu.PrefetchScalarGridSpec(
            num_scalar_prefetch=1,
            grid=(count,),
            in_specs=[
                pl.BlockSpec((length, chunk), lambda i, table_ref: (0, table_ref[i])),
                whole(right),
            ],
            out_specs=pl.BlockSpec((1, chunk, width), lambda i, table_ref: (i, 0, 0)),
        ),
        compiler_params=params(),
        cost_estimate=cost(2 * length * rows * width, 2 * length * (rows + width)),
        name="grad_chunks",
    )(table, left, right)


def output_grad_body(head, experts, chunk, table_ref, me_ref, attended_ref, grad_ref, out_ref, acc, mixed):
    step = pl.program_id(0)
    count = out_ref.shape[0]
    lane = lane_index(ROWS)
    packed = attended_ref[...].astype(F32)

    @pl.when(step == 0)
    def _():
        acc[...] = jnp.zeros_like(acc)
        mixed[...] = jnp.zeros_like(mixed)

    for e, gate in enumerate(gate_columns(head, experts, packed)):
        piece = (packed[:, 0:head] * gate).astype(BF16)
        mixed[:, e * head : (e + 1) * head] = piece
    acc[...] += dot_first(mixed[...], grad_ref[0])

    @pl.when(step == pl.num_programs(0) - 1)
    def _():
        for place in range(count):
            start = pl.multiple_of(table_ref[place] * chunk, 8)
            out_ref[place] = acc[pl.ds(start, chunk), :].astype(BF16)


def output_grad(table, places, attended, grads, head, experts):
    count = table.shape[0]
    length = attended.shape[0]
    width = grads.shape[2]
    rows = experts * head
    rows = rows + -rows % (8 * count)
    chunk = rows // count
    lanes = rows + -rows % LANES
    return pl.pallas_call(
        functools.partial(output_grad_body, head, experts, chunk),
        out_shape=jax.ShapeDtypeStruct((count, chunk, width), BF16),
        grid_spec=pltpu.PrefetchScalarGridSpec(
            num_scalar_prefetch=2,
            grid=(length // ROWS,),
            in_specs=[
                pl.BlockSpec((ROWS, LANES), lambda i, table_ref, place_ref: (place_ref[i], 0)),
                pl.BlockSpec((1, ROWS, width), lambda i, table_ref, place_ref: (i, 0, 0)),
            ],
            out_specs=pl.BlockSpec((count, chunk, width), lambda i, table_ref, me_ref: (0, 0, 0)),
            scratch_shapes=[
                pltpu.VMEM((lanes, width), F32),
                pltpu.VMEM((ROWS, lanes), BF16),
            ],
        ),
        compiler_params=params(),
        cost_estimate=cost(2 * length * rows * width, 4e6),
        name="output_grad",
    )(table, places, attended, grads)


def project_back_body(
    head,
    experts,
    cur_blocks,
    chunk,
    table_ref,
    me_ref,
    normed_ref,
    grad_keys_ref,
    grad_values_ref,
    expert_ref,
    gate_ref,
    grad_query_ref,
    memory_ref,
    inputs_ref,
    weight_ref,
    grad_current_ref,
    out_ref,
    sums_ref,
    acc,
    packed_scratch,
):
    step = pl.program_id(0)
    count = out_ref.shape[0]
    split = LANES * (1 + experts)
    current = step < cur_blocks

    @pl.when(step == 0)
    def _():
        acc[...] = jnp.zeros_like(acc)
        sums_ref[...] = jnp.zeros_like(sums_ref)

    lane = lane_index(ROWS)
    gates = gate_ref[...]
    grad_values = grad_values_ref[...]
    first = grad_keys_ref[...]
    for e in range(experts):
        start = LANES * (e + 1)
        gate = gates[:, head + e : head + e + 1]
        packed_scratch[:, start : start + LANES] = (gate * grad_values).astype(BF16)
        piece = expert_ref[:, start - LANES : start]
        logit = jnp.sum(piece * grad_values, axis=1, keepdims=True) * (gate * (1.0 - gate))
        first = jnp.where(lane == head + e, logit, first)
    packed_scratch[:, 0:LANES] = first.astype(BF16)
    packed = packed_scratch[...]
    acc[...] += dot_first(normed_ref[...], packed)
    grad = dot_last(packed, weight_ref[:, 0:split])
    more = dot_last(grad_query_ref[...], weight_ref[:, split : split + LANES])
    grad = grad + jnp.where(current, more, 0.0)
    rows = jnp.where(current, inputs_ref[...], memory_ref[...]).astype(F32)
    unit, _ = unit_rows(rows)
    sums_ref[0:1, :] += jnp.sum(grad * unit, axis=0, keepdims=True)
    sums_ref[1:2, :] += jnp.sum(grad, axis=0, keepdims=True)

    @pl.when(current)
    def _():
        grad_current_ref[0] = grad.astype(BF16)

    @pl.when(step == pl.num_programs(0) - 1)
    def _():
        for place in range(count):
            start = pl.multiple_of(table_ref[place] * chunk, 8)
            out_ref[place] = acc[pl.ds(start, chunk), :].astype(BF16)


def project_back(
    table, places, normed, grad_keys, grad_values, expert_values, gates, grad_query, memory, inputs, weights, head, experts
):
    count = table.shape[0]
    keys, width = normed.shape
    length = inputs.shape[0]
    mem_blocks = (keys - length) // ROWS
    cur_blocks = length // ROWS
    blocks = keys // ROWS
    split = LANES * (1 + experts)
    chunk = width // count
    fresh = lambda i, place_ref: place_ref[jnp.minimum(i, cur_blocks - 1)]
    every = lambda i, table_ref, place_ref: (
        jnp.where(i < cur_blocks, fresh(i, place_ref) + mem_blocks, i - cur_blocks),
        0,
    )
    old = lambda i, table_ref, place_ref: (jnp.maximum(i - cur_blocks, 0), 0)
    new = lambda i, table_ref, place_ref: (fresh(i, place_ref), 0)
    row = lambda size, index: pl.BlockSpec((ROWS, size), index)
    return pl.pallas_call(
        functools.partial(project_back_body, head, experts, cur_blocks, chunk),
        out_shape=(
            jax.ShapeDtypeStruct((cur_blocks, ROWS, width), BF16),
            jax.ShapeDtypeStruct((count, chunk, split), BF16),
            jax.ShapeDtypeStruct((8, width), F32),
        ),
        grid_spec=pltpu.PrefetchScalarGridSpec(
            num_scalar_prefetch=2,
            grid=(blocks,),
            in_specs=[
                row(width, every),
                row(LANES, every),
                row(LANES, every),
                row(LANES * experts, every),
                row(LANES, every),
                row(LANES, new),
                row(width, old),
                row(width, new),
                whole(weights),
            ],
            out_specs=(
                pl.BlockSpec(
                    (1, ROWS, width),
                    lambda i, table_ref, place_ref: (jnp.minimum(i, cur_blocks - 1), 0, 0),
                ),
                pl.BlockSpec((count, chunk, split), lambda i, table_ref, me_ref: (0, 0, 0)),
                pl.BlockSpec((8, width), lambda i, table_ref, me_ref: (0, 0)),
            ),
            scratch_shapes=[
                pltpu.VMEM((width, split), F32),
                pltpu.VMEM((ROWS, split), BF16),
            ],
        ),
        compiler_params=params(),
        cost_estimate=cost(4 * keys * width * split, 20e6),
        name="project_back",
    )(
        table,
        places,
        normed,
        grad_keys,
        grad_values,
        expert_values,
        gates,
        grad_query,
        memory,
        inputs,
        weights,
    )


def first_norm_back(me, left, right, inputs, grad_resid, gains):
    width = inputs.shape[1]

    def body(me_ref, left_ref, right_ref, inputs_ref, resid_ref, gains_ref, out_ref):
        unit, inverse = unit_rows(inputs_ref[...].astype(F32))
        grad = left_ref[0].astype(F32) + right_ref[0].astype(F32)
        out_ref[0] = (
            resid_ref[...] + norm_backward(grad, unit, inverse, gains_ref[0:1, :])
        ).astype(BF16)

    return pl.pallas_call(
        body,
        out_shape=jax.ShapeDtypeStruct((1, ROWS, width), BF16),
        grid_spec=pltpu.PrefetchScalarGridSpec(
            num_scalar_prefetch=1,
            grid=(1,),
            in_specs=[
                whole(left),
                whole(right),
                pl.BlockSpec((ROWS, width), lambda i, me_ref: (me_ref[0], 0)),
                whole(grad_resid),
                whole(gains),
            ],
            out_specs=fixed((1, ROWS, width)),
        ),
        compiler_params=params(),
        cost_estimate=cost(20 * ROWS * width, 4e6),
        name="first_norm_back",
    )(me, left, right, inputs, grad_resid, gains)


def add_rows(me, left, right, resid):
    width = resid.shape[1]

    def body(me_ref, left_ref, right_ref, resid_ref, out_ref):
        out_ref[0] = (
            resid_ref[...] + left_ref[0].astype(F32) + right_ref[0].astype(F32)
        ).astype(BF16)

    return pl.pallas_call(
        body,
        out_shape=jax.ShapeDtypeStruct((1, ROWS, width), BF16),
        grid_spec=pltpu.PrefetchScalarGridSpec(
            num_scalar_prefetch=1,
            grid=(1,),
            in_specs=[
                whole(left),
                whole(right),
                pl.BlockSpec((ROWS, width), lambda i, me_ref: (me_ref[0], 0)),
            ],
            out_specs=fixed((1, ROWS, width)),
        ),
        compiler_params=params(),
        cost_estimate=cost(2 * ROWS * width, 3e6),
        name="add_rows",
    )(me, left, right, resid)


def unpack_projection(table, held, head, experts):
    count, chunk, split = held.shape
    rows = count * chunk

    def body(table_ref, held_ref, key_ref, router_ref, value_ref):
        first = held_ref[0, :, 0:LANES].astype(F32)
        key_ref[...] = first[:, 0:head]
        router_ref[...] = first[:, head : head + experts]
        for e in range(experts):
            start = LANES * (e + 1)
            piece = held_ref[0, :, start : start + LANES].astype(F32)
            value_ref[:, e * head : (e + 1) * head] = piece[:, 0:head]

    moved = lambda i, table_ref: (table_ref[i], 0)
    return pl.pallas_call(
        body,
        out_shape=(
            jax.ShapeDtypeStruct((rows, head), F32),
            jax.ShapeDtypeStruct((rows, experts), F32),
            jax.ShapeDtypeStruct((rows, experts * head), F32),
        ),
        grid_spec=pltpu.PrefetchScalarGridSpec(
            num_scalar_prefetch=1,
            grid=(count,),
            in_specs=[pl.BlockSpec((1, chunk, split), lambda i, table_ref: (i, 0, 0))],
            out_specs=(
                pl.BlockSpec((chunk, head), moved),
                pl.BlockSpec((chunk, experts), moved),
                pl.BlockSpec((chunk, experts * head), moved),
            ),
        ),
        name="unpack_projection",
    )(table, held)


def pack_query_grads(table, weight):
    count = table.shape[0]
    rows, width = weight.shape
    chunk = rows // count

    def body(table_ref, weight_ref, out_ref):
        out_ref[0] = weight_ref[...].astype(BF16)

    return pl.pallas_call(
        body,
        out_shape=jax.ShapeDtypeStruct((count, chunk, width), BF16),
        grid_spec=pltpu.PrefetchScalarGridSpec(
            num_scalar_prefetch=1,
            grid=(count,),
            in_specs=[pl.BlockSpec((chunk, width), lambda i, table_ref: (table_ref[i], 0))],
            out_specs=pl.BlockSpec((1, chunk, width), lambda i, table_ref: (i, 0, 0)),
        ),
        name="pack_query_grads",
    )(table, weight)


def unpack_query(table, held, head, experts):
    count, chunk, width = held.shape
    rows = count * chunk

    def body(table_ref, held_ref, query_ref, router_ref, position_ref):
        first = held_ref[0, :, 0:LANES].astype(F32)
        query_ref[...] = first[:, 0:head]
        router_ref[...] = first[:, head : head + experts]
        position_ref[...] = held_ref[0, :, LANES:].astype(F32)[:, 0:head]

    moved = lambda i, table_ref: (table_ref[i], 0)
    return pl.pallas_call(
        body,
        out_shape=(
            jax.ShapeDtypeStruct((rows, head), F32),
            jax.ShapeDtypeStruct((rows, experts), F32),
            jax.ShapeDtypeStruct((rows, head), F32),
        ),
        grid_spec=pltpu.PrefetchScalarGridSpec(
            num_scalar_prefetch=1,
            grid=(count,),
            in_specs=[pl.BlockSpec((1, chunk, width), lambda i, table_ref: (i, 0, 0))],
            out_specs=(
                pl.BlockSpec((chunk, head), moved),
                pl.BlockSpec((chunk, experts), moved),
                pl.BlockSpec((chunk, head), moved),
            ),
        ),
        name="unpack_query",
    )(table, held)


def on_device(
    inputs,
    memory,
    memory_positions,
    value_routes,
    output_routes,
    norm_gains,
    norm_biases,
    query_weight,
    key_weight,
    value_weight,
    value_router,
    output_router,
    output_weight,
    position_weight,
    content_bias,
    position_bias,
    up_weight,
    down_weight,
    cotangent,
):
    length, width = inputs.shape[1:]
    mem_count = memory.shape[1]
    keys = mem_count + length
    head = query_weight.shape[1]
    experts = value_router.shape[1]
    pos_width = position_weight.shape[0]
    picks = value_routes.shape[3]
    t_index = lax.axis_index("tensor")
    me = t_index.reshape(1).astype(jnp.int32)
    t_bits = axis_bits("tensor")
    t_table = chunk_table(t_bits, "tensor")
    t_count = lax.axis_size("tensor")
    dp_order = axis_bits("dp")[:SPLITS]
    dp_table = chunk_table(dp_order, "dp")
    tokens = inputs.reshape(length, width)
    upstream = cotangent.reshape(length, width)
    past = memory.reshape(mem_count, width)

    weights = [output_weight]
    for bit in reversed(t_bits):
        weights = weights + [swap(piece, "tensor", bit) for piece in weights]

    coarse_count = (2 * mem_count + length) // FINE
    coarse = trig_tables(-2.0 * mem_count, coarse_count, float(FINE), pos_width)
    fine = trig_tables(0.0, FINE, 1.0, pos_width)
    (
        normed,
        key_cat,
        values,
        expert_values,
        gates,
        content_query,
        bias_query,
        out_gate,
        trig,
        joined,
        counts,
    ) = project(
        past,
        tokens,
        norm_gains,
        norm_biases,
        key_weight,
        value_weight,
        value_router,
        query_weight,
        output_router,
        content_bias.reshape(1, head),
        position_bias.reshape(1, head),
        value_routes.reshape(keys, picks),
        output_routes.reshape(length, picks),
        memory_positions,
        coarse,
        fine,
    )
    probs, attended_own = attend(
        content_query, bias_query, trig, position_weight, key_cat, values, out_gate, experts
    )
    attended = [attended_own]
    for bit in reversed(t_bits):
        attended = attended + [swap(piece, "tensor", bit) for piece in attended]
    resid, normed_two, active, grad_upper, grad_normed_rel, share_rel = forward_ffn(
        t_table[::-1],
        attended,
        weights,
        tokens,
        upstream,
        up_weight,
        down_weight,
        norm_gains,
        norm_biases,
        experts,
    )

    def tensor_scatter(held):
        for bit in t_bits[:-1]:
            half = held.shape[0] // 2
            held = add_pieces(held[:half], swap(held[half:], "tensor", bit))
        half = held.shape[0] // 2
        return held[:half], swap(held[half:], "tensor", t_bits[-1])

    def tensor_gather(held):
        return gather_chunks(held, "tensor", t_bits)

    left, right = tensor_scatter(grad_normed_rel)
    grad_down_rel = grad_chunks(dp_table, active, upstream)
    grad_up_rel = grad_chunks(dp_table, normed_two, grad_upper)
    grad_down_sum = dp_sum(grad_down_rel, dp_order)
    grad_up_sum = dp_sum(grad_up_rel, dp_order)
    grad_resid, low_own, packed, sums_two = second_norm_back(
        me, attended, weights, left, right, resid, upstream, norm_gains, experts
    )
    t_order = relative_order(t_bits)
    arrived = []
    for place, distance in enumerate(t_order):
        piece = packed[place : place + 1]
        arrived.append(piece if distance == 0 else swap(piece, "tensor", distance))
    by_distance = [arrived[t_order.index(distance)] for distance in range(t_count)]
    grads = jnp.concatenate(by_distance, axis=0)
    grad_keys, grad_values, grad_query, query_weights, bias_sums = attend_back(
        me,
        probs,
        grads,
        key_cat,
        values,
        content_query,
        bias_query,
        trig,
        position_weight,
        normed,
    )
    query_sum = dp_sum(pack_query_grads(dp_table, query_weights), dp_order)
    low_all = tensor_gather(low_own)
    output_sum = dp_sum(
        output_grad(dp_table, t_table, attended_own, low_all, head, experts), dp_order
    )
    left_two, right_two = tensor_scatter(share_rel)
    output_own = add_rows(me, left_two, right_two, resid)
    output = place_chunks(tensor_gather(output_own), t_table, BF16)

    grad_current_rel, late_rel, sums_one = project_back(
        dp_table,
        t_table,
        normed,
        grad_keys,
        grad_values,
        expert_values,
        gates,
        grad_query,
        past,
        tokens,
        joined,
        head,
        experts,
    )
    left_one, right_one = tensor_scatter(grad_current_rel)
    late_sum = dp_sum(late_rel, dp_order)
    grad_inputs_own = first_norm_back(me, left_one, right_one, tokens, grad_resid, norm_gains)
    grad_inputs = place_chunks(tensor_gather(grad_inputs_own), t_table, BF16)

    norm_sums = jnp.concatenate([sums_one[0:1], sums_two[0:1], sums_one[1:2], sums_two[1:2]])
    for bit in t_bits:
        norm_sums = norm_sums + swap(norm_sums, "tensor", bit)
    share = width // t_count
    own_sums = lax.dynamic_slice_in_dim(norm_sums, t_index * share, share, 1)
    small = jnp.concatenate(
        [own_sums.reshape(-1, LANES), bias_sums[0:2], counts[0:2]], axis=0
    )
    small_rows = small.shape[0]
    small = jnp.pad(small, ((0, -small_rows % 8), (0, 0)))
    for bit in axis_bits("dp"):
        small = small + swap(small, "dp", bit)
    own = small[: small_rows - 4].reshape(4, share)
    extra = small[small_rows - 4 : small_rows]

    grad_key, grad_value_router, grad_value = unpack_projection(dp_table, late_sum, head, experts)
    grad_query_weight, grad_output_router, grad_position = unpack_query(
        dp_table, query_sum, head, experts
    )
    grad_up = place_chunks(grad_up_sum, dp_table, F32)
    grad_down = place_chunks(grad_down_sum, dp_table, F32)
    grad_out = place_chunks(output_sum, dp_table, F32)[: experts * head]
    return (
        output.reshape(1, length, width),
        grad_inputs.reshape(1, length, width),
        own[0:2],
        own[2:4],
        grad_query_weight,
        grad_key,
        grad_value,
        grad_value_router,
        grad_output_router,
        grad_out,
        grad_position,
        extra[0, 0:head],
        extra[1, 0:head],
        grad_up,
        grad_down,
        extra[2:4, head : head + experts].astype(jnp.int32),
    )


def solution(mesh):
    placed = (
        P("dp", None, None),
        P("dp", None, None),
        P("dp", None),
        P("dp", None, "tensor", None),
        P("dp", None, "tensor", None),
        P(),
        P(),
        P(None, "tensor"),
        P(None, "tensor"),
        P(None, "tensor"),
        P(None, "tensor"),
        P(None, "tensor"),
        P("tensor", None),
        P(None, "tensor"),
        P("tensor"),
        P("tensor"),
        P(None, "tensor"),
        P("tensor", None),
        P("dp", None, None),
    )
    return jax.shard_map(
        on_device,
        mesh=mesh,
        in_specs=placed,
        out_specs=(
            P("dp", None, None),
            P("dp", None, None),
            P(None, "tensor"),
            P(None, "tensor"),
            P(None, "tensor"),
            P(None, "tensor"),
            P(None, "tensor"),
            P(None, "tensor"),
            P(None, "tensor"),
            P("tensor", None),
            P(None, "tensor"),
            P("tensor"),
            P("tensor"),
            P(None, "tensor"),
            P("tensor", None),
            P(None, "tensor"),
        ),
        check_vma=False,
    )
```

```python
import functools
import math

import jax
import jax.numpy as jnp
from jax import lax
from jax.experimental import pallas as pl
from jax.experimental.pallas import tpu as pltpu
from jax.sharding import PartitionSpec as P

NORM_EPSILON = 1e-05
GELU_SCALE = 0.7978845608028654
GELU_CUBIC = 0.044715
LANES = 128
ROWS = 256
FINE = 32
SPLITS = 3
SECOND = ("up", "out",)
ORDER = (
    "ffn", "gna", "snb", "sh", "U1", "D1", "sha", "vb", "U2", "D2",
    "ab", "V1", "low", "orow", "U3", "D3", "og", "pb", "U4", "oc",
    "D4", "V2", "O1", "n0", "gca", "pro", "n1", "V3", "L1", "D5",
    "n2", "O2", "V4", "fnb", "L2", "U5", "O3", "n3", "L3", "V5",
    "gi", "n4", "Du", "pri", "O4", "L4", "nu", "Vu", "O5", "L5",
    "Uu", "Lu", "Ou",
)
VMEM = 56 * 1024 * 1024
FLOPS_US = 1.1e9
SHRINK = 1000
BF16 = jnp.bfloat16
F32 = jnp.float32


def dot_first(left, right):
    return lax.dot_general(left, right, (((0,), (0,)), ((), ())), preferred_element_type=F32)


def dot_last(left, right):
    return lax.dot_general(left, right, (((1,), (1,)), ((), ())), preferred_element_type=F32)


def dot_plain(left, right):
    return jnp.dot(left, right, preferred_element_type=F32)


def gelu_parts(values):
    square = values * values
    tangent = jnp.tanh(GELU_SCALE * (values + GELU_CUBIC * values * square))
    half = 0.5 * (1.0 + tangent)
    slope = half + 0.5 * values * (1.0 - tangent * tangent) * (
        GELU_SCALE * (1.0 + 3.0 * GELU_CUBIC * square)
    )
    return (values * half, slope)


def unit_rows(values):
    average = jnp.mean(values, axis=-1, keepdims=True)
    centered = values - average
    spread = jnp.mean(centered * centered, axis=-1, keepdims=True)
    inverse = lax.rsqrt(spread + NORM_EPSILON)
    return (centered * inverse, inverse)


def norm_backward(upstream, unit, inverse, gain):
    grad_unit = upstream * gain
    return inverse * (
        grad_unit
        - jnp.mean(grad_unit, axis=-1, keepdims=True)
        - unit * jnp.mean(grad_unit * unit, axis=-1, keepdims=True)
    )


def lane_index(rows):
    return lax.broadcasted_iota(jnp.int32, (rows, LANES), 1)


def whole(array):
    rank = array.ndim
    return pl.BlockSpec(
        array.shape, lambda *_: (0,) * rank, pipeline_mode=pl.Buffered(1)
    )


def fixed(shape):
    return pl.BlockSpec(shape, lambda *_: (0,) * len(shape))


def params():
    return pltpu.CompilerParams(vmem_limit_bytes=VMEM)


def cost(flops, moved, special=0):
    return pl.CostEstimate(flops=int(flops) // SHRINK, bytes_accessed=int(moved) // SHRINK, transcendentals=0)


def axis_bits(name):
    count = lax.axis_size(name)
    bits = []
    bit = 1
    while bit < count:
        bits.append(bit)
        bit = bit * 2
    return bits


def relative_order(bits):
    count = 2 ** len(bits)
    order = []
    for place in range(count):
        value = 0
        for depth, bit in enumerate(bits):
            if place & (count >> (depth + 1)):
                value = value | bit
        order.append(value)
    return order


def swap(piece, name, bit):
    return lax.ppermute(piece, name, [(i, i ^ bit) for i in range(lax.axis_size(name))])


def add_pieces(left, right):
    return (left.astype(F32) + right.astype(F32)).astype(BF16)


def after(value, *others):
    return lax.optimization_barrier((value,) + others)[0]


class DpSum:
    def __init__(self, keep, send, bits):
        self.keep = keep
        self.send = send
        self.bits = bits
        self.more = [bit for bit in axis_bits("dp") if bit not in bits]
        self.folded = 0
        self.depth = 0
        self.got = None

    def go(self):
        self.got = swap(self.send, "dp", self.bits[self.folded])

    def fold(self, *others):
        got = after(self.got, *others)
        self.folded = self.folded + 1
        if self.folded < len(self.bits):
            half = self.keep.shape[0] // 2
            self.send = add_pieces(self.keep[half:], got[half:])
            self.keep = add_pieces(self.keep[:half], got[:half])
        else:
            self.keep = add_pieces(self.keep, got)
            for bit in self.more:
                self.keep = add_pieces(self.keep, swap(self.keep, "dp", bit))
            self.depth = len(self.bits)

    def back(self):
        self.depth = self.depth - 1
        self.got = swap(self.keep, "dp", self.bits[self.depth])

    def join(self, *others):
        got = after(self.got, *others)
        self.keep = jnp.concatenate([self.keep, got], axis=0)


def chunk_table(bits, name):
    place = jnp.bitwise_and(lax.axis_index(name), 2 ** len(bits) - 1)
    return jnp.bitwise_xor(jnp.array(relative_order(bits), jnp.int32), place)

def angles(place, coarse_ref, fine_ref):
    count = place.shape[1]
    slots = coarse_ref.shape[0] // 2
    freq = coarse_ref.shape[1] // 2
    coarse_rows = lax.broadcasted_iota(jnp.int32, (slots, count), 0)
    fine_rows = lax.broadcasted_iota(jnp.int32, (FINE, count), 0)
    coarse_hit = (coarse_rows == place // FINE).astype(BF16)
    fine_hit = (fine_rows == lax.rem(place, FINE)).astype(BF16)
    big = dot_first(coarse_hit, coarse_ref[0:slots, :]) + dot_first(
        coarse_hit, coarse_ref[slots:, :]
    )
    small = dot_first(fine_hit, fine_ref[0:FINE, :]) + dot_first(fine_hit, fine_ref[FINE:, :])
    cosine = big[:, 0:freq] * small[:, 0:freq] - big[:, freq:] * small[:, freq:]
    sine = big[:, freq:] * small[:, 0:freq] + big[:, 0:freq] * small[:, freq:]
    return cosine, sine


def trig_tables(first, count, step, pos_width):
    freq = pos_width // 2
    omega = jnp.exp(jnp.arange(freq, dtype=F32) * (-2.0 * math.log(10000.0) / pos_width))
    angle = (jnp.arange(count, dtype=F32) * step + first)[:, None] * omega
    table = jnp.concatenate([jnp.cos(angle), jnp.sin(angle)], axis=1)
    lead = lax.reduce_precision(table, 8, 7)
    return jnp.concatenate([lead, table - lead], axis=0).astype(BF16)


def fill_weights(head, experts, key_ref, router_ref, value_ref, scratch):
    scratch[0:head, :] = key_ref[...]
    scratch[head : head + experts, :] = router_ref[...]
    for e in range(experts):
        start = LANES * (e + 1)
        scratch[start : start + head, :] = value_ref[e * head : (e + 1) * head, :]


def front_body(
    head,
    experts,
    length,
    shift,
    memory_ref,
    inputs_ref,
    gains_ref,
    biases_ref,
    key_ref,
    value_ref,
    value_router_ref,
    query_ref,
    output_router_ref,
    position_ref,
    content_bias_ref,
    position_bias_ref,
    value_route_ref,
    output_route_ref,
    place_ref,
    coarse_ref,
    fine_ref,
    normed_ref,
    key_cat_ref,
    values_ref,
    gate_ref,
    content_query_ref,
    bias_query_ref,
    count_ref,
    probs_ref,
    attended_ref,
    weight_scratch,
    bias_scratch,
    key_scratch,
    value_scratch,
    query_scratch,
):
    step = pl.program_id(0)
    span = memory_ref.shape[0]
    keys = key_scratch.shape[0]
    mem_steps = (keys - length) // span
    split = LANES * (1 + experts)
    freq = coarse_ref.shape[1] // 2

    @pl.when(step == 0)
    def _():
        weight_scratch[...] = jnp.zeros_like(weight_scratch)
        bias_scratch[...] = jnp.zeros_like(bias_scratch)
        count_ref[...] = jnp.zeros_like(count_ref)
        fill_weights(head, experts, key_ref, value_router_ref, value_ref, weight_scratch)
        weight_scratch[split : split + head, :] = query_ref[...]
        weight_scratch[split + head : split + head + experts, :] = output_router_ref[...]
        bias_scratch[0:1, 0:head] = content_bias_ref[...]
        bias_scratch[1:2, 0:head] = position_bias_ref[...]

    old = step < mem_steps
    rows = jnp.where(old, memory_ref[...], inputs_ref[...]).astype(F32)
    unit, _ = unit_rows(rows)
    normed = (unit * gains_ref[0:1, :] + biases_ref[0:1, :]).astype(BF16)
    normed_ref[...] = normed
    product = dot_last(normed, weight_scratch[0:split, :])
    lane = lane_index(span)
    first = product[:, 0:LANES]
    key_piece = jnp.where(lane < head, first, 0.0).astype(BF16)

    def picks(route):
        row = lax.broadcasted_iota(jnp.int32, (LANES, span), 0) - head
        hit = (route[0:1, :] == row).astype(F32) + (route[1:2, :] == row).astype(F32)
        return hit.T

    chosen = picks(value_route_ref[...])
    gate = jax.nn.sigmoid(first) * chosen
    gate_ref[...] = gate
    total = jnp.zeros((span, LANES), F32)
    for e in range(experts):
        start = LANES * (e + 1)
        total = total + gate[:, head + e : head + e + 1] * product[:, start : start + LANES]
    values = total.astype(BF16)
    values_ref[...] = values
    current_place = lax.broadcasted_iota(jnp.int32, (1, span), 1) + (step - mem_steps) * span
    cosine, sine = angles(
        jnp.where(old, place_ref[...], current_place) + shift, coarse_ref, fine_ref
    )
    cos_low = cosine.astype(BF16)
    sin_low = sine.astype(BF16)
    key_cat_ref[:, 0:LANES] = key_piece
    key_cat_ref[:, LANES : LANES + freq] = cos_low
    key_cat_ref[:, LANES + freq :] = sin_low
    base = pl.multiple_of(step * span, span)
    key_scratch[pl.ds(base, span), 0:LANES] = key_piece
    key_scratch[pl.ds(base, span), LANES : LANES + freq] = cos_low
    key_scratch[pl.ds(base, span), LANES + freq :] = sin_low
    value_scratch[pl.ds(base, span), :] = values

    def variant(place):
        def run():
            last = dot_last(normed, weight_scratch[split:, :])
            query = jnp.where(lane < head, last, 0.0)
            content = (query + bias_scratch[0:1, :]).astype(BF16)
            biased = (query + bias_scratch[1:2, :]).astype(BF16)
            content_query_ref[...] = content
            bias_query_ref[...] = biased
            out_chosen = picks(output_route_ref[...])
            out_gate = jax.nn.sigmoid(last) * out_chosen
            count_ref[0:1, :] += jnp.sum(chosen, axis=0, keepdims=True)
            count_ref[1:2, :] += jnp.sum(out_chosen, axis=0, keepdims=True)
            rest = out_gate - out_gate.astype(BF16).astype(F32)
            extra = out_gate + pltpu.roll(rest, experts, 1)
            relative = dot_plain(biased[:, 0:head], position_ref[...])
            rel_sin = relative[:, 0:freq]
            rel_cos = relative[:, freq:]
            query_scratch[:, 0:LANES] = content
            query_scratch[:, LANES : LANES + freq] = (rel_sin * sine + rel_cos * cosine).astype(
                BF16
            )
            query_scratch[:, LANES + freq :] = (rel_cos * sine - rel_sin * cosine).astype(BF16)
            factor = head ** (-0.5) * math.log2(math.e)
            row = lax.broadcasted_iota(jnp.int32, (ROWS, ROWS), 0)
            col = lax.broadcasted_iota(jnp.int32, (ROWS, ROWS), 1)
            for part in range(span // ROWS):
                piece = slice(part * ROWS, (part + 1) * ROWS)
                seen = keys - length + place * span + (part + 1) * ROWS
                scores = dot_last(query_scratch[piece, :], key_scratch[0:seen, :])
                body = scores[:, 0 : seen - ROWS]
                tail = jnp.where(col <= row, scores[:, seen - ROWS :], -jnp.inf)
                top = factor * jnp.maximum(
                    jnp.max(body, axis=1, keepdims=True), jnp.max(tail, axis=1, keepdims=True)
                )
                body = jnp.exp2(body * factor - top)
                tail = jnp.exp2(tail * factor - top)
                share = 1.0 / (
                    jnp.sum(body, axis=1, keepdims=True) + jnp.sum(tail, axis=1, keepdims=True)
                )
                body = (body * share).astype(BF16)
                tail = (tail * share).astype(BF16)
                probs_ref[piece, 0 : seen - ROWS] = body
                probs_ref[piece, seen - ROWS : seen] = tail
                if seen < keys:
                    probs_ref[piece, seen:] = jnp.zeros((ROWS, keys - seen), BF16)
                result = dot_plain(body, value_scratch[0 : seen - ROWS, :]) + dot_plain(
                    tail, value_scratch[seen - ROWS : seen, :]
                )
                attended_ref[piece, :] = jnp.where(
                    lane[piece, :] < head, result, extra[piece, :]
                ).astype(BF16)

        return run

    for place in range(length // span):
        pl.when(step == mem_steps + place)(variant(place))


def front(
    memory,
    inputs,
    gains,
    biases,
    key_weight,
    value_weight,
    value_router,
    query_weight,
    output_router,
    position_weight,
    content_bias,
    position_bias,
    value_routes,
    output_routes,
    places,
    coarse,
    fine,
):
    mem_count, width = memory.shape
    length = inputs.shape[0]
    head = key_weight.shape[0]
    experts = value_router.shape[0]
    pos_width = coarse.shape[1]
    keys = mem_count + length
    span = 2 * ROWS
    mem_steps = mem_count // span
    old = lambda i: (jnp.minimum(i, mem_steps - 1), 0)
    new = lambda i: (jnp.maximum(i - mem_steps, 0), 0)
    every = lambda i: (i, 0)
    row = lambda size, index: pl.BlockSpec((span, size), index)
    turned = lambda index: (lambda i: index(i)[::-1])
    return pl.pallas_call(
        functools.partial(front_body, head, experts, length, 2 * mem_count),
        out_shape=(
            jax.ShapeDtypeStruct((keys, width), BF16),
            jax.ShapeDtypeStruct((keys, LANES + pos_width), BF16),
            jax.ShapeDtypeStruct((keys, LANES), BF16),
            jax.ShapeDtypeStruct((keys, LANES), F32),
            jax.ShapeDtypeStruct((length, LANES), BF16),
            jax.ShapeDtypeStruct((length, LANES), BF16),
            jax.ShapeDtypeStruct((8, LANES), F32),
            jax.ShapeDtypeStruct((length, keys), BF16),
            jax.ShapeDtypeStruct((length, LANES), BF16),
        ),
        grid=(keys // span,),
        in_specs=[
            row(width, old),
            row(width, new),
            whole(gains),
            whole(biases),
            whole(key_weight),
            whole(value_weight),
            whole(value_router),
            whole(query_weight),
            whole(output_router),
            whole(position_weight),
            whole(content_bias),
            whole(position_bias),
            pl.BlockSpec((value_routes.shape[0], span), turned(every)),
            pl.BlockSpec((output_routes.shape[0], span), turned(new)),
            pl.BlockSpec((1, span), turned(old)),
            whole(coarse),
            whole(fine),
        ],
        out_specs=(
            row(width, every),
            row(LANES + pos_width, every),
            row(LANES, every),
            row(LANES, every),
            row(LANES, new),
            row(LANES, new),
            fixed((8, LANES)),
            row(keys, new),
            row(LANES, new),
        ),
        scratch_shapes=[
            pltpu.VMEM((LANES * (2 + experts), width), BF16),
            pltpu.VMEM((8, LANES), F32),
            pltpu.VMEM((keys, LANES + pos_width), BF16),
            pltpu.VMEM((keys, LANES), BF16),
            pltpu.VMEM((span, LANES + pos_width), BF16),
        ],
        compiler_params=params(),
        cost_estimate=cost(30 * FLOPS_US, 30e6),
        name="front",
    )(
        memory,
        inputs,
        gains,
        biases,
        key_weight,
        value_weight,
        value_router,
        query_weight,
        output_router,
        position_weight,
        content_bias,
        position_bias,
        value_routes,
        output_routes,
        places,
        coarse,
        fine,
    )


def attend_back_body(head, heads, shift, me_ref, *refs):
    grad_refs = refs[0:heads]
    (
        probs_ref,
        key_cat_ref,
        values_ref,
        content_ref,
        bias_ref,
        coarse_ref,
        fine_ref,
        position_ref,
        normed_ref,
        grad_keys_ref,
        grad_query_ref,
        weight_ref,
        sums_ref,
        position_scratch,
        relative_scratch,
        grad_scratch,
    ) = refs[heads:]
    step = pl.program_id(0)
    keys = key_cat_ref.shape[0]
    length = pl.num_programs(0) * ROWS
    freq = coarse_ref.shape[1] // 2
    scale = head ** (-0.5)

    @pl.when(step == 0)
    def _():
        grad_keys_ref[...] = jnp.zeros_like(grad_keys_ref)
        weight_ref[...] = jnp.zeros_like(weight_ref)
        sums_ref[...] = jnp.zeros_like(sums_ref)
        position_scratch[...] = jnp.zeros_like(position_scratch)
        position_scratch[0:head, :] = position_ref[...]
        for distance, grad_ref in enumerate(grad_refs):
            grad_scratch[jnp.bitwise_xor(me_ref[0], distance)] = grad_ref[0]

    lane = lane_index(ROWS)
    packed = grad_scratch[step]
    upstream = jnp.where(lane < head, packed, jnp.zeros_like(packed))
    place = lax.broadcasted_iota(jnp.int32, (1, ROWS), 1) + step * ROWS + shift
    cosine, sine = angles(place, coarse_ref, fine_ref)

    def variant(block):
        def run():
            seen = keys - length_static + (block + 1) * ROWS
            weights_low = probs_ref[:, 0:seen]
            weights = weights_low.astype(F32)
            grad_weights = dot_last(upstream, values_ref[0:seen, :])
            inner = jnp.sum(grad_weights * weights, axis=1, keepdims=True)
            grad_scores = (weights * (grad_weights - inner)).astype(BF16)
            grad_keys_ref[:, 0:seen] += dot_first(content_ref[...], grad_scores) * scale
            grad_query = dot_plain(grad_scores, key_cat_ref[0:seen, :]) * scale
            grad_content = grad_query[:, 0:LANES]
            grad_sin = grad_query[:, LANES : LANES + freq]
            grad_cos = grad_query[:, LANES + freq :]
            relative_scratch[:, 0:freq] = (grad_sin * sine - grad_cos * cosine).astype(BF16)
            relative_scratch[:, freq:] = (grad_sin * cosine + grad_cos * sine).astype(BF16)
            relative = relative_scratch[...]
            grad_bias = dot_last(relative, position_scratch[...])
            weight_ref[LANES:, :] += dot_first(bias_ref[...], relative)
            sums_ref[0:1, :] += jnp.sum(grad_content, axis=0, keepdims=True)
            sums_ref[1:2, :] += jnp.sum(grad_bias, axis=0, keepdims=True)
            both = jnp.where(lane < head, (grad_content + grad_bias).astype(BF16), packed)
            grad_query_ref[...] = both
            weight_ref[0:LANES, :] += dot_first(both, normed_ref[...])

        return run

    length_static = heads * ROWS
    for block in range(length_static // ROWS):
        pl.when(step == block)(variant(block))


def attend_back(
    me,
    grads,
    probs,
    key_cat,
    values,
    content_query,
    bias_query,
    coarse,
    fine,
    position_weight,
    normed,
):
    length, keys = probs.shape
    head, pos_width = position_weight.shape
    width = normed.shape[1]
    mem_blocks = (keys - length) // ROWS
    heads = len(grads)
    every = lambda i, me_ref: (i, 0)
    row = lambda size: pl.BlockSpec((ROWS, size), every)
    return pl.pallas_call(
        functools.partial(attend_back_body, head, heads, 2 * (keys - length)),
        out_shape=(
            jax.ShapeDtypeStruct((LANES, keys), F32),
            jax.ShapeDtypeStruct((length, LANES), BF16),
            jax.ShapeDtypeStruct((2 * LANES, width), F32),
            jax.ShapeDtypeStruct((8, LANES), F32),
        ),
        grid_spec=pltpu.PrefetchScalarGridSpec(
            num_scalar_prefetch=1,
            grid=(length // ROWS,),
            in_specs=[whole(grad) for grad in grads]
            + [
                row(keys),
                whole(key_cat),
                whole(values),
                row(LANES),
                row(LANES),
                whole(coarse),
                whole(fine),
                whole(position_weight),
                pl.BlockSpec((ROWS, width), lambda i, me_ref: (i + mem_blocks, 0)),
            ],
            out_specs=(
                fixed((LANES, keys)),
                row(LANES),
                fixed((2 * LANES, width)),
                fixed((8, LANES)),
            ),
            scratch_shapes=[
                pltpu.VMEM((LANES, pos_width), BF16),
                pltpu.VMEM((ROWS, pos_width), BF16),
                pltpu.VMEM((heads, ROWS, LANES), BF16),
            ],
        ),
        compiler_params=params(),
        cost_estimate=cost(17 * FLOPS_US, 25e6),
        name="attend_back",
    )(
        me,
        *grads,
        probs,
        key_cat,
        values,
        content_query,
        bias_query,
        coarse,
        fine,
        position_weight,
        normed,
    )


def value_back_body(head, experts, heads, me_ref, table_ref, *refs):
    grad_refs = refs[0:heads]
    (
        probs_ref,
        normed_ref,
        gate_ref,
        grad_values_ref,
        keep_ref,
        send_ref,
        grad_scratch,
        packed_scratch,
        acc,
    ) = refs[heads:]
    step = pl.program_id(0)

    @pl.when(step == 0)
    def _():
        lane = lane_index(ROWS)
        for distance, grad_ref in enumerate(grad_refs):
            start = pl.multiple_of(jnp.bitwise_xor(me_ref[0], distance) * ROWS, ROWS)
            piece = grad_ref[0]
            grad_scratch[pl.ds(start, ROWS), :] = jnp.where(
                lane < head, piece, jnp.zeros_like(piece)
            )
        packed_scratch[...] = jnp.zeros_like(packed_scratch)
        acc[...] = jnp.zeros_like(acc)

    grad_values = dot_first(grad_scratch[...], probs_ref[...])
    grad_values_ref[...] = grad_values
    gates = gate_ref[...].T
    for e in range(experts):
        packed_scratch[e * head : (e + 1) * head, :] = (
            gates[head + e : head + e + 1, :] * grad_values[0:head, :]
        ).astype(BF16)
    acc[...] += dot_plain(packed_scratch[...], normed_ref[...])

    @pl.when(step == pl.num_programs(0) - 1)
    def _():
        half, chunk, _ = keep_ref.shape
        for place in range(half):
            start = pl.multiple_of(table_ref[place] * chunk, 8)
            keep_ref[place] = acc[pl.ds(start, chunk), :].astype(BF16)
            start = pl.multiple_of(table_ref[half + place] * chunk, 8)
            send_ref[place] = acc[pl.ds(start, chunk), :].astype(BF16)


def value_back(me, table, grads, probs, normed, gates, head, experts):
    heads = len(grads)
    length, keys = probs.shape
    width = normed.shape[1]
    count = table.shape[0]
    span = 2 * ROWS
    rows = experts * head
    rows = rows + -rows % (8 * count)
    half = jax.ShapeDtypeStruct((count // 2, rows // count, width), BF16)
    return pl.pallas_call(
        functools.partial(value_back_body, head, experts, heads),
        out_shape=(jax.ShapeDtypeStruct((LANES, keys), F32), half, half),
        grid_spec=pltpu.PrefetchScalarGridSpec(
            num_scalar_prefetch=2,
            grid=(keys // span,),
            in_specs=[whole(grad) for grad in grads]
            + [
                pl.BlockSpec((length, span), lambda i, *_: (0, i)),
                pl.BlockSpec((span, width), lambda i, *_: (i, 0)),
                pl.BlockSpec((span, LANES), lambda i, *_: (i, 0)),
            ],
            out_specs=(
                pl.BlockSpec((LANES, span), lambda i, *_: (0, i)),
                fixed(half.shape),
                fixed(half.shape),
            ),
            scratch_shapes=[
                pltpu.VMEM((length, LANES), BF16),
                pltpu.VMEM((rows, span), BF16),
                pltpu.VMEM((rows, width), F32),
            ],
        ),
        compiler_params=params(),
        cost_estimate=cost(8 * FLOPS_US, 10e6),
        name="value_back",
    )(me, table, *grads, probs, normed, gates)


def spread_weights(head, experts, weight_refs, scratch):
    scratch[...] = jnp.zeros_like(scratch)
    for j, weight_ref in enumerate(weight_refs):
        for e in range(experts):
            start = LANES * (experts * j + e)
            scratch[start : start + head, :] = weight_ref[e * head : (e + 1) * head, :]


def gate_spread(head, experts):
    shape = (LANES, experts * LANES)
    row = lax.broadcasted_iota(jnp.int32, shape, 0) - head
    block = lax.broadcasted_iota(jnp.int32, shape, 1) // LANES
    return ((row == block) | (row == block + experts)).astype(BF16)


def forward_body(head, experts, heads, place_ref, down_table_ref, up_table_ref, *refs):
    pair = 2
    attended_refs = [refs[part * heads : (part + 1) * heads] for part in range(pair)]
    rest = refs[pair * heads :]
    weight_refs = rest[0:heads]
    rest = rest[heads:]
    inputs_refs = rest[0:pair]
    cotangent_refs = rest[pair : 2 * pair]
    (
        up_ref,
        down_ref,
        gains_ref,
        biases_ref,
        resid_ref,
        grad_normed_ref,
        share_ref,
        down_keep_ref,
        down_send_ref,
        up_keep_ref,
        up_send_ref,
        weight_scratch,
        mixed_scratch,
        active_scratch,
        normed_scratch,
        upper_scratch,
        cotangent_scratch,
        down_acc,
        up_acc,
    ) = rest[2 * pair :]
    step = pl.program_id(0)
    final = pl.num_programs(0) - 1

    @pl.when(step == 0)
    def _():
        spread_weights(head, experts, weight_refs, weight_scratch)

    lane = lane_index(ROWS)
    spread = gate_spread(head, experts)
    for part in range(pair):
        piece = slice(part * ROWS, (part + 1) * ROWS)
        for j, attended_ref in enumerate(attended_refs[part]):
            packed = attended_ref[...]
            gate = dot_plain(packed, spread)
            attended = jnp.where(lane < head, packed.astype(F32), 0.0)
            for e in range(experts):
                start = LANES * (experts * j + e)
                mixed_scratch[piece, start : start + LANES] = (
                    attended * gate[:, e * LANES : (e + 1) * LANES]
                ).astype(BF16)
    mixed_out = dot_plain(mixed_scratch[...], weight_scratch[...])
    for part in range(pair):
        piece = slice(part * ROWS, (part + 1) * ROWS)
        cotangent = cotangent_refs[part][...]
        cotangent_scratch[piece, :] = cotangent
        resid = inputs_refs[part][...].astype(F32) + mixed_out[piece, :]
        if part == 0:

            @pl.when(step == final)
            def _():
                resid_ref[...] = resid

        unit, _ = unit_rows(resid)
        normed = (unit * gains_ref[1:2, :] + biases_ref[1:2, :]).astype(BF16)
        normed_scratch[piece, :] = normed
        upper = dot_plain(normed, up_ref[...])
        active, slope = gelu_parts(upper)
        active = active.astype(BF16)
        active_scratch[piece, :] = active
        grad_upper = (dot_last(cotangent, down_ref[...]) * slope).astype(BF16)
        upper_scratch[piece, :] = grad_upper
        grad_normed_ref[part] = dot_last(grad_upper, up_ref[...]).astype(BF16)
        share_ref[part] = dot_plain(active, down_ref[...]).astype(BF16)
    down_grad = dot_first(active_scratch[...], cotangent_scratch[...])
    up_grad = dot_first(normed_scratch[...], upper_scratch[...])

    @pl.when(step == 0)
    def _():
        down_acc[...] = down_grad
        up_acc[...] = up_grad

    @pl.when(step > 0)
    def _():
        down_acc[...] += down_grad
        up_acc[...] += up_grad

    @pl.when(step == final)
    def _():
        for table_ref, acc, keep_ref, send_ref in (
            (down_table_ref, down_acc, down_keep_ref, down_send_ref),
            (up_table_ref, up_acc, up_keep_ref, up_send_ref),
        ):
            half, chunk, _ = keep_ref.shape
            for place in range(half):
                start = pl.multiple_of(table_ref[place] * chunk, chunk)
                keep_ref[place] = acc[pl.ds(start, chunk), :].astype(BF16)
                start = pl.multiple_of(table_ref[half + place] * chunk, chunk)
                send_ref[place] = acc[pl.ds(start, chunk), :].astype(BF16)


def forward_ffn(
    places,
    down_table,
    up_table,
    attended,
    weights,
    inputs,
    cotangent,
    up,
    down,
    gains,
    biases,
    experts,
):
    heads = len(attended)
    length, width = inputs.shape
    head = weights[0].shape[0] // experts
    hidden = up.shape[1]
    blocks = length // ROWS
    count = down_table.shape[0]
    chunk = hidden // count
    steps = blocks // 2
    place = lambda i, part: (steps - 1 - i) * 2 + part
    row = lambda size, part: pl.BlockSpec(
        (ROWS, size), lambda i, place_ref, *_: (place_ref[place(i, part)], 0)
    )
    relative = pl.BlockSpec((2, ROWS, width), lambda i, *_: (steps - 1 - i, 0, 0))
    half = lambda rows: jax.ShapeDtypeStruct((count // 2, rows, width), BF16)
    return pl.pallas_call(
        functools.partial(forward_body, head, experts, heads),
        out_shape=(
            jax.ShapeDtypeStruct((ROWS, width), F32),
            jax.ShapeDtypeStruct((blocks, ROWS, width), BF16),
            jax.ShapeDtypeStruct((blocks, ROWS, width), BF16),
            half(chunk),
            half(chunk),
            half(width // count),
            half(width // count),
        ),
        grid_spec=pltpu.PrefetchScalarGridSpec(
            num_scalar_prefetch=3,
            grid=(steps,),
            in_specs=[row(LANES, 0) for _ in attended]
            + [row(LANES, 1) for _ in attended]
            + [whole(weight) for weight in weights]
            + [row(width, 0), row(width, 1), row(width, 0), row(width, 1)]
            + [whole(up), whole(down), whole(gains), whole(biases)],
            out_specs=(
                fixed((ROWS, width)),
                relative,
                relative,
                fixed((count // 2, chunk, width)),
                fixed((count // 2, chunk, width)),
                fixed((count // 2, width // count, hidden)),
                fixed((count // 2, width // count, hidden)),
            ),
            scratch_shapes=[
                pltpu.VMEM((heads * experts * LANES, width), BF16),
                pltpu.VMEM((2 * ROWS, heads * experts * LANES), BF16),
                pltpu.VMEM((2 * ROWS, hidden), BF16),
                pltpu.VMEM((2 * ROWS, width), BF16),
                pltpu.VMEM((2 * ROWS, hidden), BF16),
                pltpu.VMEM((2 * ROWS, width), BF16),
                pltpu.VMEM((hidden, width), F32),
                pltpu.VMEM((width, hidden), F32),
            ],
        ),
        compiler_params=params(),
        cost_estimate=cost(28 * FLOPS_US, 30e6),
        name="forward_ffn",
    )(
        places,
        down_table,
        up_table,
        *attended,
        *attended,
        *weights,
        inputs,
        inputs,
        cotangent,
        cotangent,
        up,
        down,
        gains,
        biases,
    )


def second_norm_back_body(head, experts, heads, me_ref, *refs):
    attended_refs = refs[0:heads]
    weight_refs = refs[heads : 2 * heads]
    (
        left_ref,
        right_ref,
        resid_ref,
        cotangent_ref,
        gains_ref,
        grad_resid_ref,
        low_ref,
        packed_ref,
        sums_ref,
        weight_scratch,
        product_scratch,
    ) = refs[2 * heads :]
    spread_weights(head, experts, weight_refs, weight_scratch)
    unit, inverse = unit_rows(resid_ref[...])
    grad = left_ref[0].astype(F32) + right_ref[0].astype(F32)
    sums_ref[...] = jnp.zeros_like(sums_ref)
    sums_ref[2:3, :] = jnp.sum(grad * unit, axis=0, keepdims=True)
    sums_ref[3:4, :] = jnp.sum(grad, axis=0, keepdims=True)
    grad_resid = cotangent_ref[...].astype(F32) + norm_backward(
        grad, unit, inverse, gains_ref[1:2, :]
    )
    grad_resid_ref[...] = grad_resid
    low = grad_resid.astype(BF16)
    low_ref[0] = low
    grad_mixed = dot_last(low, weight_scratch[...])
    lane = lane_index(ROWS)
    spread = gate_spread(head, experts)
    collect = spread.T[:, 0:LANES]
    for j, attended_ref in enumerate(attended_refs):
        packed = attended_ref[...]
        gate = dot_plain(packed, spread)
        attended = jnp.where(lane < head, packed.astype(F32), 0.0)
        total = jnp.zeros((ROWS, LANES), F32)
        for e in range(experts):
            start = LANES * (experts * j + e)
            block = slice(e * LANES, (e + 1) * LANES)
            piece = grad_mixed[:, start : start + LANES]
            total = total + gate[:, block] * piece
            product_scratch[:, block] = piece * attended
        product = product_scratch[...]
        lead = product.astype(BF16)
        rest = (product - lead.astype(F32)).astype(BF16)
        logits = dot_plain(lead, collect) + dot_plain(rest, collect)
        own = packed.astype(F32)
        own = own + pltpu.roll(own, LANES - experts, 1)
        logits = logits * own * (1.0 - own)
        total = jnp.where((lane >= head) & (lane < head + experts), logits, total)
        packed_ref[j] = total.astype(BF16)


def second_norm_back(me, attended, weights, left, right, resid, cotangent, gains, experts):
    heads = len(attended)
    width = resid.shape[1]
    head = weights[0].shape[0] // experts
    own = lambda i, me_ref: (me_ref[0], 0)
    row = lambda size: pl.BlockSpec((ROWS, size), own)
    return pl.pallas_call(
        functools.partial(second_norm_back_body, head, experts, heads),
        out_shape=(
            jax.ShapeDtypeStruct((ROWS, width), F32),
            jax.ShapeDtypeStruct((1, ROWS, width), BF16),
            jax.ShapeDtypeStruct((heads, ROWS, LANES), BF16),
            jax.ShapeDtypeStruct((8, width), F32),
        ),
        grid_spec=pltpu.PrefetchScalarGridSpec(
            num_scalar_prefetch=1,
            grid=(1,),
            in_specs=[row(LANES) for _ in attended]
            + [whole(weight) for weight in weights]
            + [whole(left), whole(right), whole(resid), row(width), whole(gains)],
            out_specs=(
                fixed((ROWS, width)),
                fixed((1, ROWS, width)),
                fixed((heads, ROWS, LANES)),
                fixed((8, width)),
            ),
            scratch_shapes=[
                pltpu.VMEM((heads * experts * LANES, width), BF16),
                pltpu.VMEM((ROWS, experts * LANES), F32),
            ],
        ),
        compiler_params=params(),
        cost_estimate=cost(7 * FLOPS_US, 12e6),
        name="second_norm_back",
    )(me, *attended, *weights, left, right, resid, cotangent, gains)


def output_grad_body(
    head, experts, place_ref, table_ref, attended_ref, *refs
):
    blocks = place_ref.shape[0]
    grad_refs = refs[0:blocks]
    keep_ref, send_ref, mixed, rows, acc = refs[blocks:]
    half, chunk, _ = keep_ref.shape
    for place, grad_ref in enumerate(grad_refs):
        start = pl.multiple_of(place_ref[place] * ROWS, ROWS)
        packed = attended_ref[pl.ds(start, ROWS), :].astype(F32).T
        piece = slice(place * ROWS, (place + 1) * ROWS)
        for e in range(experts):
            gate = packed[head + e : head + e + 1, :] + packed[
                head + experts + e : head + experts + e + 1, :
            ]
            mixed[e * head : (e + 1) * head, piece] = (packed[0:head, :] * gate).astype(BF16)
        rows[piece, :] = grad_ref[0]
    mixed[experts * head :, :] = jnp.zeros_like(mixed[experts * head :, :])
    acc[...] = dot_plain(mixed[...], rows[...])
    for place in range(half):
        start = pl.multiple_of(table_ref[place] * chunk, 8)
        keep_ref[place] = acc[pl.ds(start, chunk), :].astype(BF16)
        start = pl.multiple_of(table_ref[half + place] * chunk, 8)
        send_ref[place] = acc[pl.ds(start, chunk), :].astype(BF16)


def output_grad(places, table, attended, grads, head, experts):
    count = table.shape[0]
    length = attended.shape[0]
    width = grads[0].shape[2]
    rows = experts * head
    rows = rows + -rows % (8 * count)
    chunk = rows // count
    half = jax.ShapeDtypeStruct((count // 2, chunk, width), BF16)
    return pl.pallas_call(
        functools.partial(output_grad_body, head, experts),
        out_shape=(half, half),
        grid_spec=pltpu.PrefetchScalarGridSpec(
            num_scalar_prefetch=2,
            grid=(1,),
            in_specs=[whole(attended)] + [whole(grad) for grad in grads],
            out_specs=(fixed(half.shape), fixed(half.shape)),
            scratch_shapes=[
                pltpu.VMEM((rows, length), BF16),
                pltpu.VMEM((length, width), BF16),
                pltpu.VMEM((rows, width), F32),
            ],
        ),
        compiler_params=params(),
        cost_estimate=cost(5 * FLOPS_US, 4e6),
        name="output_grad",
    )(places, table, attended, *grads)


def project_back_body(head, experts, place_ref, table_ref, *refs):
    pair = 2
    groups = []
    for index in range(7):
        groups.append(refs[index * pair : (index + 1) * pair])
    normed_refs, grad_keys_refs, grad_values_refs, gate_refs, query_refs, memory_refs, inputs_refs = (
        groups
    )
    (
        key_ref,
        value_ref,
        value_router_ref,
        query_ref,
        output_router_ref,
        query_grad_ref,
        bias_sums_ref,
        counts_ref,
        grad_current_ref,
        keep_ref,
        send_ref,
        sums_ref,
        extra_ref,
        acc,
        weight_scratch,
        packed_scratch,
        normed_scratch,
    ) = refs[7 * pair :]
    step = pl.program_id(0)
    final = pl.num_programs(0) - 1
    split = LANES * (1 + experts)
    cur_steps = place_ref.shape[0] // pair
    current = step < cur_steps

    @pl.when(step == 0)
    def _():
        acc[...] = jnp.zeros_like(acc)
        sums_ref[...] = jnp.zeros_like(sums_ref)
        weight_scratch[...] = jnp.zeros_like(weight_scratch)
        packed_scratch[...] = jnp.zeros_like(packed_scratch)
        fill_weights(head, experts, key_ref, value_router_ref, value_ref, weight_scratch)
        weight_scratch[split : split + head, :] = query_ref[...]
        weight_scratch[split + head : split + head + experts, :] = output_router_ref[...]

    for part in range(pair):
        piece = slice(part * ROWS, (part + 1) * ROWS)
        normed = normed_refs[part][...]
        normed_scratch[piece, :] = normed
        gates = gate_refs[part][...].T
        grad_values = grad_values_refs[part][0:head, :]
        expert_values = dot_last(weight_scratch[LANES:split, :], normed)
        packed_scratch[0:head, piece] = grad_keys_refs[part][0:head, :].astype(BF16)
        logits = []
        for e in range(experts):
            start = LANES * (e + 1)
            gate = gates[head + e : head + e + 1, :]
            packed_scratch[start : start + head, piece] = (gate * grad_values).astype(BF16)
            values = expert_values[start - LANES : start - LANES + head, :]
            logits.append(
                jnp.sum(values * grad_values, axis=0, keepdims=True) * (gate * (1.0 - gate))
            )
        packed_scratch[head : head + experts, piece] = jnp.concatenate(logits, axis=0).astype(BF16)
    acc[0:LANES, :] += dot_plain(packed_scratch[0:LANES, :], normed_scratch[...])
    grads = dot_first(packed_scratch[...], weight_scratch[0:split, :])
    for part in range(pair):
        piece = slice(part * ROWS, (part + 1) * ROWS)
        grad = grads[piece, :]
        more = dot_plain(query_refs[part][...], weight_scratch[split:, :])
        grad = grad + jnp.where(current, more, 0.0)
        rows = jnp.where(current, inputs_refs[part][...], memory_refs[part][...]).astype(F32)
        unit, _ = unit_rows(rows)
        sums_ref[0:1, :] += jnp.sum(grad * unit, axis=0, keepdims=True)
        sums_ref[1:2, :] += jnp.sum(grad, axis=0, keepdims=True)

        @pl.when(current)
        def _():
            grad_current_ref[part] = grad.astype(BF16)

    @pl.when(step == final)
    def _():
        acc[LANES:, :] = query_grad_ref[...]
        half, chunk, _ = keep_ref.shape
        for place in range(half):
            start = pl.multiple_of(table_ref[place] * chunk, 8)
            keep_ref[place] = acc[pl.ds(start, chunk), :].astype(BF16)
            start = pl.multiple_of(table_ref[half + place] * chunk, 8)
            send_ref[place] = acc[pl.ds(start, chunk), :].astype(BF16)
        extra_ref[...] = jnp.zeros_like(extra_ref)
        extra_ref[0:2, 0:LANES] = bias_sums_ref[0:2, :]
        extra_ref[2:4, 0:LANES] = counts_ref[0:2, :]


def project_back(
    places,
    table,
    normed,
    grad_keys,
    grad_values,
    gates,
    grad_query,
    memory,
    inputs,
    key_weight,
    value_weight,
    value_router,
    query_weight,
    output_router,
    query_grads,
    bias_sums,
    counts,
):
    count = table.shape[0]
    keys, width = normed.shape
    length = inputs.shape[0]
    head = key_weight.shape[0]
    experts = value_router.shape[0]
    mem_blocks = (keys - length) // ROWS
    cur_blocks = length // ROWS
    cur_steps = cur_blocks // 2
    split = LANES * (1 + experts)
    fresh = lambda i, part, place_ref: place_ref[2 * jnp.minimum(i, cur_steps - 1) + part]
    past = lambda i, part: 2 * jnp.maximum(i - cur_steps, 0) + part
    every = lambda i, part, place_ref: jnp.where(
        i < cur_steps, fresh(i, part, place_ref) + mem_blocks, past(i, part)
    )

    def rows(size, index):
        return [
            pl.BlockSpec((ROWS, size), lambda i, place_ref, _, p=part: (index(i, p, place_ref), 0))
            for part in range(2)
        ]

    def columns(index):
        return [
            pl.BlockSpec((LANES, ROWS), lambda i, place_ref, _, p=part: (0, index(i, p, place_ref)))
            for part in range(2)
        ]

    half = jax.ShapeDtypeStruct((count // 2, 3 * LANES // count, width), BF16)
    return pl.pallas_call(
        functools.partial(project_back_body, head, experts),
        out_shape=(
            jax.ShapeDtypeStruct((cur_blocks, ROWS, width), BF16),
            half,
            half,
            jax.ShapeDtypeStruct((8, width), F32),
            jax.ShapeDtypeStruct((8, width), F32),
        ),
        grid_spec=pltpu.PrefetchScalarGridSpec(
            num_scalar_prefetch=2,
            grid=(keys // (2 * ROWS),),
            in_specs=rows(width, every)
            + columns(every)
            + columns(every)
            + rows(LANES, every)
            + rows(LANES, fresh)
            + rows(width, lambda i, part, place_ref: past(i, part))
            + rows(width, fresh)
            + [
                whole(key_weight),
                whole(value_weight),
                whole(value_router),
                whole(query_weight),
                whole(output_router),
                whole(query_grads),
                whole(bias_sums),
                whole(counts),
            ],
            out_specs=(
                pl.BlockSpec(
                    (2, ROWS, width), lambda i, *_: (jnp.minimum(i, cur_steps - 1), 0, 0)
                ),
                fixed(half.shape),
                fixed(half.shape),
                fixed((8, width)),
                fixed((8, width)),
            ),
            scratch_shapes=[
                pltpu.VMEM((3 * LANES, width), F32),
                pltpu.VMEM((split + LANES, width), BF16),
                pltpu.VMEM((split, 2 * ROWS), BF16),
                pltpu.VMEM((2 * ROWS, width), BF16),
            ],
        ),
        compiler_params=params(),
        cost_estimate=cost(16 * FLOPS_US, 20e6),
        name="project_back",
    )(
        places,
        table,
        normed,
        normed,
        grad_keys,
        grad_keys,
        grad_values,
        grad_values,
        gates,
        gates,
        grad_query,
        grad_query,
        memory,
        memory,
        inputs,
        inputs,
        key_weight,
        value_weight,
        value_router,
        query_weight,
        output_router,
        query_grads,
        bias_sums,
        counts,
    )


def first_norm_back(me, left, right, inputs, grad_resid, gains):
    width = inputs.shape[1]

    def body(me_ref, left_ref, right_ref, inputs_ref, resid_ref, gains_ref, out_ref):
        unit, inverse = unit_rows(inputs_ref[...].astype(F32))
        grad = left_ref[0].astype(F32) + right_ref[0].astype(F32)
        out_ref[0] = (
            resid_ref[...] + norm_backward(grad, unit, inverse, gains_ref[0:1, :])
        ).astype(BF16)

    return pl.pallas_call(
        body,
        out_shape=jax.ShapeDtypeStruct((1, ROWS, width), BF16),
        grid_spec=pltpu.PrefetchScalarGridSpec(
            num_scalar_prefetch=1,
            grid=(1,),
            in_specs=[
                whole(left),
                whole(right),
                pl.BlockSpec((ROWS, width), lambda i, me_ref: (me_ref[0], 0)),
                whole(grad_resid),
                whole(gains),
            ],
            out_specs=fixed((1, ROWS, width)),
        ),
        compiler_params=params(),
        cost_estimate=cost(3 * FLOPS_US, 4e6),
        name="first_norm_back",
    )(me, left, right, inputs, grad_resid, gains)


def place_rows(places, pieces):
    _, rows, width = pieces[0].shape
    count = len(pieces)

    def body(place_ref, *refs):
        out_ref = refs[count]
        for place in range(count):
            start = pl.multiple_of(place_ref[place] * rows, rows)
            out_ref[pl.ds(start, rows), :] = refs[place][0]

    return pl.pallas_call(
        body,
        out_shape=jax.ShapeDtypeStruct((count * rows, width), pieces[0].dtype),
        grid_spec=pltpu.PrefetchScalarGridSpec(
            num_scalar_prefetch=1,
            grid=(1,),
            in_specs=[whole(piece) for piece in pieces],
            out_specs=fixed((count * rows, width)),
        ),
        compiler_params=params(),
        cost_estimate=cost(3 * FLOPS_US, 4e6),
        name="place_rows",
    )(places, *pieces)


def unpack_rows(table, own, got, rows_out):
    half, rows, width = own.shape
    total = 2 * half * rows
    part = width // 2

    def body(table_ref, own_ref, got_ref, out_ref, *scratch):
        rows_ref = scratch[0] if scratch else out_ref
        for place in range(half):
            start = pl.multiple_of(table_ref[place] * rows, 8)
            rows_ref[pl.ds(start, rows), :] = own_ref[place].astype(F32)
            start = pl.multiple_of(table_ref[half + place] * rows, 8)
            rows_ref[pl.ds(start, rows), :] = got_ref[place].astype(F32)
        if scratch:
            out_ref[...] = rows_ref[0:rows_out, :]

    chunks = pl.BlockSpec((half, rows, part), lambda i, _: (0, 0, i))
    return pl.pallas_call(
        body,
        out_shape=jax.ShapeDtypeStruct((rows_out, width), F32),
        grid_spec=pltpu.PrefetchScalarGridSpec(
            num_scalar_prefetch=1,
            grid=(2,),
            in_specs=[chunks, chunks],
            out_specs=pl.BlockSpec((rows_out, part), lambda i, _: (0, i)),
            scratch_shapes=[] if total == rows_out else [pltpu.VMEM((total, part), F32)],
        ),
        compiler_params=params(),
        cost_estimate=cost(5 * FLOPS_US, 6e6),
        name="unpack_rows",
    )(table, own, got)


def unpack_heads(table, own, got, head, experts):
    half, chunk, width = own.shape

    def body(
        table_ref,
        own_ref,
        got_ref,
        key_ref,
        value_router_ref,
        query_ref,
        output_router_ref,
        position_ref,
        rows,
    ):
        for place in range(half):
            start = pl.multiple_of(table_ref[place] * chunk, 8)
            rows[pl.ds(start, chunk), :] = own_ref[place].astype(F32)
            start = pl.multiple_of(table_ref[half + place] * chunk, 8)
            rows[pl.ds(start, chunk), :] = got_ref[place].astype(F32)
        key_ref[...] = rows[0:head, :]
        value_router_ref[...] = rows[head : head + experts, :]
        query_ref[...] = rows[LANES : LANES + head, :]
        output_router_ref[...] = rows[LANES + head : LANES + head + experts, :]
        position_ref[...] = rows[2 * LANES : 2 * LANES + head, :]

    one = jax.ShapeDtypeStruct((head, width), F32)
    few = jax.ShapeDtypeStruct((experts, width), F32)
    return pl.pallas_call(
        body,
        out_shape=(one, few, one, few, one),
        grid_spec=pltpu.PrefetchScalarGridSpec(
            num_scalar_prefetch=1,
            grid=(1,),
            in_specs=[whole(own), whole(got)],
            out_specs=tuple(fixed(kind.shape) for kind in (one, few, one, few, one)),
            scratch_shapes=[pltpu.VMEM((2 * half * chunk, width), F32)],
        ),
        compiler_params=params(),
        cost_estimate=cost(3 * FLOPS_US, 3e6),
        name="unpack_heads",
    )(table, own, got)


def unpack_small(me, norms, extra, head, share):
    def body(
        me_ref,
        norms_ref,
        extra_ref,
        gains_ref,
        biases_ref,
        content_ref,
        position_ref,
        counts_ref,
    ):
        start = pl.multiple_of(me_ref[0] * share, LANES)
        gains_ref[0:1, :] = norms_ref[0:1, pl.ds(start, share)]
        gains_ref[1:2, :] = norms_ref[2:3, pl.ds(start, share)]
        biases_ref[0:1, :] = norms_ref[1:2, pl.ds(start, share)]
        biases_ref[1:2, :] = norms_ref[3:4, pl.ds(start, share)]
        content_ref[...] = extra_ref[0:1, 0:head]
        position_ref[...] = extra_ref[1:2, 0:head]
        counts_ref[...] = extra_ref[2:4, 0:LANES].astype(jnp.int32)

    shapes = (
        ((2, share), F32),
        ((2, share), F32),
        ((1, head), F32),
        ((1, head), F32),
        ((2, LANES), jnp.int32),
    )
    return pl.pallas_call(
        body,
        out_shape=tuple(jax.ShapeDtypeStruct(shape, kind) for shape, kind in shapes),
        grid_spec=pltpu.PrefetchScalarGridSpec(
            num_scalar_prefetch=1,
            grid=(1,),
            in_specs=[whole(norms), whole(extra)],
            out_specs=tuple(fixed(shape) for shape, _ in shapes),
        ),
        cost_estimate=cost(2 * FLOPS_US, 1e6),
        name="unpack_small",
    )(me, norms, extra)


def on_device(
    inputs,
    memory,
    memory_positions,
    value_routes,
    output_routes,
    norm_gains,
    norm_biases,
    query_weight,
    key_weight,
    value_weight,
    value_router,
    output_router,
    output_weight,
    position_weight,
    content_bias,
    position_bias,
    up_weight,
    down_weight,
    cotangent,
):
    length, width = inputs.shape[1:]
    mem_count = memory.shape[1]
    keys = mem_count + length
    head = query_weight.shape[1]
    experts = value_router.shape[1]
    pos_width = position_weight.shape[0]
    picks = value_routes.shape[3]
    t_index = lax.axis_index("tensor")
    me = t_index.reshape(1).astype(jnp.int32)
    t_bits = axis_bits("tensor")
    t_order = relative_order(t_bits)
    t_table = chunk_table(t_bits, "tensor")
    t_count = lax.axis_size("tensor")
    core_bit, chip_bit = t_bits
    all_bits = axis_bits("dp")
    first_bits = all_bits[:SPLITS]
    second_bits = [first_bits[1], first_bits[0]] + first_bits[2:]
    first_table = chunk_table(first_bits, "dp")
    second_table = chunk_table(second_bits, "dp")

    def bits_of(name):
        return second_bits if name in SECOND else first_bits

    def table_of(name):
        return second_table if name in SECOND else first_table

    tokens = inputs.reshape(length, width)
    upstream = cotangent.reshape(length, width)
    past = memory.reshape(mem_count, width)
    key_t = key_weight.T
    value_t = value_weight.T
    value_router_t = value_router.T
    query_t = query_weight.T
    output_router_t = output_router.T
    position_t = position_weight.T

    far_weight = swap(output_weight, "tensor", chip_bit)
    coarse = trig_tables(-2.0 * mem_count, (2 * mem_count + length) // FINE, float(FINE), pos_width)
    fine = trig_tables(0.0, FINE, 1.0, pos_width)
    (
        normed,
        key_cat,
        values,
        gates,
        content_query,
        bias_query,
        counts,
        probs,
        attended_own,
    ) = front(
        past,
        tokens,
        norm_gains,
        norm_biases,
        key_t,
        value_t,
        value_router_t,
        query_t,
        output_router_t,
        position_t,
        content_bias.reshape(1, head),
        position_bias.reshape(1, head),
        value_routes.reshape(keys, picks).T,
        output_routes.reshape(length, picks).T,
        memory_positions,
        coarse,
        fine,
    )

    totals = {}
    v = {}
    token = [attended_own]

    def tie(value):
        return after(value, *token)

    def start_sum(name, keep, send, bits):
        totals[name] = DpSum(keep, send, bits)
        totals[name].go()

    def step_sum(name):
        total = totals[name]
        if total.folded < len(total.bits):
            total.fold(*token)
            if total.folded < len(total.bits):
                total.go()
            else:
                total.back()
        else:
            total.join(*token)
            total.back()
        return total.keep

    def core_sum(held, got):
        half = held.shape[0] // 2
        return add_pieces(held[:1], got[:1]), add_pieces(held[1:half], got[1:])

    def for_core(held):
        return swap(held[held.shape[0] // 2 :], "tensor", core_bit)

    far_attended = swap(attended_own, "tensor", chip_bit)
    near_attended = swap(attended_own, "tensor", core_bit)
    far_weight = after(far_weight, attended_own)
    near_weight = swap(after(output_weight, attended_own), "tensor", core_bit)
    across_weight = swap(far_weight, "tensor", core_bit)
    across_attended = swap(far_attended, "tensor", core_bit)
    attended = [attended_own, far_attended, near_attended, across_attended]
    weights = [output_weight, far_weight, near_weight, across_weight]

    def feed_forward():
        (
            v["resid"],
            v["grad_normed"],
            v["share"],
            down_keep,
            down_send,
            up_keep,
            up_send,
        ) = forward_ffn(
            tie(t_table),
            table_of("down"),
            table_of("up"),
            attended,
            weights,
            tokens,
            upstream,
            up_weight,
            down_weight,
            norm_gains,
            norm_biases,
            experts,
        )
        v["grad_normed_got"] = for_core(v["grad_normed"])
        start_sum("down", down_keep, down_send, bits_of("down"))
        start_sum("up", up_keep, up_send, bits_of("up"))
        return down_keep

    def grad_normed_add():
        v["left"], far = core_sum(v["grad_normed"], tie(v["grad_normed_got"]))
        v["right"] = swap(far, "tensor", chip_bit)
        return far

    def second_norm():
        v["grad_resid"], low_own, packed, v["sums_two"] = second_norm_back(
            tie(me),
            attended,
            weights,
            v["left"],
            v["right"],
            v["resid"],
            upstream,
            norm_gains,
            experts,
        )
        arrived = [None] * t_count
        for place, distance in enumerate(t_order):
            piece = packed[place : place + 1]
            arrived[distance] = piece if distance == 0 else swap(piece, "tensor", distance)
        v["arrived"] = arrived
        v["low"] = [
            low_own,
            swap(low_own, "tensor", chip_bit),
            swap(low_own, "tensor", core_bit),
        ]
        return low_own

    def low_across():
        far = tie(v["low"][1])
        v["low"][1] = far
        v["low"].append(swap(far, "tensor", core_bit))
        return far

    def share_core():
        v["share"] = tie(v["share"])
        v["share_got"] = for_core(v["share"])
        return None

    def share_add():
        v["share_left"], far = core_sum(v["share"], tie(v["share_got"]))
        v["share_right"] = swap(far, "tensor", chip_bit)
        return far

    def value_grads():
        v["grad_values"], keep, send = value_back(
            tie(me), table_of("value"), v["arrived"], probs, normed, gates, head, experts
        )
        start_sum("value", keep, send, bits_of("value"))
        return v["grad_values"]

    def attention():
        v["grad_keys"], v["grad_query"], v["query_grads"], v["bias_sums"] = attend_back(
            tie(me),
            v["arrived"],
            probs,
            key_cat,
            values,
            content_query,
            bias_query,
            coarse,
            fine,
            position_t,
            normed,
        )
        return v["bias_sums"]

    def output_weight_grad():
        keep, send = output_grad(
            tie(t_table), table_of("out"), attended_own, v["low"], head, experts
        )
        start_sum("out", keep, send, bits_of("out"))
        return send

    def projections():
        v["grad_current"], keep, send, v["sums_one"], v["extra"] = project_back(
            tie(t_table),
            table_of("late"),
            normed,
            v["grad_keys"],
            v["grad_values"],
            gates,
            v["grad_query"],
            past,
            tokens,
            key_t,
            value_t,
            value_router_t,
            query_t,
            output_router_t,
            v["query_grads"],
            v["bias_sums"],
            counts,
        )
        v["grad_current_got"] = for_core(v["grad_current"])
        start_sum("late", keep, send, bits_of("late"))
        return send

    def grad_current_add():
        v["left"], far = core_sum(v["grad_current"], tie(v["grad_current_got"]))
        v["right"] = swap(far, "tensor", chip_bit)
        return far

    def first_norm():
        own = first_norm_back(
            tie(me), v["left"], v["right"], tokens, v["grad_resid"], norm_gains
        )
        v["grad_inputs"] = [
            own,
            swap(own, "tensor", chip_bit),
            swap(own, "tensor", core_bit),
        ]
        return own

    def rows_across(name):
        far = tie(v[name][1])
        v[name][1] = far
        v[name].append(swap(far, "tensor", core_bit))
        return far

    def rows_placed(name):
        v[name] = place_rows(tie(t_table), v[name])
        return v[name]

    def output_rows():
        own = (
            v["resid"][None]
            + v["share_left"].astype(F32)
            + tie(v["share_right"]).astype(F32)
        ).astype(BF16)
        v["output"] = [
            own,
            swap(own, "tensor", chip_bit),
            swap(own, "tensor", core_bit),
        ]
        return own

    def small_sum(stage):
        if stage == 0:
            total = tie(v["sums_one"]) + v["sums_two"]
            v["small_got"] = swap(total, "tensor", core_bit)
        else:
            total = v["small"] + tie(v["small_got"])
            if stage == 1:
                v["small_got"] = swap(total, "tensor", chip_bit)
            elif stage < 2 + len(all_bits):
                if stage == 2:
                    total = jnp.concatenate([total, v["extra"]], axis=0)
                v["small_got"] = swap(total, "dp", all_bits[stage - 2])
        v["small"] = total
        return total

    def small_placed():
        for stage in range(2 + len(axis_bits("dp")[:SPLITS]), 3 + len(all_bits)):
            small_sum(stage)
        small = v["small"]
        v["small_out"] = unpack_small(
            me, small[0:8], small[8:], head, width // t_count
        )
        return v["small_out"][0]

    def sum_placed(name, rows):
        total = totals[name]
        v[name] = unpack_rows(tie(table_of(name)), total.keep, total.got, rows)
        return v[name]

    def late_placed():
        total = totals["late"]
        v["late"] = unpack_heads(
            tie(table_of("late")), total.keep, total.got, head, experts
        )
        return v["late"][1]

    tasks = {
        "ffn": feed_forward,
        "gna": grad_normed_add,
        "snb": second_norm,
        "low": low_across,
        "sh": share_core,
        "sha": share_add,
        "vb": value_grads,
        "ab": attention,
        "og": output_weight_grad,
        "pb": projections,
        "gca": grad_current_add,
        "fnb": first_norm,
        "orow": output_rows,
        "oc": lambda: rows_across("output"),
        "gi": lambda: rows_across("grad_inputs"),
        "pro": lambda: rows_placed("output"),
        "pri": lambda: rows_placed("grad_inputs"),
        "nu": small_placed,
        "Du": lambda: sum_placed("down", down_weight.shape[0]),
        "Uu": lambda: sum_placed("up", up_weight.shape[0]),
        "Vu": lambda: sum_placed("value", experts * head),
        "Ou": lambda: sum_placed("out", experts * head),
        "Lu": late_placed,
    }
    for stage in range(5):
        tasks["n" + str(stage)] = functools.partial(small_sum, stage)
    sums = {"D": "down", "U": "up", "V": "value", "O": "out", "L": "late"}
    for name in ORDER:
        if name in tasks:
            done = tasks[name]()
        else:
            done = step_sum(sums[name[0]])
        token = token if done is None else [done]

    grad_gains, grad_biases, grad_content, grad_position, expert_counts = v["small_out"]
    grad_key_t, grad_value_router, grad_query_t, grad_output_router, grad_position_t = v["late"]
    return (
        v["output"].reshape(1, length, width),
        v["grad_inputs"].reshape(1, length, width),
        grad_gains,
        grad_biases,
        grad_query_t.T,
        grad_key_t.T,
        v["value"].T,
        grad_value_router.T,
        grad_output_router.T,
        v["out"],
        grad_position_t.T,
        grad_content.reshape(head),
        grad_position.reshape(head),
        v["up"],
        v["down"],
        expert_counts[:, head : head + experts],
    )


def solution(mesh):
    placed = (
        P("dp", None, None),
        P("dp", None, None),
        P("dp", None),
        P("dp", None, "tensor", None),
        P("dp", None, "tensor", None),
        P(),
        P(),
        P(None, "tensor"),
        P(None, "tensor"),
        P(None, "tensor"),
        P(None, "tensor"),
        P(None, "tensor"),
        P("tensor", None),
        P(None, "tensor"),
        P("tensor"),
        P("tensor"),
        P(None, "tensor"),
        P("tensor", None),
        P("dp", None, None),
    )
    return jax.shard_map(
        on_device,
        mesh=mesh,
        in_specs=placed,
        out_specs=(
            P("dp", None, None),
            P("dp", None, None),
            P(None, "tensor"),
            P(None, "tensor"),
            P(None, "tensor"),
            P(None, "tensor"),
            P(None, "tensor"),
            P(None, "tensor"),
            P(None, "tensor"),
            P("tensor", None),
            P(None, "tensor"),
            P("tensor"),
            P("tensor"),
            P(None, "tensor"),
            P("tensor", None),
            P(None, "tensor"),
        ),
        check_vma=False,
    )
```

```python
import functools
import math

import jax
import jax.numpy as jnp
from jax import lax
from jax.experimental import pallas as pl
from jax.experimental.pallas import tpu as pltpu
from jax.sharding import PartitionSpec as P

NORM_EPSILON = 1e-05
GELU_SCALE = 0.7978845608028654
GELU_CUBIC = 0.044715
LANES = 128
ROWS = 256
FINE = 32
SPLITS = 3
SECOND = ("up","out",)
ORDER = (
    "ffn", "gna", "sh", "sha", "snb", "F1", "orow", "vb", "F2", "low",
    "ab", "oc", "og", "F3", "pro", "L1", "pb", "n0", "W1", "n1",
    "L2", "F4", "n2", "W2", "L3", "gca", "n3", "F5", "L4", "n4",
    "W3", "fnb", "nu", "L5", "W4", "Du", "gi", "Lu", "pri", "W5",
    "Uu", "Vu", "Ou",
)
VMEM = 56 * 1024 * 1024
FLOPS_US = 1.1e9
SHRINK = 1000
BF16 = jnp.bfloat16
F32 = jnp.float32


def dot_first(left, right):
    return lax.dot_general(left, right, (((0,), (0,)), ((), ())), preferred_element_type=F32)


def dot_last(left, right):
    return lax.dot_general(left, right, (((1,), (1,)), ((), ())), preferred_element_type=F32)


def dot_plain(left, right):
    return jnp.dot(left, right, preferred_element_type=F32)


def gelu_parts(values):
    square = values * values
    tangent = jnp.tanh(GELU_SCALE * (values + GELU_CUBIC * values * square))
    half = 0.5 * (1.0 + tangent)
    slope = half + 0.5 * values * (1.0 - tangent * tangent) * (
        GELU_SCALE * (1.0 + 3.0 * GELU_CUBIC * square)
    )
    return (values * half, slope)


def unit_rows(values):
    average = jnp.mean(values, axis=-1, keepdims=True)
    centered = values - average
    spread = jnp.mean(centered * centered, axis=-1, keepdims=True)
    inverse = lax.rsqrt(spread + NORM_EPSILON)
    return (centered * inverse, inverse)


def norm_backward(upstream, unit, inverse, gain):
    grad_unit = upstream * gain
    return inverse * (
        grad_unit
        - jnp.mean(grad_unit, axis=-1, keepdims=True)
        - unit * jnp.mean(grad_unit * unit, axis=-1, keepdims=True)
    )


def lane_index(rows):
    return lax.broadcasted_iota(jnp.int32, (rows, LANES), 1)


def whole(array):
    rank = array.ndim
    return pl.BlockSpec(
        array.shape, lambda *_: (0,) * rank, pipeline_mode=pl.Buffered(1)
    )


def fixed(shape):
    return pl.BlockSpec(shape, lambda *_: (0,) * len(shape))


def params():
    return pltpu.CompilerParams(vmem_limit_bytes=VMEM)


def cost(flops, moved, special=0):
    return pl.CostEstimate(flops=int(flops) // SHRINK, bytes_accessed=int(moved) // SHRINK, transcendentals=0)


def axis_bits(name):
    count = lax.axis_size(name)
    bits = []
    bit = 1
    while bit < count:
        bits.append(bit)
        bit = bit * 2
    return bits


def relative_order(bits):
    count = 2 ** len(bits)
    order = []
    for place in range(count):
        value = 0
        for depth, bit in enumerate(bits):
            if place & (count >> (depth + 1)):
                value = value | bit
        order.append(value)
    return order


def swap(piece, name, bit):
    return lax.ppermute(piece, name, [(i, i ^ bit) for i in range(lax.axis_size(name))])


def add_pieces(left, right):
    return (left.astype(F32) + right.astype(F32)).astype(BF16)


def after(value, *others):
    return lax.optimization_barrier((value,) + others)[0]


class DpSum:
    def __init__(self, parts):
        self.keep = [keep for keep, _, _ in parts]
        self.send = [send for _, send, _ in parts]
        self.bits = [bits for _, _, bits in parts]
        self.stages = len(self.bits[0])
        self.more = [bit for bit in axis_bits("dp") if bit not in self.bits[0]]
        self.folded = 0
        self.depth = 0
        self.move(self.send, 0)

    def move(self, pieces, stage):
        bits = [bits[stage] for bits in self.bits]
        if len(pieces) > 1 and stage == self.stages - 1 and len(set(bits)) == 1:
            got = swap(jnp.concatenate(pieces, axis=0), "dp", bits[0])
            self.got = [got]
        else:
            self.got = [swap(piece, "dp", bit) for piece, bit in zip(pieces, bits)]

    def take(self, others):
        tied = lax.optimization_barrier(tuple(self.got) + tuple(others))
        got = tied[0 : len(self.got)]
        if len(got) < len(self.keep):
            got = [got[0][i : i + 1] for i in range(len(self.keep))]
        return got

    def step(self, *others):
        got = self.take(others)
        if self.folded < self.stages:
            self.folded = self.folded + 1
            if self.folded < self.stages:
                half = self.keep[0].shape[0] // 2
                self.send = [add_pieces(k[half:], g[half:]) for k, g in zip(self.keep, got)]
                self.keep = [add_pieces(k[:half], g[:half]) for k, g in zip(self.keep, got)]
                self.move(self.send, self.folded)
                return self.send
            self.keep = [add_pieces(k, g) for k, g in zip(self.keep, got)]
            for bit in self.more:
                self.keep = [add_pieces(k, swap(k, "dp", bit)) for k in self.keep]
            self.depth = self.stages
        else:
            self.keep = [jnp.concatenate([k, g], axis=0) for k, g in zip(self.keep, got)]
        self.depth = self.depth - 1
        self.move(self.keep, self.depth)
        return self.keep


def chunk_table(bits, name):
    place = jnp.bitwise_and(lax.axis_index(name), 2 ** len(bits) - 1)
    return jnp.bitwise_xor(jnp.array(relative_order(bits), jnp.int32), place)

def angles(place, coarse_ref, fine_ref):
    count = place.shape[1]
    slots = coarse_ref.shape[0] // 2
    freq = coarse_ref.shape[1] // 2
    coarse_rows = lax.broadcasted_iota(jnp.int32, (slots, count), 0)
    fine_rows = lax.broadcasted_iota(jnp.int32, (FINE, count), 0)
    coarse_hit = (coarse_rows == place // FINE).astype(BF16)
    fine_hit = (fine_rows == lax.rem(place, FINE)).astype(BF16)
    big = dot_first(coarse_hit, coarse_ref[0:slots, :]) + dot_first(
        coarse_hit, coarse_ref[slots:, :]
    )
    small = dot_first(fine_hit, fine_ref[0:FINE, :]) + dot_first(fine_hit, fine_ref[FINE:, :])
    cosine = big[:, 0:freq] * small[:, 0:freq] - big[:, freq:] * small[:, freq:]
    sine = big[:, freq:] * small[:, 0:freq] + big[:, 0:freq] * small[:, freq:]
    return cosine, sine


def trig_tables(first, count, step, pos_width):
    freq = pos_width // 2
    omega = jnp.exp(jnp.arange(freq, dtype=F32) * (-2.0 * math.log(10000.0) / pos_width))
    angle = (jnp.arange(count, dtype=F32) * step + first)[:, None] * omega
    table = jnp.concatenate([jnp.cos(angle), jnp.sin(angle)], axis=1)
    lead = lax.reduce_precision(table, 8, 7)
    return jnp.concatenate([lead, table - lead], axis=0).astype(BF16)


def fill_weights(head, experts, key_ref, router_ref, value_ref, scratch):
    scratch[0:head, :] = key_ref[...]
    scratch[head : head + experts, :] = router_ref[...]
    for e in range(experts):
        start = LANES * (e + 1)
        scratch[start : start + head, :] = value_ref[e * head : (e + 1) * head, :]


def front_body(
    head,
    experts,
    length,
    shift,
    memory_ref,
    inputs_ref,
    gains_ref,
    biases_ref,
    key_ref,
    value_ref,
    value_router_ref,
    query_ref,
    output_router_ref,
    position_ref,
    content_bias_ref,
    position_bias_ref,
    value_route_ref,
    output_route_ref,
    place_ref,
    coarse_ref,
    fine_ref,
    normed_ref,
    key_cat_ref,
    values_ref,
    gate_ref,
    content_query_ref,
    bias_query_ref,
    count_ref,
    probs_ref,
    attended_ref,
    weight_scratch,
    bias_scratch,
    key_scratch,
    value_scratch,
    query_scratch,
):
    step = pl.program_id(0)
    span = memory_ref.shape[0]
    keys = key_scratch.shape[0]
    mem_steps = (keys - length) // span
    split = LANES * (1 + experts)
    freq = coarse_ref.shape[1] // 2

    @pl.when(step == 0)
    def _():
        weight_scratch[...] = jnp.zeros_like(weight_scratch)
        bias_scratch[...] = jnp.zeros_like(bias_scratch)
        count_ref[...] = jnp.zeros_like(count_ref)
        fill_weights(head, experts, key_ref, value_router_ref, value_ref, weight_scratch)
        weight_scratch[split : split + head, :] = query_ref[...]
        weight_scratch[split + head : split + head + experts, :] = output_router_ref[...]
        bias_scratch[0:1, 0:head] = content_bias_ref[...]
        bias_scratch[1:2, 0:head] = position_bias_ref[...]

    old = step < mem_steps
    rows = jnp.where(old, memory_ref[...], inputs_ref[...]).astype(F32)
    unit, _ = unit_rows(rows)
    normed = (unit * gains_ref[0:1, :] + biases_ref[0:1, :]).astype(BF16)
    normed_ref[...] = normed
    product = dot_last(normed, weight_scratch[0:split, :])
    lane = lane_index(span)
    first = product[:, 0:LANES]
    key_piece = jnp.where(lane < head, first, 0.0).astype(BF16)

    def picks(route):
        row = lax.broadcasted_iota(jnp.int32, (LANES, span), 0) - head
        hit = (route[0:1, :] == row).astype(F32) + (route[1:2, :] == row).astype(F32)
        return hit.T

    chosen = picks(value_route_ref[...])
    gate = jax.nn.sigmoid(first) * chosen
    gate_ref[...] = gate.T[head : head + 8, :]
    total = jnp.zeros((span, LANES), F32)
    for e in range(experts):
        start = LANES * (e + 1)
        total = total + gate[:, head + e : head + e + 1] * product[:, start : start + LANES]
    values = total.astype(BF16)
    values_ref[...] = values
    current_place = lax.broadcasted_iota(jnp.int32, (1, span), 1) + (step - mem_steps) * span
    cosine, sine = angles(
        jnp.where(old, place_ref[...], current_place) + shift, coarse_ref, fine_ref
    )
    cos_low = cosine.astype(BF16)
    sin_low = sine.astype(BF16)
    key_cat_ref[:, 0:LANES] = key_piece
    key_cat_ref[:, LANES : LANES + freq] = cos_low
    key_cat_ref[:, LANES + freq :] = sin_low
    base = pl.multiple_of(step * span, span)
    key_scratch[pl.ds(base, span), 0:LANES] = key_piece
    key_scratch[pl.ds(base, span), LANES : LANES + freq] = cos_low
    key_scratch[pl.ds(base, span), LANES + freq :] = sin_low
    value_scratch[pl.ds(base, span), :] = values

    def variant(place):
        def run():
            last = dot_last(normed, weight_scratch[split:, :])
            query = jnp.where(lane < head, last, 0.0)
            content = (query + bias_scratch[0:1, :]).astype(BF16)
            biased = (query + bias_scratch[1:2, :]).astype(BF16)
            content_query_ref[...] = content
            bias_query_ref[...] = biased
            out_chosen = picks(output_route_ref[...])
            out_gate = jax.nn.sigmoid(last) * out_chosen
            count_ref[0:1, :] += jnp.sum(chosen, axis=0, keepdims=True)
            count_ref[1:2, :] += jnp.sum(out_chosen, axis=0, keepdims=True)
            rest = out_gate - out_gate.astype(BF16).astype(F32)
            extra = out_gate + pltpu.roll(rest, experts, 1)
            relative = dot_plain(biased[:, 0:head], position_ref[...])
            rel_sin = relative[:, 0:freq]
            rel_cos = relative[:, freq:]
            query_scratch[:, 0:LANES] = content
            query_scratch[:, LANES : LANES + freq] = (rel_sin * sine + rel_cos * cosine).astype(
                BF16
            )
            query_scratch[:, LANES + freq :] = (rel_cos * sine - rel_sin * cosine).astype(BF16)
            factor = head ** (-0.5) * math.log2(math.e)
            row = lax.broadcasted_iota(jnp.int32, (ROWS, ROWS), 0)
            col = lax.broadcasted_iota(jnp.int32, (ROWS, ROWS), 1)
            for part in range(span // ROWS):
                piece = slice(part * ROWS, (part + 1) * ROWS)
                seen = keys - length + place * span + (part + 1) * ROWS
                scores = dot_last(query_scratch[piece, :], key_scratch[0:seen, :])
                body = scores[:, 0 : seen - ROWS]
                tail = jnp.where(col <= row, scores[:, seen - ROWS :], -jnp.inf)
                top = factor * jnp.maximum(
                    jnp.max(body, axis=1, keepdims=True), jnp.max(tail, axis=1, keepdims=True)
                )
                body = jnp.exp2(body * factor - top)
                tail = jnp.exp2(tail * factor - top)
                share = 1.0 / (
                    jnp.sum(body, axis=1, keepdims=True) + jnp.sum(tail, axis=1, keepdims=True)
                )
                body = (body * share).astype(BF16)
                tail = (tail * share).astype(BF16)
                probs_ref[piece, 0 : seen - ROWS] = body
                probs_ref[piece, seen - ROWS : seen] = tail
                if seen < keys:
                    probs_ref[piece, seen:] = jnp.zeros((ROWS, keys - seen), BF16)
                result = dot_plain(body, value_scratch[0 : seen - ROWS, :]) + dot_plain(
                    tail, value_scratch[seen - ROWS : seen, :]
                )
                attended_ref[piece, :] = jnp.where(
                    lane[piece, :] < head, result, extra[piece, :]
                ).astype(BF16)

        return run

    for place in range(length // span):
        pl.when(step == mem_steps + place)(variant(place))


def front(
    memory,
    inputs,
    gains,
    biases,
    key_weight,
    value_weight,
    value_router,
    query_weight,
    output_router,
    position_weight,
    content_bias,
    position_bias,
    value_routes,
    output_routes,
    places,
    coarse,
    fine,
):
    mem_count, width = memory.shape
    length = inputs.shape[0]
    head = key_weight.shape[0]
    experts = value_router.shape[0]
    pos_width = coarse.shape[1]
    keys = mem_count + length
    span = 2 * ROWS
    mem_steps = mem_count // span
    old = lambda i: (jnp.minimum(i, mem_steps - 1), 0)
    new = lambda i: (jnp.maximum(i - mem_steps, 0), 0)
    every = lambda i: (i, 0)
    row = lambda size, index: pl.BlockSpec((span, size), index)
    turned = lambda index: (lambda i: index(i)[::-1])
    return pl.pallas_call(
        functools.partial(front_body, head, experts, length, 2 * mem_count),
        out_shape=(
            jax.ShapeDtypeStruct((keys, width), BF16),
            jax.ShapeDtypeStruct((keys, LANES + pos_width), BF16),
            jax.ShapeDtypeStruct((keys, LANES), BF16),
            jax.ShapeDtypeStruct((8, keys), F32),
            jax.ShapeDtypeStruct((length, LANES), BF16),
            jax.ShapeDtypeStruct((length, LANES), BF16),
            jax.ShapeDtypeStruct((8, LANES), F32),
            jax.ShapeDtypeStruct((length, keys), BF16),
            jax.ShapeDtypeStruct((length, LANES), BF16),
        ),
        grid=(keys // span,),
        in_specs=[
            row(width, old),
            row(width, new),
            whole(gains),
            whole(biases),
            whole(key_weight),
            whole(value_weight),
            whole(value_router),
            whole(query_weight),
            whole(output_router),
            whole(position_weight),
            whole(content_bias),
            whole(position_bias),
            pl.BlockSpec((value_routes.shape[0], span), turned(every)),
            pl.BlockSpec((output_routes.shape[0], span), turned(new)),
            pl.BlockSpec((1, span), turned(old)),
            whole(coarse),
            whole(fine),
        ],
        out_specs=(
            row(width, every),
            row(LANES + pos_width, every),
            row(LANES, every),
            pl.BlockSpec((8, span), turned(every)),
            row(LANES, new),
            row(LANES, new),
            fixed((8, LANES)),
            row(keys, new),
            row(LANES, new),
        ),
        scratch_shapes=[
            pltpu.VMEM((LANES * (2 + experts), width), BF16),
            pltpu.VMEM((8, LANES), F32),
            pltpu.VMEM((keys, LANES + pos_width), BF16),
            pltpu.VMEM((keys, LANES), BF16),
            pltpu.VMEM((span, LANES + pos_width), BF16),
        ],
        compiler_params=params(),
        cost_estimate=cost(30 * FLOPS_US, 30e6),
        name="front",
    )(
        memory,
        inputs,
        gains,
        biases,
        key_weight,
        value_weight,
        value_router,
        query_weight,
        output_router,
        position_weight,
        content_bias,
        position_bias,
        value_routes,
        output_routes,
        places,
        coarse,
        fine,
    )


def attend_back_body(head, heads, shift, me_ref, table_ref, *refs):
    grad_refs = refs[0:heads]
    (
        probs_ref,
        key_cat_ref,
        values_ref,
        content_ref,
        bias_ref,
        coarse_ref,
        fine_ref,
        position_ref,
        normed_ref,
        grad_keys_ref,
        grad_query_ref,
        keep_ref,
        send_ref,
        sums_ref,
        position_scratch,
        relative_scratch,
        grad_scratch,
        keys_scratch,
        weight_scratch,
    ) = refs[heads:]
    step = pl.program_id(0)
    keys = key_cat_ref.shape[0]
    length = pl.num_programs(0) * ROWS
    freq = coarse_ref.shape[1] // 2
    scale = head ** (-0.5)

    @pl.when(step == 0)
    def _():
        keys_scratch[...] = jnp.zeros_like(keys_scratch)
        weight_scratch[...] = jnp.zeros_like(weight_scratch)
        sums_ref[...] = jnp.zeros_like(sums_ref)
        position_scratch[...] = jnp.zeros_like(position_scratch)
        position_scratch[0:head, :] = position_ref[...]
        for distance, grad_ref in enumerate(grad_refs):
            grad_scratch[jnp.bitwise_xor(me_ref[0], distance)] = grad_ref[0]

    lane = lane_index(ROWS)
    packed = grad_scratch[step]
    upstream = jnp.where(lane < head, packed, jnp.zeros_like(packed))
    place = lax.broadcasted_iota(jnp.int32, (1, ROWS), 1) + step * ROWS + shift
    cosine, sine = angles(place, coarse_ref, fine_ref)

    def variant(block):
        def run():
            seen = keys - length_static + (block + 1) * ROWS
            weights_low = probs_ref[:, 0:seen]
            weights = weights_low.astype(F32)
            grad_weights = dot_last(upstream, values_ref[0:seen, :])
            inner = jnp.sum(grad_weights * weights, axis=1, keepdims=True)
            grad_scores = (weights * (grad_weights - inner)).astype(BF16)
            keys_scratch[:, 0:seen] += dot_first(content_ref[...], grad_scores) * scale
            grad_query = dot_plain(grad_scores, key_cat_ref[0:seen, :]) * scale
            grad_content = grad_query[:, 0:LANES]
            grad_sin = grad_query[:, LANES : LANES + freq]
            grad_cos = grad_query[:, LANES + freq :]
            relative_scratch[:, 0:freq] = (grad_sin * sine - grad_cos * cosine).astype(BF16)
            relative_scratch[:, freq:] = (grad_sin * cosine + grad_cos * sine).astype(BF16)
            relative = relative_scratch[...]
            grad_bias = dot_last(relative, position_scratch[...])
            weight_scratch[2 * LANES :, :] += dot_first(bias_ref[...], relative)
            sums_ref[0:1, :] += jnp.sum(grad_content, axis=0, keepdims=True)
            sums_ref[1:2, :] += jnp.sum(grad_bias, axis=0, keepdims=True)
            both = jnp.where(lane < head, (grad_content + grad_bias).astype(BF16), packed)
            grad_query_ref[...] = both
            weight_scratch[LANES : 2 * LANES, :] += dot_first(
                both, normed_ref[seen - ROWS : seen, :]
            )

        return run

    length_static = heads * ROWS
    for block in range(length_static // ROWS):
        pl.when(step == block)(variant(block))

    @pl.when(step == pl.num_programs(0) - 1)
    def _():
        grad_keys = keys_scratch[...].astype(BF16)
        grad_keys_ref[...] = grad_keys
        weight_scratch[0:LANES, :] = dot_plain(grad_keys, normed_ref[...])
        half, chunk, _ = keep_ref.shape
        for place in range(half):
            start = pl.multiple_of(table_ref[place] * chunk, 8)
            keep_ref[place] = weight_scratch[pl.ds(start, chunk), :].astype(BF16)
            start = pl.multiple_of(table_ref[half + place] * chunk, 8)
            send_ref[place] = weight_scratch[pl.ds(start, chunk), :].astype(BF16)


def attend_back(
    me,
    table,
    grads,
    probs,
    key_cat,
    values,
    content_query,
    bias_query,
    coarse,
    fine,
    position_weight,
    normed,
):
    length, keys = probs.shape
    head, pos_width = position_weight.shape
    width = normed.shape[1]
    count = table.shape[0]
    half = jax.ShapeDtypeStruct((count // 2, 3 * LANES // count, width), BF16)
    heads = len(grads)
    every = lambda i, *_: (i, 0)
    row = lambda size: pl.BlockSpec((ROWS, size), every)
    return pl.pallas_call(
        functools.partial(attend_back_body, head, heads, 2 * (keys - length)),
        out_shape=(
            jax.ShapeDtypeStruct((LANES, keys), BF16),
            jax.ShapeDtypeStruct((length, LANES), BF16),
            half,
            half,
            jax.ShapeDtypeStruct((8, LANES), F32),
        ),
        grid_spec=pltpu.PrefetchScalarGridSpec(
            num_scalar_prefetch=2,
            grid=(length // ROWS,),
            in_specs=[whole(grad) for grad in grads]
            + [
                row(keys),
                whole(key_cat),
                whole(values),
                row(LANES),
                row(LANES),
                whole(coarse),
                whole(fine),
                whole(position_weight),
                whole(normed),
            ],
            out_specs=(
                fixed((LANES, keys)),
                row(LANES),
                fixed(half.shape),
                fixed(half.shape),
                fixed((8, LANES)),
            ),
            scratch_shapes=[
                pltpu.VMEM((LANES, pos_width), BF16),
                pltpu.VMEM((ROWS, pos_width), BF16),
                pltpu.VMEM((heads, ROWS, LANES), BF16),
                pltpu.VMEM((LANES, keys), F32),
                pltpu.VMEM((3 * LANES, width), F32),
            ],
        ),
        compiler_params=params(),
        cost_estimate=cost(17 * FLOPS_US, 25e6),
        name="attend_back",
    )(
        me,
        table,
        *grads,
        probs,
        key_cat,
        values,
        content_query,
        bias_query,
        coarse,
        fine,
        position_weight,
        normed,
    )


def value_back_body(head, experts, heads, me_ref, table_ref, *refs):
    grad_refs = refs[0:heads]
    (
        probs_ref,
        normed_ref,
        gate_ref,
        weight_ref,
        grad_values_ref,
        logit_ref,
        keep_ref,
        send_ref,
        grad_scratch,
        packed_scratch,
        acc,
    ) = refs[heads:]
    step = pl.program_id(0)

    @pl.when(step == 0)
    def _():
        lane = lane_index(ROWS)
        for distance, grad_ref in enumerate(grad_refs):
            start = pl.multiple_of(jnp.bitwise_xor(me_ref[0], distance) * ROWS, ROWS)
            piece = grad_ref[0]
            grad_scratch[pl.ds(start, ROWS), :] = jnp.where(
                lane < head, piece, jnp.zeros_like(piece)
            )
        packed_scratch[...] = jnp.zeros_like(packed_scratch)
        acc[...] = jnp.zeros_like(acc)

    grad_values = dot_first(grad_scratch[...], probs_ref[...])
    grad_values_ref[...] = grad_values
    expert_values = dot_last(weight_ref[...], normed_ref[...])
    logits = []
    for e in range(experts):
        piece = slice(e * head, (e + 1) * head)
        gate = gate_ref[e : e + 1, :]
        packed_scratch[piece, :] = (gate * grad_values[0:head, :]).astype(BF16)
        inner = jnp.sum(expert_values[piece, :] * grad_values[0:head, :], axis=0, keepdims=True)
        logits.append(inner * gate * (1.0 - gate))
    logits.append(jnp.zeros((8 - experts, logits[0].shape[1]), F32))
    logit = jnp.concatenate(logits, axis=0)
    logit_ref[...] = logit
    packed_scratch[experts * head : experts * head + 8, :] = logit.astype(BF16)
    acc[...] += dot_plain(packed_scratch[...], normed_ref[...])

    @pl.when(step == pl.num_programs(0) - 1)
    def _():
        half, chunk, _ = keep_ref.shape
        for place in range(half):
            start = pl.multiple_of(table_ref[place] * chunk, 8)
            keep_ref[place] = acc[pl.ds(start, chunk), :].astype(BF16)
            start = pl.multiple_of(table_ref[half + place] * chunk, 8)
            send_ref[place] = acc[pl.ds(start, chunk), :].astype(BF16)


def value_back(me, table, grads, probs, normed, gates, weight, head, experts):
    heads = len(grads)
    length, keys = probs.shape
    width = normed.shape[1]
    count = table.shape[0]
    span = 2 * ROWS
    rows = experts * head + 8
    rows = rows + -rows % (8 * count)
    half = jax.ShapeDtypeStruct((count // 2, rows // count, width), BF16)
    return pl.pallas_call(
        functools.partial(value_back_body, head, experts, heads),
        out_shape=(
            jax.ShapeDtypeStruct((LANES, keys), F32),
            jax.ShapeDtypeStruct((8, keys), F32),
            half,
            half,
        ),
        grid_spec=pltpu.PrefetchScalarGridSpec(
            num_scalar_prefetch=2,
            grid=(keys // span,),
            in_specs=[whole(grad) for grad in grads]
            + [
                pl.BlockSpec((length, span), lambda i, *_: (0, i)),
                pl.BlockSpec((span, width), lambda i, *_: (i, 0)),
                pl.BlockSpec((8, span), lambda i, *_: (0, i)),
                whole(weight),
            ],
            out_specs=(
                pl.BlockSpec((LANES, span), lambda i, *_: (0, i)),
                pl.BlockSpec((8, span), lambda i, *_: (0, i)),
                fixed(half.shape),
                fixed(half.shape),
            ),
            scratch_shapes=[
                pltpu.VMEM((length, LANES), BF16),
                pltpu.VMEM((rows, span), BF16),
                pltpu.VMEM((rows, width), F32),
            ],
        ),
        compiler_params=params(),
        cost_estimate=cost(8 * FLOPS_US, 10e6),
        name="value_back",
    )(me, table, *grads, probs, normed, gates, weight)


def spread_weights(head, experts, weight_refs, scratch):
    scratch[...] = jnp.zeros_like(scratch)
    for j, weight_ref in enumerate(weight_refs):
        for e in range(experts):
            start = LANES * (experts * j + e)
            scratch[start : start + head, :] = weight_ref[e * head : (e + 1) * head, :]


def gate_spread(head, experts):
    shape = (LANES, experts * LANES)
    row = lax.broadcasted_iota(jnp.int32, shape, 0) - head
    block = lax.broadcasted_iota(jnp.int32, shape, 1) // LANES
    return ((row == block) | (row == block + experts)).astype(BF16)


def forward_body(head, experts, heads, place_ref, down_table_ref, up_table_ref, *refs):
    pair = 2
    attended_refs = [refs[part * heads : (part + 1) * heads] for part in range(pair)]
    rest = refs[pair * heads :]
    weight_refs = rest[0:heads]
    rest = rest[heads:]
    inputs_refs = rest[0:pair]
    cotangent_refs = rest[pair : 2 * pair]
    (
        up_ref,
        down_ref,
        gains_ref,
        biases_ref,
        resid_ref,
        grad_normed_ref,
        share_ref,
        down_keep_ref,
        down_send_ref,
        up_keep_ref,
        up_send_ref,
        weight_scratch,
        mixed_scratch,
        active_scratch,
        normed_scratch,
        upper_scratch,
        cotangent_scratch,
        down_acc,
        up_acc,
    ) = rest[2 * pair :]
    step = pl.program_id(0)
    final = pl.num_programs(0) - 1

    @pl.when(step == 0)
    def _():
        spread_weights(head, experts, weight_refs, weight_scratch)

    lane = lane_index(ROWS)
    spread = gate_spread(head, experts)
    for part in range(pair):
        piece = slice(part * ROWS, (part + 1) * ROWS)
        for j, attended_ref in enumerate(attended_refs[part]):
            packed = attended_ref[...]
            gate = dot_plain(packed, spread)
            attended = jnp.where(lane < head, packed.astype(F32), 0.0)
            for e in range(experts):
                start = LANES * (experts * j + e)
                mixed_scratch[piece, start : start + LANES] = (
                    attended * gate[:, e * LANES : (e + 1) * LANES]
                ).astype(BF16)
    mixed_out = dot_plain(mixed_scratch[...], weight_scratch[...])
    for part in range(pair):
        piece = slice(part * ROWS, (part + 1) * ROWS)
        cotangent = cotangent_refs[part][...]
        cotangent_scratch[piece, :] = cotangent
        resid = inputs_refs[part][...].astype(F32) + mixed_out[piece, :]
        if part == 0:

            @pl.when(step == final)
            def _():
                resid_ref[...] = resid

        unit, _ = unit_rows(resid)
        normed = (unit * gains_ref[1:2, :] + biases_ref[1:2, :]).astype(BF16)
        normed_scratch[piece, :] = normed
        upper = dot_plain(normed, up_ref[...])
        active, slope = gelu_parts(upper)
        active = active.astype(BF16)
        active_scratch[piece, :] = active
        grad_upper = (dot_last(cotangent, down_ref[...]) * slope).astype(BF16)
        upper_scratch[piece, :] = grad_upper
        grad_normed_ref[part] = dot_last(grad_upper, up_ref[...]).astype(BF16)
        share_ref[part] = dot_plain(active, down_ref[...]).astype(BF16)
    down_grad = dot_first(active_scratch[...], cotangent_scratch[...])
    up_grad = dot_first(normed_scratch[...], upper_scratch[...])

    @pl.when(step == 0)
    def _():
        down_acc[...] = down_grad
        up_acc[...] = up_grad

    @pl.when(step > 0)
    def _():
        down_acc[...] += down_grad
        up_acc[...] += up_grad

    @pl.when(step == final)
    def _():
        for table_ref, acc, keep_ref, send_ref in (
            (down_table_ref, down_acc, down_keep_ref, down_send_ref),
            (up_table_ref, up_acc, up_keep_ref, up_send_ref),
        ):
            half, chunk, _ = keep_ref.shape
            for place in range(half):
                start = pl.multiple_of(table_ref[place] * chunk, chunk)
                keep_ref[place] = acc[pl.ds(start, chunk), :].astype(BF16)
                start = pl.multiple_of(table_ref[half + place] * chunk, chunk)
                send_ref[place] = acc[pl.ds(start, chunk), :].astype(BF16)


def forward_ffn(
    places,
    down_table,
    up_table,
    attended,
    weights,
    inputs,
    cotangent,
    up,
    down,
    gains,
    biases,
    experts,
):
    heads = len(attended)
    length, width = inputs.shape
    head = weights[0].shape[0] // experts
    hidden = up.shape[1]
    blocks = length // ROWS
    count = down_table.shape[0]
    chunk = hidden // count
    steps = blocks // 2
    place = lambda i, part: (steps - 1 - i) * 2 + part
    row = lambda size, part: pl.BlockSpec(
        (ROWS, size), lambda i, place_ref, *_: (place_ref[place(i, part)], 0)
    )
    relative = pl.BlockSpec((2, ROWS, width), lambda i, *_: (steps - 1 - i, 0, 0))
    half = lambda rows: jax.ShapeDtypeStruct((count // 2, rows, width), BF16)
    return pl.pallas_call(
        functools.partial(forward_body, head, experts, heads),
        out_shape=(
            jax.ShapeDtypeStruct((ROWS, width), F32),
            jax.ShapeDtypeStruct((blocks, ROWS, width), BF16),
            jax.ShapeDtypeStruct((blocks, ROWS, width), BF16),
            half(chunk),
            half(chunk),
            half(width // count),
            half(width // count),
        ),
        grid_spec=pltpu.PrefetchScalarGridSpec(
            num_scalar_prefetch=3,
            grid=(steps,),
            in_specs=[row(LANES, 0) for _ in attended]
            + [row(LANES, 1) for _ in attended]
            + [whole(weight) for weight in weights]
            + [row(width, 0), row(width, 1), row(width, 0), row(width, 1)]
            + [whole(up), whole(down), whole(gains), whole(biases)],
            out_specs=(
                fixed((ROWS, width)),
                relative,
                relative,
                fixed((count // 2, chunk, width)),
                fixed((count // 2, chunk, width)),
                fixed((count // 2, width // count, hidden)),
                fixed((count // 2, width // count, hidden)),
            ),
            scratch_shapes=[
                pltpu.VMEM((heads * experts * LANES, width), BF16),
                pltpu.VMEM((2 * ROWS, heads * experts * LANES), BF16),
                pltpu.VMEM((2 * ROWS, hidden), BF16),
                pltpu.VMEM((2 * ROWS, width), BF16),
                pltpu.VMEM((2 * ROWS, hidden), BF16),
                pltpu.VMEM((2 * ROWS, width), BF16),
                pltpu.VMEM((hidden, width), F32),
                pltpu.VMEM((width, hidden), F32),
            ],
        ),
        compiler_params=params(),
        cost_estimate=cost(28 * FLOPS_US, 30e6),
        name="forward_ffn",
    )(
        places,
        down_table,
        up_table,
        *attended,
        *attended,
        *weights,
        inputs,
        inputs,
        cotangent,
        cotangent,
        up,
        down,
        gains,
        biases,
    )


def second_norm_back_body(head, experts, heads, me_ref, *refs):
    attended_refs = refs[0:heads]
    weight_refs = refs[heads : 2 * heads]
    (
        left_ref,
        right_ref,
        resid_ref,
        cotangent_ref,
        gains_ref,
        grad_resid_ref,
        low_ref,
        packed_ref,
        sums_ref,
        weight_scratch,
        product_scratch,
    ) = refs[2 * heads :]
    spread_weights(head, experts, weight_refs, weight_scratch)
    unit, inverse = unit_rows(resid_ref[...])
    grad = left_ref[0].astype(F32) + right_ref[0].astype(F32)
    sums_ref[...] = jnp.zeros_like(sums_ref)
    sums_ref[2:3, :] = jnp.sum(grad * unit, axis=0, keepdims=True)
    sums_ref[3:4, :] = jnp.sum(grad, axis=0, keepdims=True)
    grad_resid = cotangent_ref[...].astype(F32) + norm_backward(
        grad, unit, inverse, gains_ref[1:2, :]
    )
    grad_resid_ref[...] = grad_resid
    low = grad_resid.astype(BF16)
    low_ref[0] = low
    grad_mixed = dot_last(low, weight_scratch[...])
    lane = lane_index(ROWS)
    spread = gate_spread(head, experts)
    collect = spread.T[:, 0:LANES]
    for j, attended_ref in enumerate(attended_refs):
        packed = attended_ref[...]
        gate = dot_plain(packed, spread)
        attended = jnp.where(lane < head, packed.astype(F32), 0.0)
        total = jnp.zeros((ROWS, LANES), F32)
        for e in range(experts):
            start = LANES * (experts * j + e)
            block = slice(e * LANES, (e + 1) * LANES)
            piece = grad_mixed[:, start : start + LANES]
            total = total + gate[:, block] * piece
            product_scratch[:, block] = piece * attended
        product = product_scratch[...]
        lead = product.astype(BF16)
        rest = (product - lead.astype(F32)).astype(BF16)
        logits = dot_plain(lead, collect) + dot_plain(rest, collect)
        own = packed.astype(F32)
        own = own + pltpu.roll(own, LANES - experts, 1)
        logits = logits * own * (1.0 - own)
        total = jnp.where((lane >= head) & (lane < head + experts), logits, total)
        packed_ref[j] = total.astype(BF16)


def second_norm_back(me, attended, weights, left, right, resid, cotangent, gains, experts):
    heads = len(attended)
    width = resid.shape[1]
    head = weights[0].shape[0] // experts
    own = lambda i, me_ref: (me_ref[0], 0)
    row = lambda size: pl.BlockSpec((ROWS, size), own)
    return pl.pallas_call(
        functools.partial(second_norm_back_body, head, experts, heads),
        out_shape=(
            jax.ShapeDtypeStruct((ROWS, width), F32),
            jax.ShapeDtypeStruct((1, ROWS, width), BF16),
            jax.ShapeDtypeStruct((heads, ROWS, LANES), BF16),
            jax.ShapeDtypeStruct((8, width), F32),
        ),
        grid_spec=pltpu.PrefetchScalarGridSpec(
            num_scalar_prefetch=1,
            grid=(1,),
            in_specs=[row(LANES) for _ in attended]
            + [whole(weight) for weight in weights]
            + [whole(left), whole(right), whole(resid), row(width), whole(gains)],
            out_specs=(
                fixed((ROWS, width)),
                fixed((1, ROWS, width)),
                fixed((heads, ROWS, LANES)),
                fixed((8, width)),
            ),
            scratch_shapes=[
                pltpu.VMEM((heads * experts * LANES, width), BF16),
                pltpu.VMEM((ROWS, experts * LANES), F32),
            ],
        ),
        compiler_params=params(),
        cost_estimate=cost(7 * FLOPS_US, 12e6),
        name="second_norm_back",
    )(me, *attended, *weights, left, right, resid, cotangent, gains)


def output_grad_body(
    head, experts, place_ref, table_ref, attended_ref, *refs
):
    blocks = place_ref.shape[0]
    grad_refs = refs[0:blocks]
    keep_ref, send_ref, mixed, rows, acc = refs[blocks:]
    half, chunk, _ = keep_ref.shape
    for place, grad_ref in enumerate(grad_refs):
        start = pl.multiple_of(place_ref[place] * ROWS, ROWS)
        packed = attended_ref[pl.ds(start, ROWS), :].astype(F32).T
        piece = slice(place * ROWS, (place + 1) * ROWS)
        for e in range(experts):
            gate = packed[head + e : head + e + 1, :] + packed[
                head + experts + e : head + experts + e + 1, :
            ]
            mixed[e * head : (e + 1) * head, piece] = (packed[0:head, :] * gate).astype(BF16)
        rows[piece, :] = grad_ref[0]
    mixed[experts * head :, :] = jnp.zeros_like(mixed[experts * head :, :])
    acc[...] = dot_plain(mixed[...], rows[...])
    for place in range(half):
        start = pl.multiple_of(table_ref[place] * chunk, 8)
        keep_ref[place] = acc[pl.ds(start, chunk), :].astype(BF16)
        start = pl.multiple_of(table_ref[half + place] * chunk, 8)
        send_ref[place] = acc[pl.ds(start, chunk), :].astype(BF16)


def output_grad(places, table, attended, grads, head, experts):
    count = table.shape[0]
    length = attended.shape[0]
    width = grads[0].shape[2]
    rows = experts * head
    rows = rows + -rows % (8 * count)
    chunk = rows // count
    half = jax.ShapeDtypeStruct((count // 2, chunk, width), BF16)
    return pl.pallas_call(
        functools.partial(output_grad_body, head, experts),
        out_shape=(half, half),
        grid_spec=pltpu.PrefetchScalarGridSpec(
            num_scalar_prefetch=2,
            grid=(1,),
            in_specs=[whole(attended)] + [whole(grad) for grad in grads],
            out_specs=(fixed(half.shape), fixed(half.shape)),
            scratch_shapes=[
                pltpu.VMEM((rows, length), BF16),
                pltpu.VMEM((length, width), BF16),
                pltpu.VMEM((rows, width), F32),
            ],
        ),
        compiler_params=params(),
        cost_estimate=cost(5 * FLOPS_US, 4e6),
        name="output_grad",
    )(places, table, attended, *grads)


def project_back_body(head, experts, place_ref, *refs):
    pair = 2
    groups = []
    for index in range(7):
        groups.append(refs[index * pair : (index + 1) * pair])
    grad_keys_refs, grad_values_refs, gate_refs, logit_refs, query_refs, memory_refs, inputs_refs = (
        groups
    )
    (
        key_ref,
        value_ref,
        value_router_ref,
        query_ref,
        output_router_ref,
        bias_sums_ref,
        counts_ref,
        grad_current_ref,
        sums_ref,
        extra_ref,
        weight_scratch,
        packed_scratch,
    ) = refs[7 * pair :]
    step = pl.program_id(0)
    split = LANES * (1 + experts)
    cur_steps = place_ref.shape[0] // pair
    current = step < cur_steps

    @pl.when(step == 0)
    def _():
        sums_ref[...] = jnp.zeros_like(sums_ref)
        extra_ref[...] = jnp.zeros_like(extra_ref)
        extra_ref[0:2, 0:LANES] = bias_sums_ref[0:2, :]
        extra_ref[2:4, 0:LANES] = counts_ref[0:2, :]
        weight_scratch[...] = jnp.zeros_like(weight_scratch)
        packed_scratch[...] = jnp.zeros_like(packed_scratch)
        fill_weights(head, experts, key_ref, value_router_ref, value_ref, weight_scratch)
        weight_scratch[split : split + head, :] = query_ref[...]
        weight_scratch[split + head : split + head + experts, :] = output_router_ref[...]

    for part in range(pair):
        piece = slice(part * ROWS, (part + 1) * ROWS)
        grad_values = grad_values_refs[part][0:head, :]
        packed_scratch[0:head, piece] = grad_keys_refs[part][0:head, :]
        packed_scratch[head : head + 8, piece] = logit_refs[part][...].astype(BF16)
        for e in range(experts):
            start = LANES * (e + 1)
            gate = gate_refs[part][e : e + 1, :]
            packed_scratch[start : start + head, piece] = (gate * grad_values).astype(BF16)
    grads = dot_first(packed_scratch[...], weight_scratch[0:split, :])
    for part in range(pair):
        piece = slice(part * ROWS, (part + 1) * ROWS)
        grad = grads[piece, :]
        more = dot_plain(query_refs[part][...], weight_scratch[split:, :])
        grad = grad + jnp.where(current, more, 0.0)
        rows = jnp.where(current, inputs_refs[part][...], memory_refs[part][...]).astype(F32)
        unit, _ = unit_rows(rows)
        sums_ref[0:1, :] += jnp.sum(grad * unit, axis=0, keepdims=True)
        sums_ref[1:2, :] += jnp.sum(grad, axis=0, keepdims=True)

        @pl.when(current)
        def _():
            grad_current_ref[part] = grad.astype(BF16)


def project_back(
    places,
    grad_keys,
    grad_values,
    gates,
    logits,
    grad_query,
    memory,
    inputs,
    key_weight,
    value_weight,
    value_router,
    query_weight,
    output_router,
    bias_sums,
    counts,
):
    keys = grad_keys.shape[1]
    length, width = inputs.shape
    head = key_weight.shape[0]
    experts = value_router.shape[0]
    mem_blocks = (keys - length) // ROWS
    cur_blocks = length // ROWS
    cur_steps = cur_blocks // 2
    split = LANES * (1 + experts)
    fresh = lambda i, part, place_ref: place_ref[2 * jnp.minimum(i, cur_steps - 1) + part]
    past = lambda i, part, place_ref: 2 * jnp.maximum(i - cur_steps, 0) + part
    every = lambda i, part, place_ref: jnp.where(
        i < cur_steps, fresh(i, part, place_ref) + mem_blocks, past(i, part, place_ref)
    )

    def rows(size, index):
        return [
            pl.BlockSpec((ROWS, size), lambda i, place_ref, p=part: (index(i, p, place_ref), 0))
            for part in range(2)
        ]

    def columns(size):
        return [
            pl.BlockSpec((size, ROWS), lambda i, place_ref, p=part: (0, every(i, p, place_ref)))
            for part in range(2)
        ]

    twice = lambda *arrays: [array for array in arrays for _ in range(2)]
    weights = [key_weight, value_weight, value_router, query_weight, output_router]
    return pl.pallas_call(
        functools.partial(project_back_body, head, experts),
        out_shape=(
            jax.ShapeDtypeStruct((cur_blocks, ROWS, width), BF16),
            jax.ShapeDtypeStruct((8, width), F32),
            jax.ShapeDtypeStruct((8, width), F32),
        ),
        grid_spec=pltpu.PrefetchScalarGridSpec(
            num_scalar_prefetch=1,
            grid=(keys // (2 * ROWS),),
            in_specs=columns(LANES)
            + columns(LANES)
            + columns(8)
            + columns(8)
            + rows(LANES, fresh)
            + rows(width, past)
            + rows(width, fresh)
            + [whole(weight) for weight in weights]
            + [whole(bias_sums), whole(counts)],
            out_specs=(
                pl.BlockSpec(
                    (2, ROWS, width), lambda i, *_: (jnp.minimum(i, cur_steps - 1), 0, 0)
                ),
                fixed((8, width)),
                fixed((8, width)),
            ),
            scratch_shapes=[
                pltpu.VMEM((split + LANES, width), BF16),
                pltpu.VMEM((split, 2 * ROWS), BF16),
            ],
        ),
        compiler_params=params(),
        cost_estimate=cost(12 * FLOPS_US, 15e6),
        name="project_back",
    )(
        places,
        *twice(grad_keys, grad_values, gates, logits, grad_query, memory, inputs),
        *weights,
        bias_sums,
        counts,
    )


def first_norm_back(me, left, right, inputs, grad_resid, gains):
    width = inputs.shape[1]

    def body(me_ref, left_ref, right_ref, inputs_ref, resid_ref, gains_ref, out_ref):
        unit, inverse = unit_rows(inputs_ref[...].astype(F32))
        grad = left_ref[0].astype(F32) + right_ref[0].astype(F32)
        out_ref[0] = (
            resid_ref[...] + norm_backward(grad, unit, inverse, gains_ref[0:1, :])
        ).astype(BF16)

    return pl.pallas_call(
        body,
        out_shape=jax.ShapeDtypeStruct((1, ROWS, width), BF16),
        grid_spec=pltpu.PrefetchScalarGridSpec(
            num_scalar_prefetch=1,
            grid=(1,),
            in_specs=[
                whole(left),
                whole(right),
                pl.BlockSpec((ROWS, width), lambda i, me_ref: (me_ref[0], 0)),
                whole(grad_resid),
                whole(gains),
            ],
            out_specs=fixed((1, ROWS, width)),
        ),
        compiler_params=params(),
        cost_estimate=cost(3 * FLOPS_US, 4e6),
        name="first_norm_back",
    )(me, left, right, inputs, grad_resid, gains)


def place_rows(places, pieces):
    _, rows, width = pieces[0].shape
    count = len(pieces)

    def body(place_ref, *refs):
        out_ref = refs[count]
        for place in range(count):
            start = pl.multiple_of(place_ref[place] * rows, rows)
            out_ref[pl.ds(start, rows), :] = refs[place][0]

    return pl.pallas_call(
        body,
        out_shape=jax.ShapeDtypeStruct((count * rows, width), pieces[0].dtype),
        grid_spec=pltpu.PrefetchScalarGridSpec(
            num_scalar_prefetch=1,
            grid=(1,),
            in_specs=[whole(piece) for piece in pieces],
            out_specs=fixed((count * rows, width)),
        ),
        compiler_params=params(),
        cost_estimate=cost(3 * FLOPS_US, 4e6),
        name="place_rows",
    )(places, *pieces)


def unpack_rows(table, own, got, rows_out, more=0):
    half, rows, width = own.shape
    total = 2 * half * rows
    part = width // 2

    def body(table_ref, own_ref, got_ref, out_ref, *rest):
        scratch = rest[1:] if more else rest
        rows_ref = scratch[0] if scratch else out_ref
        for place in range(half):
            start = pl.multiple_of(table_ref[place] * rows, 8)
            rows_ref[pl.ds(start, rows), :] = own_ref[place].astype(F32)
            start = pl.multiple_of(table_ref[half + place] * rows, 8)
            rows_ref[pl.ds(start, rows), :] = got_ref[place].astype(F32)
        if scratch:
            out_ref[...] = rows_ref[0:rows_out, :]
        if more:
            rest[0][...] = rows_ref[rows_out : rows_out + more, :]

    shapes = [jax.ShapeDtypeStruct((rows_out, width), F32)]
    if more:
        shapes.append(jax.ShapeDtypeStruct((more, width), F32))
    chunks = pl.BlockSpec((half, rows, part), lambda i, _: (0, 0, i))
    return pl.pallas_call(
        body,
        out_shape=tuple(shapes),
        grid_spec=pltpu.PrefetchScalarGridSpec(
            num_scalar_prefetch=1,
            grid=(2,),
            in_specs=[chunks, chunks],
            out_specs=tuple(
                pl.BlockSpec((shape.shape[0], part), lambda i, _: (0, i)) for shape in shapes
            ),
            scratch_shapes=[] if total == rows_out else [pltpu.VMEM((total, part), F32)],
        ),
        compiler_params=params(),
        cost_estimate=cost(5 * FLOPS_US, 6e6),
        name="unpack_rows",
    )(table, own, got)


def unpack_heads(table, own, got, head, experts):
    half, chunk, width = own.shape

    def body(
        table_ref,
        own_ref,
        got_ref,
        key_ref,
        query_ref,
        output_router_ref,
        position_ref,
        rows,
    ):
        for place in range(half):
            start = pl.multiple_of(table_ref[place] * chunk, 8)
            rows[pl.ds(start, chunk), :] = own_ref[place].astype(F32)
            start = pl.multiple_of(table_ref[half + place] * chunk, 8)
            rows[pl.ds(start, chunk), :] = got_ref[place].astype(F32)
        key_ref[...] = rows[0:head, :]
        query_ref[...] = rows[LANES : LANES + head, :]
        output_router_ref[...] = rows[LANES + head : LANES + head + experts, :]
        position_ref[...] = rows[2 * LANES : 2 * LANES + head, :]

    one = jax.ShapeDtypeStruct((head, width), F32)
    few = jax.ShapeDtypeStruct((experts, width), F32)
    return pl.pallas_call(
        body,
        out_shape=(one, one, few, one),
        grid_spec=pltpu.PrefetchScalarGridSpec(
            num_scalar_prefetch=1,
            grid=(1,),
            in_specs=[whole(own), whole(got)],
            out_specs=tuple(fixed(kind.shape) for kind in (one, one, few, one)),
            scratch_shapes=[pltpu.VMEM((2 * half * chunk, width), F32)],
        ),
        compiler_params=params(),
        cost_estimate=cost(3 * FLOPS_US, 3e6),
        name="unpack_heads",
    )(table, own, got)


def unpack_small(me, norms, extra, head, share):
    def body(
        me_ref,
        norms_ref,
        extra_ref,
        gains_ref,
        biases_ref,
        content_ref,
        position_ref,
        counts_ref,
    ):
        start = pl.multiple_of(me_ref[0] * share, LANES)
        gains_ref[0:1, :] = norms_ref[0:1, pl.ds(start, share)]
        gains_ref[1:2, :] = norms_ref[2:3, pl.ds(start, share)]
        biases_ref[0:1, :] = norms_ref[1:2, pl.ds(start, share)]
        biases_ref[1:2, :] = norms_ref[3:4, pl.ds(start, share)]
        content_ref[...] = extra_ref[0:1, 0:head]
        position_ref[...] = extra_ref[1:2, 0:head]
        counts_ref[...] = extra_ref[2:4, 0:LANES].astype(jnp.int32)

    shapes = (
        ((2, share), F32),
        ((2, share), F32),
        ((1, head), F32),
        ((1, head), F32),
        ((2, LANES), jnp.int32),
    )
    return pl.pallas_call(
        body,
        out_shape=tuple(jax.ShapeDtypeStruct(shape, kind) for shape, kind in shapes),
        grid_spec=pltpu.PrefetchScalarGridSpec(
            num_scalar_prefetch=1,
            grid=(1,),
            in_specs=[whole(norms), whole(extra)],
            out_specs=tuple(fixed(shape) for shape, _ in shapes),
        ),
        cost_estimate=cost(2 * FLOPS_US, 1e6),
        name="unpack_small",
    )(me, norms, extra)


def on_device(
    inputs,
    memory,
    memory_positions,
    value_routes,
    output_routes,
    norm_gains,
    norm_biases,
    query_weight,
    key_weight,
    value_weight,
    value_router,
    output_router,
    output_weight,
    position_weight,
    content_bias,
    position_bias,
    up_weight,
    down_weight,
    cotangent,
):
    length, width = inputs.shape[1:]
    mem_count = memory.shape[1]
    keys = mem_count + length
    head = query_weight.shape[1]
    experts = value_router.shape[1]
    pos_width = position_weight.shape[0]
    picks = value_routes.shape[3]
    t_index = lax.axis_index("tensor")
    me = t_index.reshape(1).astype(jnp.int32)
    t_bits = axis_bits("tensor")
    t_order = relative_order(t_bits)
    t_table = chunk_table(t_bits, "tensor")
    t_count = lax.axis_size("tensor")
    core_bit, chip_bit = t_bits
    all_bits = axis_bits("dp")
    first_bits = all_bits[:SPLITS]
    second_bits = [first_bits[1], first_bits[0]] + first_bits[2:]
    first_table = chunk_table(first_bits, "dp")
    second_table = chunk_table(second_bits, "dp")

    def bits_of(name):
        return second_bits if name in SECOND else first_bits

    def table_of(name):
        return second_table if name in SECOND else first_table

    tokens = inputs.reshape(length, width)
    upstream = cotangent.reshape(length, width)
    past = memory.reshape(mem_count, width)
    key_t = key_weight.T
    value_t = value_weight.T
    value_router_t = value_router.T
    query_t = query_weight.T
    output_router_t = output_router.T
    position_t = position_weight.T

    far_weight = swap(output_weight, "tensor", chip_bit)
    coarse = trig_tables(-2.0 * mem_count, (2 * mem_count + length) // FINE, float(FINE), pos_width)
    fine = trig_tables(0.0, FINE, 1.0, pos_width)
    (
        normed,
        key_cat,
        values,
        gates,
        content_query,
        bias_query,
        counts,
        probs,
        attended_own,
    ) = front(
        past,
        tokens,
        norm_gains,
        norm_biases,
        key_t,
        value_t,
        value_router_t,
        query_t,
        output_router_t,
        position_t,
        content_bias.reshape(1, head),
        position_bias.reshape(1, head),
        value_routes.reshape(keys, picks).T,
        output_routes.reshape(length, picks).T,
        memory_positions,
        coarse,
        fine,
    )

    totals = {}
    v = {}
    token = [attended_own]

    def tie(value):
        return after(value, *token)

    def core_sum(held, got):
        half = held.shape[0] // 2
        return add_pieces(held[:1], got[:1]), add_pieces(held[1:half], got[1:])

    def for_core(held):
        return swap(held[held.shape[0] // 2 :], "tensor", core_bit)

    far_attended = swap(attended_own, "tensor", chip_bit)
    near_attended = swap(attended_own, "tensor", core_bit)
    far_weight = after(far_weight, attended_own)
    near_weight = swap(after(output_weight, attended_own), "tensor", core_bit)
    across_weight = swap(far_weight, "tensor", core_bit)
    across_attended = swap(far_attended, "tensor", core_bit)
    attended = [attended_own, far_attended, near_attended, across_attended]
    weights = [output_weight, far_weight, near_weight, across_weight]

    def feed_forward():
        (
            v["resid"],
            v["grad_normed"],
            v["share"],
            down_keep,
            down_send,
            up_keep,
            up_send,
        ) = forward_ffn(
            tie(t_table),
            table_of("down"),
            table_of("up"),
            attended,
            weights,
            tokens,
            upstream,
            up_weight,
            down_weight,
            norm_gains,
            norm_biases,
            experts,
        )
        v["grad_normed_got"] = for_core(v["grad_normed"])
        totals["F"] = DpSum(
            [(down_keep, down_send, bits_of("down")), (up_keep, up_send, bits_of("up"))]
        )
        return down_keep

    def grad_normed_add():
        v["left"], far = core_sum(v["grad_normed"], tie(v["grad_normed_got"]))
        v["right"] = swap(far, "tensor", chip_bit)
        return far

    def share_core():
        v["share"] = tie(v["share"])
        v["share_got"] = for_core(v["share"])
        return None

    def share_add():
        v["share_left"], far = core_sum(v["share"], tie(v["share_got"]))
        v["share_right"] = swap(far, "tensor", chip_bit)
        return far

    def second_norm():
        v["grad_resid"], low_own, packed, v["sums_two"] = second_norm_back(
            tie(me),
            attended,
            weights,
            v["left"],
            v["right"],
            v["resid"],
            upstream,
            norm_gains,
            experts,
        )
        arrived = [None] * t_count
        for place, distance in enumerate(t_order):
            piece = packed[place : place + 1]
            arrived[distance] = piece if distance == 0 else swap(piece, "tensor", distance)
        v["arrived"] = arrived
        v["low"] = [
            low_own,
            swap(low_own, "tensor", chip_bit),
            swap(low_own, "tensor", core_bit),
        ]
        return low_own

    def low_across():
        far = tie(v["low"][1])
        v["low"][1] = far
        v["low"].append(swap(far, "tensor", core_bit))
        return far

    def start_pair():
        if "value_part" in v and "out_part" in v:
            totals["W"] = DpSum([v["value_part"], v["out_part"]])

    def value_grads():
        v["grad_values"], v["logits"], keep, send = value_back(
            tie(me),
            table_of("value"),
            v["arrived"],
            probs,
            normed,
            gates,
            value_t,
            head,
            experts,
        )
        v["value_part"] = (keep, send, bits_of("value"))
        start_pair()
        return v["grad_values"]

    def attention():
        v["grad_keys"], v["grad_query"], keep, send, v["bias_sums"] = attend_back(
            tie(me),
            table_of("late"),
            v["arrived"],
            probs,
            key_cat,
            values,
            content_query,
            bias_query,
            coarse,
            fine,
            position_t,
            normed,
        )
        totals["L"] = DpSum([(keep, send, bits_of("late"))])
        return v["bias_sums"]

    def output_weight_grad():
        keep, send = output_grad(
            tie(t_table), table_of("out"), attended_own, v["low"], head, experts
        )
        v["out_part"] = (keep, send, bits_of("out"))
        start_pair()
        return send

    def projections():
        v["grad_current"], v["sums_one"], v["extra"] = project_back(
            tie(t_table),
            v["grad_keys"],
            v["grad_values"],
            gates,
            v["logits"],
            v["grad_query"],
            past,
            tokens,
            key_t,
            value_t,
            value_router_t,
            query_t,
            output_router_t,
            v["bias_sums"],
            counts,
        )
        v["grad_current_got"] = for_core(v["grad_current"])
        return v["extra"]

    def grad_current_add():
        v["left"], far = core_sum(v["grad_current"], tie(v["grad_current_got"]))
        v["right"] = swap(far, "tensor", chip_bit)
        return far

    def first_norm():
        own = first_norm_back(
            tie(me), v["left"], v["right"], tokens, v["grad_resid"], norm_gains
        )
        v["grad_inputs"] = [
            own,
            swap(own, "tensor", chip_bit),
            swap(own, "tensor", core_bit),
        ]
        return own

    def rows_across(name):
        far = tie(v[name][1])
        v[name][1] = far
        v[name].append(swap(far, "tensor", core_bit))
        return far

    def rows_placed(name):
        v[name] = place_rows(tie(t_table), v[name])
        return v[name]

    def output_rows():
        own = (
            v["resid"][None]
            + v["share_left"].astype(F32)
            + tie(v["share_right"]).astype(F32)
        ).astype(BF16)
        v["output"] = [
            own,
            swap(own, "tensor", chip_bit),
            swap(own, "tensor", core_bit),
        ]
        return own

    def small_sum(stage):
        if stage == 0:
            total = tie(v["sums_one"]) + v["sums_two"]
            v["small_got"] = swap(total, "tensor", core_bit)
        else:
            total = v["small"] + tie(v["small_got"])
            if stage == 1:
                v["small_got"] = swap(total, "tensor", chip_bit)
            elif stage < 2 + len(all_bits):
                if stage == 2:
                    total = jnp.concatenate([total, v["extra"]], axis=0)
                v["small_got"] = swap(total, "dp", all_bits[stage - 2])
        v["small"] = total
        return total

    def small_placed():
        for stage in range(2 + len(axis_bits("dp")[:SPLITS]), 3 + len(all_bits)):
            small_sum(stage)
        small = v["small"]
        v["small_out"] = unpack_small(
            me, small[0:8], small[8:], head, width // t_count
        )
        return v["small_out"][0]

    def sum_placed(name, rows, total, part, more=0):
        total = totals[total]
        v[name] = unpack_rows(
            tie(table_of(name)), total.keep[part], total.got[part], rows, more
        )
        return v[name][0]

    def late_placed():
        total = totals["L"]
        v["late"] = unpack_heads(
            tie(table_of("late")), total.keep[0], total.got[0], head, experts
        )
        return v["late"][2]

    tasks = {
        "ffn": feed_forward,
        "sh": share_core,
        "sha": share_add,
        "oc": lambda: rows_across("output"),
        "gi": lambda: rows_across("grad_inputs"),
        "pro": lambda: rows_placed("output"),
        "pri": lambda: rows_placed("grad_inputs"),
        "gna": grad_normed_add,
        "snb": second_norm,
        "low": low_across,
        "vb": value_grads,
        "ab": attention,
        "og": output_weight_grad,
        "pb": projections,
        "gca": grad_current_add,
        "fnb": first_norm,
        "orow": output_rows,
        "nu": small_placed,
        "Du": lambda: sum_placed("down", down_weight.shape[0], "F", 0),
        "Uu": lambda: sum_placed("up", up_weight.shape[0], "F", 1),
        "Vu": lambda: sum_placed("value", experts * head, "W", 0, experts),
        "Ou": lambda: sum_placed("out", experts * head, "W", 1),
        "Lu": late_placed,
    }
    for stage in range(5):
        tasks["n" + str(stage)] = functools.partial(small_sum, stage)
    for name in ORDER:
        if name in tasks:
            done = tasks[name]()
        else:
            done = totals[name[0]].step(*token)
        if done is not None:
            token = list(done) if isinstance(done, list) else [done]

    grad_gains, grad_biases, grad_content, grad_position, expert_counts = v["small_out"]
    grad_key_t, grad_query_t, grad_output_router, grad_position_t = v["late"]
    grad_value_t, grad_value_router = v["value"]
    return (
        v["output"].reshape(1, length, width),
        v["grad_inputs"].reshape(1, length, width),
        grad_gains,
        grad_biases,
        grad_query_t.T,
        grad_key_t.T,
        grad_value_t.T,
        grad_value_router.T,
        grad_output_router.T,
        v["out"][0],
        grad_position_t.T,
        grad_content.reshape(head),
        grad_position.reshape(head),
        v["up"][0],
        v["down"][0],
        expert_counts[:, head : head + experts],
    )


def solution(mesh):
    placed = (
        P("dp", None, None),
        P("dp", None, None),
        P("dp", None),
        P("dp", None, "tensor", None),
        P("dp", None, "tensor", None),
        P(),
        P(),
        P(None, "tensor"),
        P(None, "tensor"),
        P(None, "tensor"),
        P(None, "tensor"),
        P(None, "tensor"),
        P("tensor", None),
        P(None, "tensor"),
        P("tensor"),
        P("tensor"),
        P(None, "tensor"),
        P("tensor", None),
        P("dp", None, None),
    )
    return jax.shard_map(
        on_device,
        mesh=mesh,
        in_specs=placed,
        out_specs=(
            P("dp", None, None),
            P("dp", None, None),
            P(None, "tensor"),
            P(None, "tensor"),
            P(None, "tensor"),
            P(None, "tensor"),
            P(None, "tensor"),
            P(None, "tensor"),
            P(None, "tensor"),
            P("tensor", None),
            P(None, "tensor"),
            P("tensor"),
            P("tensor"),
            P(None, "tensor"),
            P("tensor", None),
            P(None, "tensor"),
        ),
        check_vma=False,
    )
```

```python
import functools
import math

import jax
import jax.numpy as jnp
from jax import lax
from jax.experimental import pallas as pl
from jax.experimental.pallas import tpu as pltpu
from jax.sharding import PartitionSpec as P

NORM_EPSILON = 1e-05
GELU_SCALE = 0.7978845608028654
GELU_CUBIC = 0.044715
LANES = 128
ROWS = 256
FINE = 32
SPLITS = 3
SECOND = ("up","out",)
ORDER = (
    "ffn", "gna", "sh", "sha", "snb", "F1", "orow", "vb", "F2", "low",
    "ab", "oc", "og", "F3", "pro", "L1", "pb", "n0", "W1", "n1",
    "L2", "F4", "n2", "W2", "L3", "gca", "n3", "F5", "L4", "n4",
    "W3", "fnb", "nu", "L5", "W4", "Du", "gi", "Lu", "pri", "W5",
    "Uu", "Vu", "Ou",
)
VMEM = 56 * 1024 * 1024
FLOPS_US = 1.1e9
SHRINK = 1000
BF16 = jnp.bfloat16
F32 = jnp.float32


def dot_first(left, right):
    return lax.dot_general(left, right, (((0,), (0,)), ((), ())), preferred_element_type=F32)


def dot_last(left, right):
    return lax.dot_general(left, right, (((1,), (1,)), ((), ())), preferred_element_type=F32)


def dot_plain(left, right):
    return jnp.dot(left, right, preferred_element_type=F32)


def gelu_parts(values):
    square = values * values
    tangent = jnp.tanh(GELU_SCALE * (values + GELU_CUBIC * values * square))
    half = 0.5 * (1.0 + tangent)
    slope = half + 0.5 * values * (1.0 - tangent * tangent) * (
        GELU_SCALE * (1.0 + 3.0 * GELU_CUBIC * square)
    )
    return (values * half, slope)


def unit_rows(values):
    average = jnp.mean(values, axis=-1, keepdims=True)
    centered = values - average
    spread = jnp.mean(centered * centered, axis=-1, keepdims=True)
    inverse = lax.rsqrt(spread + NORM_EPSILON)
    return (centered * inverse, inverse)


def norm_backward(upstream, unit, inverse, gain):
    grad_unit = upstream * gain
    return inverse * (
        grad_unit
        - jnp.mean(grad_unit, axis=-1, keepdims=True)
        - unit * jnp.mean(grad_unit * unit, axis=-1, keepdims=True)
    )


def lane_index(rows):
    return lax.broadcasted_iota(jnp.int32, (rows, LANES), 1)


def whole(array):
    rank = array.ndim
    return pl.BlockSpec(
        array.shape, lambda *_: (0,) * rank, pipeline_mode=pl.Buffered(1)
    )


def fixed(shape):
    return pl.BlockSpec(shape, lambda *_: (0,) * len(shape))


def params():
    return pltpu.CompilerParams(vmem_limit_bytes=VMEM)


def cost(flops, moved, special=0):
    return pl.CostEstimate(flops=int(flops) // SHRINK, bytes_accessed=int(moved) // SHRINK, transcendentals=0)


def axis_bits(name):
    count = lax.axis_size(name)
    bits = []
    bit = 1
    while bit < count:
        bits.append(bit)
        bit = bit * 2
    return bits


def relative_order(bits):
    count = 2 ** len(bits)
    order = []
    for place in range(count):
        value = 0
        for depth, bit in enumerate(bits):
            if place & (count >> (depth + 1)):
                value = value | bit
        order.append(value)
    return order


def swap(piece, name, bit):
    return lax.ppermute(piece, name, [(i, i ^ bit) for i in range(lax.axis_size(name))])


def add_pieces(left, right):
    return (left.astype(F32) + right.astype(F32)).astype(BF16)


def after(value, *others):
    return lax.optimization_barrier((value,) + others)[0]


class DpSum:
    def __init__(self, parts):
        self.keep = [keep for keep, _, _ in parts]
        self.send = [send for _, send, _ in parts]
        self.bits = [bits for _, _, bits in parts]
        self.stages = len(self.bits[0])
        self.more = [bit for bit in axis_bits("dp") if bit not in self.bits[0]]
        self.folded = 0
        self.depth = 0
        self.move(self.send, 0)

    def move(self, pieces, stage):
        bits = [bits[stage] for bits in self.bits]
        if len(pieces) > 1 and stage == self.stages - 1 and len(set(bits)) == 1:
            got = swap(jnp.concatenate(pieces, axis=0), "dp", bits[0])
            self.got = [got]
        else:
            self.got = [swap(piece, "dp", bit) for piece, bit in zip(pieces, bits)]

    def take(self, others):
        tied = lax.optimization_barrier(tuple(self.got) + tuple(others))
        got = tied[0 : len(self.got)]
        if len(got) < len(self.keep):
            got = [got[0][i : i + 1] for i in range(len(self.keep))]
        return got

    def step(self, *others):
        got = self.take(others)
        if self.folded < self.stages:
            self.folded = self.folded + 1
            if self.folded < self.stages:
                half = self.keep[0].shape[0] // 2
                self.send = [add_pieces(k[half:], g[half:]) for k, g in zip(self.keep, got)]
                self.keep = [add_pieces(k[:half], g[:half]) for k, g in zip(self.keep, got)]
                self.move(self.send, self.folded)
                return self.send
            self.keep = [add_pieces(k, g) for k, g in zip(self.keep, got)]
            for bit in self.more:
                self.keep = [add_pieces(k, swap(k, "dp", bit)) for k in self.keep]
            self.depth = self.stages
        else:
            self.keep = [jnp.concatenate([k, g], axis=0) for k, g in zip(self.keep, got)]
        self.depth = self.depth - 1
        self.move(self.keep, self.depth)
        return self.keep


def chunk_table(bits, name):
    place = jnp.bitwise_and(lax.axis_index(name), 2 ** len(bits) - 1)
    return jnp.bitwise_xor(jnp.array(relative_order(bits), jnp.int32), place)

def angles(place, coarse_ref, fine_ref):
    count = place.shape[1]
    slots = coarse_ref.shape[0] // 2
    freq = coarse_ref.shape[1] // 2
    leading = place // FINE
    trailing = lax.rem(place, FINE)
    coarse_rows = lax.broadcasted_iota(jnp.int32, (2 * slots, count), 0)
    fine_rows = lax.broadcasted_iota(jnp.int32, (2 * FINE, count), 0)
    coarse_hit = ((coarse_rows == leading) | (coarse_rows == leading + slots)).astype(BF16)
    fine_hit = ((fine_rows == trailing) | (fine_rows == trailing + FINE)).astype(BF16)
    big = dot_first(coarse_hit, coarse_ref[...])
    small = dot_first(fine_hit, fine_ref[...])
    cosine = big[:, 0:freq] * small[:, 0:freq] - big[:, freq:] * small[:, freq:]
    sine = big[:, freq:] * small[:, 0:freq] + big[:, 0:freq] * small[:, freq:]
    return cosine, sine


def trig_tables(first, count, step, pos_width):
    freq = pos_width // 2
    omega = jnp.exp(jnp.arange(freq, dtype=F32) * (-2.0 * math.log(10000.0) / pos_width))
    angle = (jnp.arange(count, dtype=F32) * step + first)[:, None] * omega
    table = jnp.concatenate([jnp.cos(angle), jnp.sin(angle)], axis=1)
    lead = lax.reduce_precision(table, 8, 7)
    return jnp.concatenate([lead, table - lead], axis=0).astype(BF16)


def fill_weights(head, experts, key_ref, router_ref, value_ref, scratch):
    scratch[0:head, :] = key_ref[...]
    scratch[head : head + experts, :] = router_ref[...]
    for e in range(experts):
        start = LANES * (e + 1)
        scratch[start : start + head, :] = value_ref[e * head : (e + 1) * head, :]


def front_body(
    head,
    experts,
    length,
    shift,
    memory_ref,
    inputs_ref,
    gains_ref,
    biases_ref,
    key_ref,
    value_ref,
    value_router_ref,
    query_ref,
    output_router_ref,
    position_ref,
    content_bias_ref,
    position_bias_ref,
    value_route_ref,
    output_route_ref,
    place_ref,
    coarse_ref,
    fine_ref,
    normed_ref,
    key_cat_ref,
    values_ref,
    gate_ref,
    content_query_ref,
    bias_query_ref,
    count_ref,
    probs_ref,
    attended_ref,
    weight_scratch,
    bias_scratch,
    key_scratch,
    value_scratch,
    query_scratch,
):
    step = pl.program_id(0)
    span = memory_ref.shape[0]
    keys = key_scratch.shape[0]
    mem_steps = (keys - length) // span
    split = LANES * (1 + experts)
    freq = coarse_ref.shape[1] // 2

    @pl.when(step == 0)
    def _():
        weight_scratch[...] = jnp.zeros_like(weight_scratch)
        bias_scratch[...] = jnp.zeros_like(bias_scratch)
        count_ref[...] = jnp.zeros_like(count_ref)
        fill_weights(head, experts, key_ref, value_router_ref, value_ref, weight_scratch)
        weight_scratch[split : split + head, :] = query_ref[...]
        weight_scratch[split + head : split + head + experts, :] = output_router_ref[...]
        bias_scratch[0:1, 0:head] = content_bias_ref[...]
        bias_scratch[1:2, 0:head] = position_bias_ref[...]

    old = step < mem_steps
    rows = jnp.where(old, memory_ref[...], inputs_ref[...]).astype(F32)
    unit, _ = unit_rows(rows)
    normed = (unit * gains_ref[0:1, :] + biases_ref[0:1, :]).astype(BF16)
    normed_ref[...] = normed
    product = dot_last(normed, weight_scratch[0:split, :])
    lane = lane_index(span)
    first = product[:, 0:LANES]
    key_piece = jnp.where(lane < head, first, 0.0).astype(BF16)

    def picks(route):
        row = lax.broadcasted_iota(jnp.int32, (LANES, span), 0) - head
        hit = (route[0:1, :] == row).astype(F32) + (route[1:2, :] == row).astype(F32)
        return hit.T

    chosen = picks(value_route_ref[...])
    gate = jax.nn.sigmoid(first) * chosen
    gate_ref[...] = gate.T[head : head + 8, :]
    total = jnp.zeros((span, LANES), F32)
    for e in range(experts):
        start = LANES * (e + 1)
        total = total + gate[:, head + e : head + e + 1] * product[:, start : start + LANES]
    values = total.astype(BF16)
    values_ref[...] = values
    current_place = lax.broadcasted_iota(jnp.int32, (1, span), 1) + (step - mem_steps) * span
    cosine, sine = angles(
        jnp.where(old, place_ref[...], current_place) + shift, coarse_ref, fine_ref
    )
    cos_low = cosine.astype(BF16)
    sin_low = sine.astype(BF16)
    key_cat_ref[:, 0:LANES] = key_piece
    key_cat_ref[:, LANES : LANES + freq] = cos_low
    key_cat_ref[:, LANES + freq :] = sin_low
    base = pl.multiple_of(step * span, span)
    key_scratch[pl.ds(base, span), 0:LANES] = key_piece
    key_scratch[pl.ds(base, span), LANES : LANES + freq] = cos_low
    key_scratch[pl.ds(base, span), LANES + freq :] = sin_low
    value_scratch[pl.ds(base, span), :] = values

    def variant(place):
        def run():
            last = dot_last(normed, weight_scratch[split:, :])
            query = jnp.where(lane < head, last, 0.0)
            content = (query + bias_scratch[0:1, :]).astype(BF16)
            biased = (query + bias_scratch[1:2, :]).astype(BF16)
            content_query_ref[...] = content
            bias_query_ref[...] = biased
            out_chosen = picks(output_route_ref[...])
            out_gate = jax.nn.sigmoid(last) * out_chosen
            count_ref[0:1, :] += jnp.sum(chosen, axis=0, keepdims=True)
            count_ref[1:2, :] += jnp.sum(out_chosen, axis=0, keepdims=True)
            rest = out_gate - out_gate.astype(BF16).astype(F32)
            extra = out_gate + pltpu.roll(rest, experts, 1)
            relative = dot_plain(biased[:, 0:head], position_ref[...])
            rel_sin = relative[:, 0:freq]
            rel_cos = relative[:, freq:]
            query_scratch[:, 0:LANES] = content
            query_scratch[:, LANES : LANES + freq] = (rel_sin * sine + rel_cos * cosine).astype(
                BF16
            )
            query_scratch[:, LANES + freq :] = (rel_cos * sine - rel_sin * cosine).astype(BF16)
            factor = head ** (-0.5) * math.log2(math.e)
            row = lax.broadcasted_iota(jnp.int32, (ROWS, ROWS), 0)
            col = lax.broadcasted_iota(jnp.int32, (ROWS, ROWS), 1)
            for part in range(span // ROWS):
                piece = slice(part * ROWS, (part + 1) * ROWS)
                seen = keys - length + place * span + (part + 1) * ROWS
                scores = dot_last(query_scratch[piece, :], key_scratch[0:seen, :])
                body = scores[:, 0 : seen - ROWS]
                tail = jnp.where(col <= row, scores[:, seen - ROWS :], -jnp.inf)
                top = factor * jnp.maximum(
                    jnp.max(body, axis=1, keepdims=True), jnp.max(tail, axis=1, keepdims=True)
                )
                body = jnp.exp2(body * factor - top)
                tail = jnp.exp2(tail * factor - top)
                share = 1.0 / (
                    jnp.sum(body, axis=1, keepdims=True) + jnp.sum(tail, axis=1, keepdims=True)
                )
                body = (body * share).astype(BF16)
                tail = (tail * share).astype(BF16)
                probs_ref[piece, 0 : seen - ROWS] = body
                probs_ref[piece, seen - ROWS : seen] = tail
                if seen < keys:
                    probs_ref[piece, seen:] = jnp.zeros((ROWS, keys - seen), BF16)
                result = dot_plain(body, value_scratch[0 : seen - ROWS, :]) + dot_plain(
                    tail, value_scratch[seen - ROWS : seen, :]
                )
                attended_ref[piece, :] = jnp.where(
                    lane[piece, :] < head, result, extra[piece, :]
                ).astype(BF16)

        return run

    for place in range(length // span):
        pl.when(step == mem_steps + place)(variant(place))


def front(
    memory,
    inputs,
    gains,
    biases,
    key_weight,
    value_weight,
    value_router,
    query_weight,
    output_router,
    position_weight,
    content_bias,
    position_bias,
    value_routes,
    output_routes,
    places,
    coarse,
    fine,
):
    mem_count, width = memory.shape
    length = inputs.shape[0]
    head = key_weight.shape[0]
    experts = value_router.shape[0]
    pos_width = coarse.shape[1]
    keys = mem_count + length
    span = 2 * ROWS
    mem_steps = mem_count // span
    old = lambda i: (jnp.minimum(i, mem_steps - 1), 0)
    new = lambda i: (jnp.maximum(i - mem_steps, 0), 0)
    every = lambda i: (i, 0)
    row = lambda size, index: pl.BlockSpec((span, size), index)
    turned = lambda index: (lambda i: index(i)[::-1])
    return pl.pallas_call(
        functools.partial(front_body, head, experts, length, 2 * mem_count),
        out_shape=(
            jax.ShapeDtypeStruct((keys, width), BF16),
            jax.ShapeDtypeStruct((keys, LANES + pos_width), BF16),
            jax.ShapeDtypeStruct((keys, LANES), BF16),
            jax.ShapeDtypeStruct((8, keys), F32),
            jax.ShapeDtypeStruct((length, LANES), BF16),
            jax.ShapeDtypeStruct((length, LANES), BF16),
            jax.ShapeDtypeStruct((8, LANES), F32),
            jax.ShapeDtypeStruct((length, keys), BF16),
            jax.ShapeDtypeStruct((length, LANES), BF16),
        ),
        grid=(keys // span,),
        in_specs=[
            row(width, old),
            row(width, new),
            whole(gains),
            whole(biases),
            whole(key_weight),
            whole(value_weight),
            whole(value_router),
            whole(query_weight),
            whole(output_router),
            whole(position_weight),
            whole(content_bias),
            whole(position_bias),
            pl.BlockSpec((value_routes.shape[0], span), turned(every)),
            pl.BlockSpec((output_routes.shape[0], span), turned(new)),
            pl.BlockSpec((1, span), turned(old)),
            whole(coarse),
            whole(fine),
        ],
        out_specs=(
            row(width, every),
            row(LANES + pos_width, every),
            row(LANES, every),
            pl.BlockSpec((8, span), turned(every)),
            row(LANES, new),
            row(LANES, new),
            fixed((8, LANES)),
            row(keys, new),
            row(LANES, new),
        ),
        scratch_shapes=[
            pltpu.VMEM((LANES * (2 + experts), width), BF16),
            pltpu.VMEM((8, LANES), F32),
            pltpu.VMEM((keys, LANES + pos_width), BF16),
            pltpu.VMEM((keys, LANES), BF16),
            pltpu.VMEM((span, LANES + pos_width), BF16),
        ],
        compiler_params=params(),
        cost_estimate=cost(30 * FLOPS_US, 30e6),
        name="front",
    )(
        memory,
        inputs,
        gains,
        biases,
        key_weight,
        value_weight,
        value_router,
        query_weight,
        output_router,
        position_weight,
        content_bias,
        position_bias,
        value_routes,
        output_routes,
        places,
        coarse,
        fine,
    )


def attend_back_body(head, heads, shift, me_ref, table_ref, *refs):
    grad_refs = refs[0:heads]
    (
        probs_ref,
        key_cat_ref,
        values_ref,
        content_ref,
        bias_ref,
        coarse_ref,
        fine_ref,
        position_ref,
        normed_ref,
        grad_keys_ref,
        grad_query_ref,
        keep_ref,
        send_ref,
        sums_ref,
        position_scratch,
        relative_scratch,
        grad_scratch,
        keys_scratch,
        weight_scratch,
        key_cat_scratch,
        normed_scratch,
        copy_sems,
    ) = refs[heads:]
    step = pl.program_id(0)
    key_copy = pltpu.make_async_copy(key_cat_ref, key_cat_scratch, copy_sems.at[0])
    normed_copy = pltpu.make_async_copy(normed_ref, normed_scratch, copy_sems.at[1])
    keys = key_cat_scratch.shape[0]
    length = pl.num_programs(0) * ROWS
    freq = coarse_ref.shape[1] // 2
    scale = head ** (-0.5)

    @pl.when(step == 0)
    def _():
        key_copy.start()
        normed_copy.start()
        keys_scratch[...] = jnp.zeros_like(keys_scratch)
        weight_scratch[...] = jnp.zeros_like(weight_scratch)
        sums_ref[...] = jnp.zeros_like(sums_ref)
        position_scratch[...] = jnp.zeros_like(position_scratch)
        position_scratch[0:head, :] = position_ref[...]
        for distance, grad_ref in enumerate(grad_refs):
            grad_scratch[jnp.bitwise_xor(me_ref[0], distance)] = grad_ref[0]

    lane = lane_index(ROWS)
    packed = grad_scratch[step]
    upstream = jnp.where(lane < head, packed, jnp.zeros_like(packed))
    place = lax.broadcasted_iota(jnp.int32, (1, ROWS), 1) + step * ROWS + shift
    cosine, sine = angles(place, coarse_ref, fine_ref)

    def variant(block):
        def run():
            seen = keys - length_static + (block + 1) * ROWS
            weights_low = probs_ref[:, 0:seen]
            weights = weights_low.astype(F32)
            grad_weights = dot_last(upstream, values_ref[0:seen, :])
            inner = jnp.sum(grad_weights * weights, axis=1, keepdims=True)
            grad_scores = (weights * (grad_weights - inner)).astype(BF16)
            keys_scratch[:, 0:seen] += dot_first(content_ref[...], grad_scores) * scale
            if block == 0:
                key_copy.wait()
                normed_copy.wait()
            grad_query = dot_plain(grad_scores, key_cat_scratch[0:seen, :]) * scale
            grad_content = grad_query[:, 0:LANES]
            grad_sin = grad_query[:, LANES : LANES + freq]
            grad_cos = grad_query[:, LANES + freq :]
            relative_scratch[:, 0:freq] = (grad_sin * sine - grad_cos * cosine).astype(BF16)
            relative_scratch[:, freq:] = (grad_sin * cosine + grad_cos * sine).astype(BF16)
            relative = relative_scratch[...]
            grad_bias = dot_last(relative, position_scratch[...])
            weight_scratch[2 * LANES :, :] += dot_first(bias_ref[...], relative)
            sums_ref[0:1, :] += jnp.sum(grad_content, axis=0, keepdims=True)
            sums_ref[1:2, :] += jnp.sum(grad_bias, axis=0, keepdims=True)
            both = jnp.where(lane < head, (grad_content + grad_bias).astype(BF16), packed)
            grad_query_ref[...] = both
            weight_scratch[LANES : 2 * LANES, :] += dot_first(
                both, normed_scratch[seen - ROWS : seen, :]
            )

        return run

    length_static = heads * ROWS
    for block in range(length_static // ROWS):
        pl.when(step == block)(variant(block))

    @pl.when(step == pl.num_programs(0) - 1)
    def _():
        grad_keys = keys_scratch[...].astype(BF16)
        grad_keys_ref[...] = grad_keys
        weight_scratch[0:LANES, :] = dot_plain(grad_keys, normed_scratch[...])
        half, chunk, _ = keep_ref.shape
        for place in range(half):
            start = pl.multiple_of(table_ref[place] * chunk, 8)
            keep_ref[place] = weight_scratch[pl.ds(start, chunk), :].astype(BF16)
            start = pl.multiple_of(table_ref[half + place] * chunk, 8)
            send_ref[place] = weight_scratch[pl.ds(start, chunk), :].astype(BF16)


def attend_back(
    me,
    table,
    grads,
    probs,
    key_cat,
    values,
    content_query,
    bias_query,
    coarse,
    fine,
    position_weight,
    normed,
):
    length, keys = probs.shape
    head, pos_width = position_weight.shape
    width = normed.shape[1]
    count = table.shape[0]
    half = jax.ShapeDtypeStruct((count // 2, 3 * LANES // count, width), BF16)
    heads = len(grads)
    every = lambda i, *_: (i, 0)
    row = lambda size: pl.BlockSpec((ROWS, size), every)
    return pl.pallas_call(
        functools.partial(attend_back_body, head, heads, 2 * (keys - length)),
        out_shape=(
            jax.ShapeDtypeStruct((LANES, keys), BF16),
            jax.ShapeDtypeStruct((length, LANES), BF16),
            half,
            half,
            jax.ShapeDtypeStruct((8, LANES), F32),
        ),
        grid_spec=pltpu.PrefetchScalarGridSpec(
            num_scalar_prefetch=2,
            grid=(length // ROWS,),
            in_specs=[whole(grad) for grad in grads]
            + [
                row(keys),
                pl.BlockSpec(memory_space=pl.ANY),
                whole(values),
                row(LANES),
                row(LANES),
                whole(coarse),
                whole(fine),
                whole(position_weight),
                pl.BlockSpec(memory_space=pl.ANY),
            ],
            out_specs=(
                fixed((LANES, keys)),
                row(LANES),
                fixed(half.shape),
                fixed(half.shape),
                fixed((8, LANES)),
            ),
            scratch_shapes=[
                pltpu.VMEM((LANES, pos_width), BF16),
                pltpu.VMEM((ROWS, pos_width), BF16),
                pltpu.VMEM((heads, ROWS, LANES), BF16),
                pltpu.VMEM((LANES, keys), F32),
                pltpu.VMEM((3 * LANES, width), F32),
                pltpu.VMEM(key_cat.shape, BF16),
                pltpu.VMEM(normed.shape, BF16),
                pltpu.SemaphoreType.DMA((2,)),
            ],
        ),
        compiler_params=params(),
        cost_estimate=cost(17 * FLOPS_US, 25e6),
        name="attend_back",
    )(
        me,
        table,
        *grads,
        probs,
        key_cat,
        values,
        content_query,
        bias_query,
        coarse,
        fine,
        position_weight,
        normed,
    )


def value_back_body(head, experts, heads, me_ref, table_ref, *refs):
    grad_refs = refs[0:heads]
    (
        probs_ref,
        normed_ref,
        gate_ref,
        weight_ref,
        grad_values_ref,
        logit_ref,
        keep_ref,
        send_ref,
        grad_scratch,
        packed_scratch,
        acc,
    ) = refs[heads:]
    step = pl.program_id(0)

    @pl.when(step == 0)
    def _():
        lane = lane_index(ROWS)
        for distance, grad_ref in enumerate(grad_refs):
            start = pl.multiple_of(jnp.bitwise_xor(me_ref[0], distance) * ROWS, ROWS)
            piece = grad_ref[0]
            grad_scratch[pl.ds(start, ROWS), :] = jnp.where(
                lane < head, piece, jnp.zeros_like(piece)
            )
        packed_scratch[...] = jnp.zeros_like(packed_scratch)
        acc[...] = jnp.zeros_like(acc)

    grad_values = dot_first(grad_scratch[...], probs_ref[...])
    grad_values_ref[...] = grad_values
    expert_values = dot_last(weight_ref[...], normed_ref[...])
    logits = []
    for e in range(experts):
        piece = slice(e * head, (e + 1) * head)
        gate = gate_ref[e : e + 1, :]
        packed_scratch[piece, :] = (gate * grad_values[0:head, :]).astype(BF16)
        inner = jnp.sum(expert_values[piece, :] * grad_values[0:head, :], axis=0, keepdims=True)
        logits.append(inner * gate * (1.0 - gate))
    logits.append(jnp.zeros((8 - experts, logits[0].shape[1]), F32))
    logit = jnp.concatenate(logits, axis=0)
    logit_ref[...] = logit
    packed_scratch[experts * head : experts * head + 8, :] = logit.astype(BF16)
    acc[...] += dot_plain(packed_scratch[...], normed_ref[...])

    @pl.when(step == pl.num_programs(0) - 1)
    def _():
        half, chunk, _ = keep_ref.shape
        for place in range(half):
            start = pl.multiple_of(table_ref[place] * chunk, 8)
            keep_ref[place] = acc[pl.ds(start, chunk), :].astype(BF16)
            start = pl.multiple_of(table_ref[half + place] * chunk, 8)
            send_ref[place] = acc[pl.ds(start, chunk), :].astype(BF16)


def value_back(me, table, grads, probs, normed, gates, weight, head, experts):
    heads = len(grads)
    length, keys = probs.shape
    width = normed.shape[1]
    count = table.shape[0]
    span = 2 * ROWS
    rows = experts * head + 8
    rows = rows + -rows % (8 * count)
    half = jax.ShapeDtypeStruct((count // 2, rows // count, width), BF16)
    return pl.pallas_call(
        functools.partial(value_back_body, head, experts, heads),
        out_shape=(
            jax.ShapeDtypeStruct((LANES, keys), F32),
            jax.ShapeDtypeStruct((8, keys), F32),
            half,
            half,
        ),
        grid_spec=pltpu.PrefetchScalarGridSpec(
            num_scalar_prefetch=2,
            grid=(keys // span,),
            in_specs=[whole(grad) for grad in grads]
            + [
                pl.BlockSpec((length, span), lambda i, *_: (0, i)),
                pl.BlockSpec((span, width), lambda i, *_: (i, 0)),
                pl.BlockSpec((8, span), lambda i, *_: (0, i)),
                whole(weight),
            ],
            out_specs=(
                pl.BlockSpec((LANES, span), lambda i, *_: (0, i)),
                pl.BlockSpec((8, span), lambda i, *_: (0, i)),
                fixed(half.shape),
                fixed(half.shape),
            ),
            scratch_shapes=[
                pltpu.VMEM((length, LANES), BF16),
                pltpu.VMEM((rows, span), BF16),
                pltpu.VMEM((rows, width), F32),
            ],
        ),
        compiler_params=params(),
        cost_estimate=cost(8 * FLOPS_US, 10e6),
        name="value_back",
    )(me, table, *grads, probs, normed, gates, weight)


def spread_weights(head, experts, weight_refs, scratch):
    scratch[...] = jnp.zeros_like(scratch)
    for j, weight_ref in enumerate(weight_refs):
        for e in range(experts):
            start = LANES * (experts * j + e)
            scratch[start : start + head, :] = weight_ref[e * head : (e + 1) * head, :]


def gate_spread(head, experts):
    shape = (LANES, experts * LANES)
    row = lax.broadcasted_iota(jnp.int32, shape, 0) - head
    block = lax.broadcasted_iota(jnp.int32, shape, 1) // LANES
    return ((row == block) | (row == block + experts)).astype(BF16)


def forward_body(head, experts, heads, place_ref, down_table_ref, up_table_ref, *refs):
    pair = 2
    attended_refs = [refs[part * heads : (part + 1) * heads] for part in range(pair)]
    rest = refs[pair * heads :]
    weight_refs = rest[0:heads]
    rest = rest[heads:]
    inputs_refs = rest[0:pair]
    cotangent_refs = rest[pair : 2 * pair]
    (
        up_ref,
        down_ref,
        gains_ref,
        biases_ref,
        resid_ref,
        grad_normed_ref,
        share_ref,
        down_keep_ref,
        down_send_ref,
        up_keep_ref,
        up_send_ref,
        weight_scratch,
        mixed_scratch,
        active_scratch,
        normed_scratch,
        upper_scratch,
        cotangent_scratch,
        down_acc,
        up_acc,
        up_scratch,
        down_scratch,
        weight_sems,
    ) = rest[2 * pair :]
    step = pl.program_id(0)
    final = pl.num_programs(0) - 1
    up_copy = pltpu.make_async_copy(up_ref, up_scratch, weight_sems.at[0])
    down_copy = pltpu.make_async_copy(down_ref, down_scratch, weight_sems.at[1])

    @pl.when(step == 0)
    def _():
        up_copy.start()
        down_copy.start()
        spread_weights(head, experts, weight_refs, weight_scratch)

    lane = lane_index(ROWS)
    spread = gate_spread(head, experts)
    for part in range(pair):
        piece = slice(part * ROWS, (part + 1) * ROWS)
        for j, attended_ref in enumerate(attended_refs[part]):
            packed = attended_ref[...]
            gate = dot_plain(packed, spread)
            attended = jnp.where(lane < head, packed.astype(F32), 0.0)
            for e in range(experts):
                start = LANES * (experts * j + e)
                mixed_scratch[piece, start : start + LANES] = (
                    attended * gate[:, e * LANES : (e + 1) * LANES]
                ).astype(BF16)
    pieces = [slice(part * ROWS, (part + 1) * ROWS) for part in range(pair)]
    state = [{} for _ in range(pair)]

    def mix(part):
        state[part]["mixed"] = dot_plain(mixed_scratch[pieces[part], :], weight_scratch[...])

    def grad_in(part):
        cotangent = cotangent_refs[part][...]
        cotangent_scratch[pieces[part], :] = cotangent
        state[part]["grad"] = dot_last(cotangent, down_scratch[...])

    def norm(part):
        resid = inputs_refs[part][...].astype(F32) + state[part]["mixed"]
        if part == 0:

            @pl.when(step == final)
            def _():
                resid_ref[...] = resid

        unit, _ = unit_rows(resid)
        normed = (unit * gains_ref[1:2, :] + biases_ref[1:2, :]).astype(BF16)
        normed_scratch[pieces[part], :] = normed
        state[part]["normed"] = normed

    def upper(part):
        state[part]["upper"] = dot_plain(state[part]["normed"], up_scratch[...])

    def activate(part):
        active, slope = gelu_parts(state[part]["upper"])
        active = active.astype(BF16)
        active_scratch[pieces[part], :] = active
        grad_upper = (state[part]["grad"] * slope).astype(BF16)
        upper_scratch[pieces[part], :] = grad_upper
        state[part]["active"] = active
        state[part]["grad_upper"] = grad_upper

    def leave(part):
        grad_normed_ref[part] = dot_last(state[part]["grad_upper"], up_scratch[...]).astype(BF16)
        share_ref[part] = dot_plain(state[part]["active"], down_scratch[...]).astype(BF16)

    mix(0)

    @pl.when(step == 0)
    def _():
        up_copy.wait()
        down_copy.wait()

    norm(0)
    grad_in(0)
    upper(0)
    mix(1)
    activate(0)
    norm(1)
    leave(0)
    grad_in(1)
    upper(1)
    activate(1)
    leave(1)
    down_grad = dot_first(active_scratch[...], cotangent_scratch[...])
    up_grad = dot_first(normed_scratch[...], upper_scratch[...])

    @pl.when(step == 0)
    def _():
        down_acc[...] = down_grad
        up_acc[...] = up_grad

    @pl.when(step > 0)
    def _():
        down_acc[...] += down_grad
        up_acc[...] += up_grad

    @pl.when(step == final)
    def _():
        for table_ref, acc, keep_ref, send_ref in (
            (down_table_ref, down_acc, down_keep_ref, down_send_ref),
            (up_table_ref, up_acc, up_keep_ref, up_send_ref),
        ):
            half, chunk, _ = keep_ref.shape
            for place in range(half):
                start = pl.multiple_of(table_ref[place] * chunk, chunk)
                keep_ref[place] = acc[pl.ds(start, chunk), :].astype(BF16)
                start = pl.multiple_of(table_ref[half + place] * chunk, chunk)
                send_ref[place] = acc[pl.ds(start, chunk), :].astype(BF16)


def forward_ffn(
    places,
    down_table,
    up_table,
    attended,
    weights,
    inputs,
    cotangent,
    up,
    down,
    gains,
    biases,
    experts,
):
    heads = len(attended)
    length, width = inputs.shape
    head = weights[0].shape[0] // experts
    hidden = up.shape[1]
    blocks = length // ROWS
    count = down_table.shape[0]
    chunk = hidden // count
    steps = blocks // 2
    place = lambda i, part: (steps - 1 - i) * 2 + part
    row = lambda size, part: pl.BlockSpec(
        (ROWS, size), lambda i, place_ref, *_: (place_ref[place(i, part)], 0)
    )
    relative = pl.BlockSpec((2, ROWS, width), lambda i, *_: (steps - 1 - i, 0, 0))
    half = lambda rows: jax.ShapeDtypeStruct((count // 2, rows, width), BF16)
    return pl.pallas_call(
        functools.partial(forward_body, head, experts, heads),
        out_shape=(
            jax.ShapeDtypeStruct((ROWS, width), F32),
            jax.ShapeDtypeStruct((blocks, ROWS, width), BF16),
            jax.ShapeDtypeStruct((blocks, ROWS, width), BF16),
            half(chunk),
            half(chunk),
            half(width // count),
            half(width // count),
        ),
        grid_spec=pltpu.PrefetchScalarGridSpec(
            num_scalar_prefetch=3,
            grid=(steps,),
            in_specs=[row(LANES, 0) for _ in attended]
            + [row(LANES, 1) for _ in attended]
            + [whole(weight) for weight in weights]
            + [row(width, 0), row(width, 1), row(width, 0), row(width, 1)]
            + [pl.BlockSpec(memory_space=pl.ANY), pl.BlockSpec(memory_space=pl.ANY)]
            + [whole(gains), whole(biases)],
            out_specs=(
                fixed((ROWS, width)),
                relative,
                relative,
                fixed((count // 2, chunk, width)),
                fixed((count // 2, chunk, width)),
                fixed((count // 2, width // count, hidden)),
                fixed((count // 2, width // count, hidden)),
            ),
            scratch_shapes=[
                pltpu.VMEM((heads * experts * LANES, width), BF16),
                pltpu.VMEM((2 * ROWS, heads * experts * LANES), BF16),
                pltpu.VMEM((2 * ROWS, hidden), BF16),
                pltpu.VMEM((2 * ROWS, width), BF16),
                pltpu.VMEM((2 * ROWS, hidden), BF16),
                pltpu.VMEM((2 * ROWS, width), BF16),
                pltpu.VMEM((hidden, width), F32),
                pltpu.VMEM((width, hidden), F32),
                pltpu.VMEM(up.shape, BF16),
                pltpu.VMEM(down.shape, BF16),
                pltpu.SemaphoreType.DMA((2,)),
            ],
        ),
        compiler_params=params(),
        cost_estimate=cost(28 * FLOPS_US, 30e6),
        name="forward_ffn",
    )(
        places,
        down_table,
        up_table,
        *attended,
        *attended,
        *weights,
        inputs,
        inputs,
        cotangent,
        cotangent,
        up,
        down,
        gains,
        biases,
    )


def second_norm_back_body(head, experts, heads, me_ref, *refs):
    attended_refs = refs[0:heads]
    weight_refs = refs[heads : 2 * heads]
    (
        left_ref,
        right_ref,
        resid_ref,
        cotangent_ref,
        gains_ref,
        grad_resid_ref,
        low_ref,
        packed_ref,
        sums_ref,
        weight_scratch,
        product_scratch,
    ) = refs[2 * heads :]
    spread_weights(head, experts, weight_refs, weight_scratch)
    unit, inverse = unit_rows(resid_ref[...])
    grad = left_ref[0].astype(F32) + right_ref[0].astype(F32)
    sums_ref[...] = jnp.zeros_like(sums_ref)
    sums_ref[2:3, :] = jnp.sum(grad * unit, axis=0, keepdims=True)
    sums_ref[3:4, :] = jnp.sum(grad, axis=0, keepdims=True)
    grad_resid = cotangent_ref[...].astype(F32) + norm_backward(
        grad, unit, inverse, gains_ref[1:2, :]
    )
    grad_resid_ref[...] = grad_resid
    low = grad_resid.astype(BF16)
    low_ref[0] = low
    grad_mixed = dot_last(low, weight_scratch[...])
    lane = lane_index(ROWS)
    spread = gate_spread(head, experts)
    collect = spread.T[:, 0:LANES]
    for j, attended_ref in enumerate(attended_refs):
        packed = attended_ref[...]
        gate = dot_plain(packed, spread)
        attended = jnp.where(lane < head, packed.astype(F32), 0.0)
        total = jnp.zeros((ROWS, LANES), F32)
        for e in range(experts):
            start = LANES * (experts * j + e)
            block = slice(e * LANES, (e + 1) * LANES)
            piece = grad_mixed[:, start : start + LANES]
            total = total + gate[:, block] * piece
            product_scratch[:, block] = piece * attended
        product = product_scratch[...]
        lead = product.astype(BF16)
        rest = (product - lead.astype(F32)).astype(BF16)
        logits = dot_plain(lead, collect) + dot_plain(rest, collect)
        own = packed.astype(F32)
        own = own + pltpu.roll(own, LANES - experts, 1)
        logits = logits * own * (1.0 - own)
        total = jnp.where((lane >= head) & (lane < head + experts), logits, total)
        packed_ref[j] = total.astype(BF16)


def second_norm_back(me, attended, weights, left, right, resid, cotangent, gains, experts):
    heads = len(attended)
    width = resid.shape[1]
    head = weights[0].shape[0] // experts
    own = lambda i, me_ref: (me_ref[0], 0)
    row = lambda size: pl.BlockSpec((ROWS, size), own)
    return pl.pallas_call(
        functools.partial(second_norm_back_body, head, experts, heads),
        out_shape=(
            jax.ShapeDtypeStruct((ROWS, width), F32),
            jax.ShapeDtypeStruct((1, ROWS, width), BF16),
            jax.ShapeDtypeStruct((heads, ROWS, LANES), BF16),
            jax.ShapeDtypeStruct((8, width), F32),
        ),
        grid_spec=pltpu.PrefetchScalarGridSpec(
            num_scalar_prefetch=1,
            grid=(1,),
            in_specs=[row(LANES) for _ in attended]
            + [whole(weight) for weight in weights]
            + [whole(left), whole(right), whole(resid), row(width), whole(gains)],
            out_specs=(
                fixed((ROWS, width)),
                fixed((1, ROWS, width)),
                fixed((heads, ROWS, LANES)),
                fixed((8, width)),
            ),
            scratch_shapes=[
                pltpu.VMEM((heads * experts * LANES, width), BF16),
                pltpu.VMEM((ROWS, experts * LANES), F32),
            ],
        ),
        compiler_params=params(),
        cost_estimate=cost(7 * FLOPS_US, 12e6),
        name="second_norm_back",
    )(me, *attended, *weights, left, right, resid, cotangent, gains)


def output_grad_body(
    head, experts, place_ref, table_ref, attended_ref, *refs
):
    blocks = place_ref.shape[0]
    grad_refs = refs[0:blocks]
    keep_ref, send_ref, mixed, rows, acc = refs[blocks:]
    half, chunk, _ = keep_ref.shape
    for place, grad_ref in enumerate(grad_refs):
        start = pl.multiple_of(place_ref[place] * ROWS, ROWS)
        packed = attended_ref[pl.ds(start, ROWS), :].astype(F32).T
        piece = slice(place * ROWS, (place + 1) * ROWS)
        for e in range(experts):
            gate = packed[head + e : head + e + 1, :] + packed[
                head + experts + e : head + experts + e + 1, :
            ]
            mixed[e * head : (e + 1) * head, piece] = (packed[0:head, :] * gate).astype(BF16)
        rows[piece, :] = grad_ref[0]
    mixed[experts * head :, :] = jnp.zeros_like(mixed[experts * head :, :])
    acc[...] = dot_plain(mixed[...], rows[...])
    for place in range(half):
        start = pl.multiple_of(table_ref[place] * chunk, 8)
        keep_ref[place] = acc[pl.ds(start, chunk), :].astype(BF16)
        start = pl.multiple_of(table_ref[half + place] * chunk, 8)
        send_ref[place] = acc[pl.ds(start, chunk), :].astype(BF16)


def output_grad(places, table, attended, grads, head, experts):
    count = table.shape[0]
    length = attended.shape[0]
    width = grads[0].shape[2]
    rows = experts * head
    rows = rows + -rows % (8 * count)
    chunk = rows // count
    half = jax.ShapeDtypeStruct((count // 2, chunk, width), BF16)
    return pl.pallas_call(
        functools.partial(output_grad_body, head, experts),
        out_shape=(half, half),
        grid_spec=pltpu.PrefetchScalarGridSpec(
            num_scalar_prefetch=2,
            grid=(1,),
            in_specs=[whole(attended)] + [whole(grad) for grad in grads],
            out_specs=(fixed(half.shape), fixed(half.shape)),
            scratch_shapes=[
                pltpu.VMEM((rows, length), BF16),
                pltpu.VMEM((length, width), BF16),
                pltpu.VMEM((rows, width), F32),
            ],
        ),
        compiler_params=params(),
        cost_estimate=cost(5 * FLOPS_US, 4e6),
        name="output_grad",
    )(places, table, attended, *grads)


def project_back_body(head, experts, place_ref, *refs):
    pair = 2
    groups = []
    for index in range(7):
        groups.append(refs[index * pair : (index + 1) * pair])
    grad_keys_refs, grad_values_refs, gate_refs, logit_refs, query_refs, memory_refs, inputs_refs = (
        groups
    )
    (
        key_ref,
        value_ref,
        value_router_ref,
        query_ref,
        output_router_ref,
        bias_sums_ref,
        counts_ref,
        grad_current_ref,
        sums_ref,
        extra_ref,
        weight_scratch,
        packed_scratch,
    ) = refs[7 * pair :]
    step = pl.program_id(0)
    split = LANES * (1 + experts)
    cur_steps = place_ref.shape[0] // pair
    current = step < cur_steps

    @pl.when(step == 0)
    def _():
        sums_ref[...] = jnp.zeros_like(sums_ref)
        extra_ref[...] = jnp.zeros_like(extra_ref)
        extra_ref[0:2, 0:LANES] = bias_sums_ref[0:2, :]
        extra_ref[2:4, 0:LANES] = counts_ref[0:2, :]
        weight_scratch[...] = jnp.zeros_like(weight_scratch)
        packed_scratch[...] = jnp.zeros_like(packed_scratch)
        fill_weights(head, experts, key_ref, value_router_ref, value_ref, weight_scratch)
        weight_scratch[split : split + head, :] = query_ref[...]
        weight_scratch[split + head : split + head + experts, :] = output_router_ref[...]

    for part in range(pair):
        piece = slice(part * ROWS, (part + 1) * ROWS)
        grad_values = grad_values_refs[part][0:head, :]
        packed_scratch[0:head, piece] = grad_keys_refs[part][0:head, :]
        packed_scratch[head : head + 8, piece] = logit_refs[part][...].astype(BF16)
        for e in range(experts):
            start = LANES * (e + 1)
            gate = gate_refs[part][e : e + 1, :]
            packed_scratch[start : start + head, piece] = (gate * grad_values).astype(BF16)
    grads = dot_first(packed_scratch[...], weight_scratch[0:split, :])
    for part in range(pair):
        piece = slice(part * ROWS, (part + 1) * ROWS)
        grad = grads[piece, :]
        more = dot_plain(query_refs[part][...], weight_scratch[split:, :])
        grad = grad + jnp.where(current, more, 0.0)
        rows = jnp.where(current, inputs_refs[part][...], memory_refs[part][...]).astype(F32)
        unit, _ = unit_rows(rows)
        sums_ref[0:1, :] += jnp.sum(grad * unit, axis=0, keepdims=True)
        sums_ref[1:2, :] += jnp.sum(grad, axis=0, keepdims=True)

        @pl.when(current)
        def _():
            grad_current_ref[part] = grad.astype(BF16)


def project_back(
    places,
    grad_keys,
    grad_values,
    gates,
    logits,
    grad_query,
    memory,
    inputs,
    key_weight,
    value_weight,
    value_router,
    query_weight,
    output_router,
    bias_sums,
    counts,
):
    keys = grad_keys.shape[1]
    length, width = inputs.shape
    head = key_weight.shape[0]
    experts = value_router.shape[0]
    mem_blocks = (keys - length) // ROWS
    cur_blocks = length // ROWS
    cur_steps = cur_blocks // 2
    split = LANES * (1 + experts)
    fresh = lambda i, part, place_ref: place_ref[2 * jnp.minimum(i, cur_steps - 1) + part]
    past = lambda i, part, place_ref: 2 * jnp.maximum(i - cur_steps, 0) + part
    every = lambda i, part, place_ref: jnp.where(
        i < cur_steps, fresh(i, part, place_ref) + mem_blocks, past(i, part, place_ref)
    )

    def rows(size, index):
        return [
            pl.BlockSpec((ROWS, size), lambda i, place_ref, p=part: (index(i, p, place_ref), 0))
            for part in range(2)
        ]

    def columns(size):
        return [
            pl.BlockSpec((size, ROWS), lambda i, place_ref, p=part: (0, every(i, p, place_ref)))
            for part in range(2)
        ]

    twice = lambda *arrays: [array for array in arrays for _ in range(2)]
    weights = [key_weight, value_weight, value_router, query_weight, output_router]
    return pl.pallas_call(
        functools.partial(project_back_body, head, experts),
        out_shape=(
            jax.ShapeDtypeStruct((cur_blocks, ROWS, width), BF16),
            jax.ShapeDtypeStruct((8, width), F32),
            jax.ShapeDtypeStruct((8, width), F32),
        ),
        grid_spec=pltpu.PrefetchScalarGridSpec(
            num_scalar_prefetch=1,
            grid=(keys // (2 * ROWS),),
            in_specs=columns(LANES)
            + columns(LANES)
            + columns(8)
            + columns(8)
            + rows(LANES, fresh)
            + rows(width, past)
            + rows(width, fresh)
            + [whole(weight) for weight in weights]
            + [whole(bias_sums), whole(counts)],
            out_specs=(
                pl.BlockSpec(
                    (2, ROWS, width), lambda i, *_: (jnp.minimum(i, cur_steps - 1), 0, 0)
                ),
                fixed((8, width)),
                fixed((8, width)),
            ),
            scratch_shapes=[
                pltpu.VMEM((split + LANES, width), BF16),
                pltpu.VMEM((split, 2 * ROWS), BF16),
            ],
        ),
        compiler_params=params(),
        cost_estimate=cost(12 * FLOPS_US, 15e6),
        name="project_back",
    )(
        places,
        *twice(grad_keys, grad_values, gates, logits, grad_query, memory, inputs),
        *weights,
        bias_sums,
        counts,
    )


def first_norm_back(me, left, right, inputs, grad_resid, gains):
    width = inputs.shape[1]

    def body(me_ref, left_ref, right_ref, inputs_ref, resid_ref, gains_ref, out_ref):
        unit, inverse = unit_rows(inputs_ref[...].astype(F32))
        grad = left_ref[0].astype(F32) + right_ref[0].astype(F32)
        out_ref[0] = (
            resid_ref[...] + norm_backward(grad, unit, inverse, gains_ref[0:1, :])
        ).astype(BF16)

    return pl.pallas_call(
        body,
        out_shape=jax.ShapeDtypeStruct((1, ROWS, width), BF16),
        grid_spec=pltpu.PrefetchScalarGridSpec(
            num_scalar_prefetch=1,
            grid=(1,),
            in_specs=[
                whole(left),
                whole(right),
                pl.BlockSpec((ROWS, width), lambda i, me_ref: (me_ref[0], 0)),
                whole(grad_resid),
                whole(gains),
            ],
            out_specs=fixed((1, ROWS, width)),
        ),
        compiler_params=params(),
        cost_estimate=cost(3 * FLOPS_US, 4e6),
        name="first_norm_back",
    )(me, left, right, inputs, grad_resid, gains)


def place_rows(places, pieces):
    _, rows, width = pieces[0].shape
    count = len(pieces)

    def body(place_ref, *refs):
        out_ref = refs[count]
        for place in range(count):
            start = pl.multiple_of(place_ref[place] * rows, rows)
            out_ref[pl.ds(start, rows), :] = refs[place][0]

    return pl.pallas_call(
        body,
        out_shape=jax.ShapeDtypeStruct((count * rows, width), pieces[0].dtype),
        grid_spec=pltpu.PrefetchScalarGridSpec(
            num_scalar_prefetch=1,
            grid=(1,),
            in_specs=[whole(piece) for piece in pieces],
            out_specs=fixed((count * rows, width)),
        ),
        compiler_params=params(),
        cost_estimate=cost(3 * FLOPS_US, 4e6),
        name="place_rows",
    )(places, *pieces)


def unpack_rows(table, own, got, rows_out, more=0):
    half, rows, width = own.shape
    total = 2 * half * rows
    part = width // 2

    def body(table_ref, own_ref, got_ref, out_ref, *rest):
        scratch = rest[1:] if more else rest
        rows_ref = scratch[0] if scratch else out_ref
        for place in range(half):
            start = pl.multiple_of(table_ref[place] * rows, 8)
            rows_ref[pl.ds(start, rows), :] = own_ref[place].astype(F32)
            start = pl.multiple_of(table_ref[half + place] * rows, 8)
            rows_ref[pl.ds(start, rows), :] = got_ref[place].astype(F32)
        if scratch:
            out_ref[...] = rows_ref[0:rows_out, :]
        if more:
            rest[0][...] = rows_ref[rows_out : rows_out + more, :]

    shapes = [jax.ShapeDtypeStruct((rows_out, width), F32)]
    if more:
        shapes.append(jax.ShapeDtypeStruct((more, width), F32))
    chunks = pl.BlockSpec((half, rows, part), lambda i, _: (0, 0, i))
    return pl.pallas_call(
        body,
        out_shape=tuple(shapes),
        grid_spec=pltpu.PrefetchScalarGridSpec(
            num_scalar_prefetch=1,
            grid=(2,),
            in_specs=[chunks, chunks],
            out_specs=tuple(
                pl.BlockSpec((shape.shape[0], part), lambda i, _: (0, i)) for shape in shapes
            ),
            scratch_shapes=[] if total == rows_out else [pltpu.VMEM((total, part), F32)],
        ),
        compiler_params=params(),
        cost_estimate=cost(5 * FLOPS_US, 6e6),
        name="unpack_rows",
    )(table, own, got)


def unpack_heads(table, own, got, head, experts):
    half, chunk, width = own.shape

    def body(
        table_ref,
        own_ref,
        got_ref,
        key_ref,
        query_ref,
        output_router_ref,
        position_ref,
        rows,
    ):
        for place in range(half):
            start = pl.multiple_of(table_ref[place] * chunk, 8)
            rows[pl.ds(start, chunk), :] = own_ref[place].astype(F32)
            start = pl.multiple_of(table_ref[half + place] * chunk, 8)
            rows[pl.ds(start, chunk), :] = got_ref[place].astype(F32)
        key_ref[...] = rows[0:head, :]
        query_ref[...] = rows[LANES : LANES + head, :]
        output_router_ref[...] = rows[LANES + head : LANES + head + experts, :]
        position_ref[...] = rows[2 * LANES : 2 * LANES + head, :]

    one = jax.ShapeDtypeStruct((head, width), F32)
    few = jax.ShapeDtypeStruct((experts, width), F32)
    return pl.pallas_call(
        body,
        out_shape=(one, one, few, one),
        grid_spec=pltpu.PrefetchScalarGridSpec(
            num_scalar_prefetch=1,
            grid=(1,),
            in_specs=[whole(own), whole(got)],
            out_specs=tuple(fixed(kind.shape) for kind in (one, one, few, one)),
            scratch_shapes=[pltpu.VMEM((2 * half * chunk, width), F32)],
        ),
        compiler_params=params(),
        cost_estimate=cost(3 * FLOPS_US, 3e6),
        name="unpack_heads",
    )(table, own, got)


def unpack_small(me, norms, extra, head, share):
    def body(
        me_ref,
        norms_ref,
        extra_ref,
        gains_ref,
        biases_ref,
        content_ref,
        position_ref,
        counts_ref,
    ):
        start = pl.multiple_of(me_ref[0] * share, LANES)
        gains_ref[0:1, :] = norms_ref[0:1, pl.ds(start, share)]
        gains_ref[1:2, :] = norms_ref[2:3, pl.ds(start, share)]
        biases_ref[0:1, :] = norms_ref[1:2, pl.ds(start, share)]
        biases_ref[1:2, :] = norms_ref[3:4, pl.ds(start, share)]
        content_ref[...] = extra_ref[0:1, 0:head]
        position_ref[...] = extra_ref[1:2, 0:head]
        counts_ref[...] = extra_ref[2:4, 0:LANES].astype(jnp.int32)

    shapes = (
        ((2, share), F32),
        ((2, share), F32),
        ((1, head), F32),
        ((1, head), F32),
        ((2, LANES), jnp.int32),
    )
    return pl.pallas_call(
        body,
        out_shape=tuple(jax.ShapeDtypeStruct(shape, kind) for shape, kind in shapes),
        grid_spec=pltpu.PrefetchScalarGridSpec(
            num_scalar_prefetch=1,
            grid=(1,),
            in_specs=[whole(norms), whole(extra)],
            out_specs=tuple(fixed(shape) for shape, _ in shapes),
        ),
        cost_estimate=cost(2 * FLOPS_US, 1e6),
        name="unpack_small",
    )(me, norms, extra)


def on_device(
    inputs,
    memory,
    memory_positions,
    value_routes,
    output_routes,
    norm_gains,
    norm_biases,
    query_weight,
    key_weight,
    value_weight,
    value_router,
    output_router,
    output_weight,
    position_weight,
    content_bias,
    position_bias,
    up_weight,
    down_weight,
    cotangent,
):
    length, width = inputs.shape[1:]
    mem_count = memory.shape[1]
    keys = mem_count + length
    head = query_weight.shape[1]
    experts = value_router.shape[1]
    pos_width = position_weight.shape[0]
    picks = value_routes.shape[3]
    t_index = lax.axis_index("tensor")
    me = t_index.reshape(1).astype(jnp.int32)
    t_bits = axis_bits("tensor")
    t_order = relative_order(t_bits)
    t_table = chunk_table(t_bits, "tensor")
    t_count = lax.axis_size("tensor")
    core_bit, chip_bit = t_bits
    all_bits = axis_bits("dp")
    first_bits = all_bits[:SPLITS]
    second_bits = [first_bits[1], first_bits[0]] + first_bits[2:]
    first_table = chunk_table(first_bits, "dp")
    second_table = chunk_table(second_bits, "dp")

    def bits_of(name):
        return second_bits if name in SECOND else first_bits

    def table_of(name):
        return second_table if name in SECOND else first_table

    tokens = inputs.reshape(length, width)
    upstream = cotangent.reshape(length, width)
    past = memory.reshape(mem_count, width)
    key_t = key_weight.T
    value_t = value_weight.T
    value_router_t = value_router.T
    query_t = query_weight.T
    output_router_t = output_router.T
    position_t = position_weight.T

    far_weight = swap(output_weight, "tensor", chip_bit)
    coarse = trig_tables(-2.0 * mem_count, (2 * mem_count + length) // FINE, float(FINE), pos_width)
    fine = trig_tables(0.0, FINE, 1.0, pos_width)
    (
        normed,
        key_cat,
        values,
        gates,
        content_query,
        bias_query,
        counts,
        probs,
        attended_own,
    ) = front(
        past,
        tokens,
        norm_gains,
        norm_biases,
        key_t,
        value_t,
        value_router_t,
        query_t,
        output_router_t,
        position_t,
        content_bias.reshape(1, head),
        position_bias.reshape(1, head),
        value_routes.reshape(keys, picks).T,
        output_routes.reshape(length, picks).T,
        memory_positions,
        coarse,
        fine,
    )

    totals = {}
    v = {}
    token = [attended_own]

    def tie(value):
        return after(value, *token)

    def core_sum(held, got):
        half = held.shape[0] // 2
        return add_pieces(held[:1], got[:1]), add_pieces(held[1:half], got[1:])

    def for_core(held):
        return swap(held[held.shape[0] // 2 :], "tensor", core_bit)

    far_attended = swap(attended_own, "tensor", chip_bit)
    near_attended = swap(attended_own, "tensor", core_bit)
    far_weight = after(far_weight, attended_own)
    near_weight = swap(after(output_weight, attended_own), "tensor", core_bit)
    across_weight = swap(far_weight, "tensor", core_bit)
    across_attended = swap(far_attended, "tensor", core_bit)
    attended = [attended_own, far_attended, near_attended, across_attended]
    weights = [output_weight, far_weight, near_weight, across_weight]

    def feed_forward():
        (
            v["resid"],
            v["grad_normed"],
            v["share"],
            down_keep,
            down_send,
            up_keep,
            up_send,
        ) = forward_ffn(
            tie(t_table),
            table_of("down"),
            table_of("up"),
            attended,
            weights,
            tokens,
            upstream,
            up_weight,
            down_weight,
            norm_gains,
            norm_biases,
            experts,
        )
        v["grad_normed_got"] = for_core(v["grad_normed"])
        totals["F"] = DpSum(
            [(down_keep, down_send, bits_of("down")), (up_keep, up_send, bits_of("up"))]
        )
        return down_keep

    def grad_normed_add():
        v["left"], far = core_sum(v["grad_normed"], tie(v["grad_normed_got"]))
        v["right"] = swap(far, "tensor", chip_bit)
        return far

    def share_core():
        v["share"] = tie(v["share"])
        v["share_got"] = for_core(v["share"])
        return None

    def share_add():
        v["share_left"], far = core_sum(v["share"], tie(v["share_got"]))
        v["share_right"] = swap(far, "tensor", chip_bit)
        return far

    def second_norm():
        v["grad_resid"], low_own, packed, v["sums_two"] = second_norm_back(
            tie(me),
            attended,
            weights,
            v["left"],
            v["right"],
            v["resid"],
            upstream,
            norm_gains,
            experts,
        )
        arrived = [None] * t_count
        for place, distance in enumerate(t_order):
            piece = packed[place : place + 1]
            arrived[distance] = piece if distance == 0 else swap(piece, "tensor", distance)
        v["arrived"] = arrived
        v["low"] = [
            low_own,
            swap(low_own, "tensor", chip_bit),
            swap(low_own, "tensor", core_bit),
        ]
        return low_own

    def low_across():
        far = tie(v["low"][1])
        v["low"][1] = far
        v["low"].append(swap(far, "tensor", core_bit))
        return far

    def start_pair():
        if "value_part" in v and "out_part" in v:
            totals["W"] = DpSum([v["value_part"], v["out_part"]])

    def value_grads():
        v["grad_values"], v["logits"], keep, send = value_back(
            tie(me),
            table_of("value"),
            v["arrived"],
            probs,
            normed,
            gates,
            value_t,
            head,
            experts,
        )
        v["value_part"] = (keep, send, bits_of("value"))
        start_pair()
        return v["grad_values"]

    def attention():
        v["grad_keys"], v["grad_query"], keep, send, v["bias_sums"] = attend_back(
            tie(me),
            table_of("late"),
            v["arrived"],
            probs,
            key_cat,
            values,
            content_query,
            bias_query,
            coarse,
            fine,
            position_t,
            normed,
        )
        totals["L"] = DpSum([(keep, send, bits_of("late"))])
        return v["bias_sums"]

    def output_weight_grad():
        keep, send = output_grad(
            tie(t_table), table_of("out"), attended_own, v["low"], head, experts
        )
        v["out_part"] = (keep, send, bits_of("out"))
        start_pair()
        return send

    def projections():
        v["grad_current"], v["sums_one"], v["extra"] = project_back(
            tie(t_table),
            v["grad_keys"],
            v["grad_values"],
            gates,
            v["logits"],
            v["grad_query"],
            past,
            tokens,
            key_t,
            value_t,
            value_router_t,
            query_t,
            output_router_t,
            v["bias_sums"],
            counts,
        )
        v["grad_current_got"] = for_core(v["grad_current"])
        return v["extra"]

    def grad_current_add():
        v["left"], far = core_sum(v["grad_current"], tie(v["grad_current_got"]))
        v["right"] = swap(far, "tensor", chip_bit)
        return far

    def first_norm():
        own = first_norm_back(
            tie(me), v["left"], v["right"], tokens, v["grad_resid"], norm_gains
        )
        v["grad_inputs"] = [
            own,
            swap(own, "tensor", chip_bit),
            swap(own, "tensor", core_bit),
        ]
        return own

    def rows_across(name):
        far = tie(v[name][1])
        v[name][1] = far
        v[name].append(swap(far, "tensor", core_bit))
        return far

    def rows_placed(name):
        v[name] = place_rows(tie(t_table), v[name])
        return v[name]

    def output_rows():
        own = (
            v["resid"][None]
            + v["share_left"].astype(F32)
            + tie(v["share_right"]).astype(F32)
        ).astype(BF16)
        v["output"] = [
            own,
            swap(own, "tensor", chip_bit),
            swap(own, "tensor", core_bit),
        ]
        return own

    def small_sum(stage):
        if stage == 0:
            total = tie(v["sums_one"]) + v["sums_two"]
            v["small_got"] = swap(total, "tensor", core_bit)
        else:
            total = v["small"] + tie(v["small_got"])
            if stage == 1:
                v["small_got"] = swap(total, "tensor", chip_bit)
            elif stage < 2 + len(all_bits):
                if stage == 2:
                    total = jnp.concatenate([total, v["extra"]], axis=0)
                v["small_got"] = swap(total, "dp", all_bits[stage - 2])
        v["small"] = total
        return total

    def small_placed():
        for stage in range(2 + len(axis_bits("dp")[:SPLITS]), 3 + len(all_bits)):
            small_sum(stage)
        small = v["small"]
        v["small_out"] = unpack_small(
            me, small[0:8], small[8:], head, width // t_count
        )
        return v["small_out"][0]

    def sum_placed(name, rows, total, part, more=0):
        total = totals[total]
        v[name] = unpack_rows(
            tie(table_of(name)), total.keep[part], total.got[part], rows, more
        )
        return v[name][0]

    def late_placed():
        total = totals["L"]
        v["late"] = unpack_heads(
            tie(table_of("late")), total.keep[0], total.got[0], head, experts
        )
        return v["late"][2]

    tasks = {
        "ffn": feed_forward,
        "sh": share_core,
        "sha": share_add,
        "oc": lambda: rows_across("output"),
        "gi": lambda: rows_across("grad_inputs"),
        "pro": lambda: rows_placed("output"),
        "pri": lambda: rows_placed("grad_inputs"),
        "gna": grad_normed_add,
        "snb": second_norm,
        "low": low_across,
        "vb": value_grads,
        "ab": attention,
        "og": output_weight_grad,
        "pb": projections,
        "gca": grad_current_add,
        "fnb": first_norm,
        "orow": output_rows,
        "nu": small_placed,
        "Du": lambda: sum_placed("down", down_weight.shape[0], "F", 0),
        "Uu": lambda: sum_placed("up", up_weight.shape[0], "F", 1),
        "Vu": lambda: sum_placed("value", experts * head, "W", 0, experts),
        "Ou": lambda: sum_placed("out", experts * head, "W", 1),
        "Lu": late_placed,
    }
    for stage in range(5):
        tasks["n" + str(stage)] = functools.partial(small_sum, stage)
    for name in ORDER:
        if name in tasks:
            done = tasks[name]()
        else:
            done = totals[name[0]].step(*token)
        if done is not None:
            token = list(done) if isinstance(done, list) else [done]

    grad_gains, grad_biases, grad_content, grad_position, expert_counts = v["small_out"]
    grad_key_t, grad_query_t, grad_output_router, grad_position_t = v["late"]
    grad_value_t, grad_value_router = v["value"]
    return (
        v["output"].reshape(1, length, width),
        v["grad_inputs"].reshape(1, length, width),
        grad_gains,
        grad_biases,
        grad_query_t.T,
        grad_key_t.T,
        grad_value_t.T,
        grad_value_router.T,
        grad_output_router.T,
        v["out"][0],
        grad_position_t.T,
        grad_content.reshape(head),
        grad_position.reshape(head),
        v["up"][0],
        v["down"][0],
        expert_counts[:, head : head + experts],
    )


def solution(mesh):
    placed = (
        P("dp", None, None),
        P("dp", None, None),
        P("dp", None),
        P("dp", None, "tensor", None),
        P("dp", None, "tensor", None),
        P(),
        P(),
        P(None, "tensor"),
        P(None, "tensor"),
        P(None, "tensor"),
        P(None, "tensor"),
        P(None, "tensor"),
        P("tensor", None),
        P(None, "tensor"),
        P("tensor"),
        P("tensor"),
        P(None, "tensor"),
        P("tensor", None),
        P("dp", None, None),
    )
    return jax.shard_map(
        on_device,
        mesh=mesh,
        in_specs=placed,
        out_specs=(
            P("dp", None, None),
            P("dp", None, None),
            P(None, "tensor"),
            P(None, "tensor"),
            P(None, "tensor"),
            P(None, "tensor"),
            P(None, "tensor"),
            P(None, "tensor"),
            P(None, "tensor"),
            P("tensor", None),
            P(None, "tensor"),
            P("tensor"),
            P("tensor"),
            P(None, "tensor"),
            P("tensor", None),
            P(None, "tensor"),
        ),
        check_vma=False,
    )
```

```python
import functools
import math

import jax
import jax.numpy as jnp
from jax import lax
from jax.experimental import pallas as pl
from jax.experimental.pallas import tpu as pltpu
from jax.sharding import PartitionSpec as P

NORM_EPSILON = 1e-05
GELU_SCALE = 0.7978845608028654
GELU_CUBIC = 0.044715
LANES = 128
ROWS = 256
FINE = 32
SPLITS = 3
SECOND = ("up","out",)
ORDER = (
    "ffn", "gna", "sh", "sha", "snb", "F1", "orow", "vb", "F2", "low",
    "ab", "oc", "og", "F3", "pro", "L1", "pb", "n0", "W1", "n1",
    "L2", "F4", "n2", "W2", "L3", "gca", "n3", "F5", "L4", "n4",
    "W3", "fnb", "nu", "L5", "W4", "Du", "gi", "Lu", "pri", "W5",
    "Uu", "Vu", "Ou",
)
VMEM = 56 * 1024 * 1024
FLOPS_US = 1.1e9
SHRINK = 1000
BF16 = jnp.bfloat16
F32 = jnp.float32


def dot_first(left, right):
    return lax.dot_general(left, right, (((0,), (0,)), ((), ())), preferred_element_type=F32)


def dot_last(left, right):
    return lax.dot_general(left, right, (((1,), (1,)), ((), ())), preferred_element_type=F32)


def dot_plain(left, right):
    return jnp.dot(left, right, preferred_element_type=F32)


def gelu_parts(values):
    square = values * values
    tangent = jnp.tanh(GELU_SCALE * (values + GELU_CUBIC * values * square))
    half = 0.5 * (1.0 + tangent)
    slope = half + 0.5 * values * (1.0 - tangent * tangent) * (
        GELU_SCALE * (1.0 + 3.0 * GELU_CUBIC * square)
    )
    return (values * half, slope)


def unit_rows(values):
    average = jnp.mean(values, axis=-1, keepdims=True)
    centered = values - average
    spread = jnp.mean(centered * centered, axis=-1, keepdims=True)
    inverse = lax.rsqrt(spread + NORM_EPSILON)
    return (centered * inverse, inverse)


def norm_backward(upstream, unit, inverse, gain):
    grad_unit = upstream * gain
    return inverse * (
        grad_unit
        - jnp.mean(grad_unit, axis=-1, keepdims=True)
        - unit * jnp.mean(grad_unit * unit, axis=-1, keepdims=True)
    )


def lane_index(rows):
    return lax.broadcasted_iota(jnp.int32, (rows, LANES), 1)


def whole(array):
    rank = array.ndim
    return pl.BlockSpec(
        array.shape, lambda *_: (0,) * rank, pipeline_mode=pl.Buffered(1)
    )


def fixed(shape):
    return pl.BlockSpec(shape, lambda *_: (0,) * len(shape))


def params():
    return pltpu.CompilerParams(vmem_limit_bytes=VMEM)


def cost(flops, moved, special=0):
    return pl.CostEstimate(flops=int(flops) // SHRINK, bytes_accessed=int(moved) // SHRINK, transcendentals=0)


def axis_bits(name):
    count = lax.axis_size(name)
    bits = []
    bit = 1
    while bit < count:
        bits.append(bit)
        bit = bit * 2
    return bits


def relative_order(bits):
    count = 2 ** len(bits)
    order = []
    for place in range(count):
        value = 0
        for depth, bit in enumerate(bits):
            if place & (count >> (depth + 1)):
                value = value | bit
        order.append(value)
    return order


def swap(piece, name, bit):
    return lax.ppermute(piece, name, [(i, i ^ bit) for i in range(lax.axis_size(name))])


def add_pieces(left, right):
    return (left.astype(F32) + right.astype(F32)).astype(BF16)


def after(value, *others):
    return lax.optimization_barrier((value,) + others)[0]


class DpSum:
    def __init__(self, parts):
        self.keep = [keep for keep, _, _ in parts]
        self.send = [send for _, send, _ in parts]
        self.bits = [bits for _, _, bits in parts]
        self.stages = len(self.bits[0])
        self.more = [bit for bit in axis_bits("dp") if bit not in self.bits[0]]
        self.folded = 0
        self.depth = 0
        self.move(self.send, 0)

    def move(self, pieces, stage):
        bits = [bits[stage] for bits in self.bits]
        if len(pieces) > 1 and stage == self.stages - 1 and len(set(bits)) == 1:
            got = swap(jnp.concatenate(pieces, axis=0), "dp", bits[0])
            self.got = [got]
        else:
            self.got = [swap(piece, "dp", bit) for piece, bit in zip(pieces, bits)]

    def take(self, others):
        tied = lax.optimization_barrier(tuple(self.got) + tuple(others))
        got = tied[0 : len(self.got)]
        if len(got) < len(self.keep):
            got = [got[0][i : i + 1] for i in range(len(self.keep))]
        return got

    def step(self, *others):
        got = self.take(others)
        if self.folded < self.stages:
            self.folded = self.folded + 1
            if self.folded < self.stages:
                half = self.keep[0].shape[0] // 2
                self.send = [add_pieces(k[half:], g[half:]) for k, g in zip(self.keep, got)]
                self.keep = [add_pieces(k[:half], g[:half]) for k, g in zip(self.keep, got)]
                self.move(self.send, self.folded)
                return self.send
            self.keep = [add_pieces(k, g) for k, g in zip(self.keep, got)]
            for bit in self.more:
                self.keep = [add_pieces(k, swap(k, "dp", bit)) for k in self.keep]
            self.depth = self.stages
        else:
            self.keep = [jnp.concatenate([k, g], axis=0) for k, g in zip(self.keep, got)]
        self.depth = self.depth - 1
        self.move(self.keep, self.depth)
        return self.keep


def chunk_table(bits, name):
    place = jnp.bitwise_and(lax.axis_index(name), 2 ** len(bits) - 1)
    return jnp.bitwise_xor(jnp.array(relative_order(bits), jnp.int32), place)

def angles(place, coarse_ref, fine_ref):
    count = place.shape[1]
    slots = coarse_ref.shape[0] // 2
    freq = coarse_ref.shape[1] // 2
    leading = place // FINE
    trailing = lax.rem(place, FINE)
    coarse_rows = lax.broadcasted_iota(jnp.int32, (2 * slots, count), 0)
    fine_rows = lax.broadcasted_iota(jnp.int32, (2 * FINE, count), 0)
    coarse_hit = ((coarse_rows == leading) | (coarse_rows == leading + slots)).astype(BF16)
    fine_hit = ((fine_rows == trailing) | (fine_rows == trailing + FINE)).astype(BF16)
    big = dot_first(coarse_hit, coarse_ref[...])
    small = dot_first(fine_hit, fine_ref[...])
    cosine = big[:, 0:freq] * small[:, 0:freq] - big[:, freq:] * small[:, freq:]
    sine = big[:, freq:] * small[:, 0:freq] + big[:, 0:freq] * small[:, freq:]
    return cosine, sine


def trig_tables(first, count, step, pos_width):
    freq = pos_width // 2
    omega = jnp.exp(jnp.arange(freq, dtype=F32) * (-2.0 * math.log(10000.0) / pos_width))
    angle = (jnp.arange(count, dtype=F32) * step + first)[:, None] * omega
    table = jnp.concatenate([jnp.cos(angle), jnp.sin(angle)], axis=1)
    lead = lax.reduce_precision(table, 8, 7)
    return jnp.concatenate([lead, table - lead], axis=0).astype(BF16)


def fill_weights(head, experts, key_ref, router_ref, value_ref, scratch):
    scratch[0:head, :] = key_ref[...]
    scratch[head : head + experts, :] = router_ref[...]
    for e in range(experts):
        start = LANES * (e + 1)
        scratch[start : start + head, :] = value_ref[e * head : (e + 1) * head, :]


def front_body(
    head,
    experts,
    length,
    shift,
    memory_ref,
    inputs_ref,
    gains_ref,
    biases_ref,
    key_ref,
    value_ref,
    value_router_ref,
    query_ref,
    output_router_ref,
    position_ref,
    content_bias_ref,
    position_bias_ref,
    value_route_ref,
    output_route_ref,
    place_ref,
    coarse_ref,
    fine_ref,
    normed_ref,
    key_cat_ref,
    values_ref,
    gate_ref,
    content_query_ref,
    bias_query_ref,
    count_ref,
    probs_ref,
    attended_ref,
    weight_scratch,
    bias_scratch,
    key_scratch,
    value_scratch,
    query_scratch,
):
    step = pl.program_id(0)
    span = memory_ref.shape[0]
    keys = key_scratch.shape[0]
    mem_steps = (keys - length) // span
    split = LANES * (1 + experts)
    freq = coarse_ref.shape[1] // 2

    @pl.when(step == 0)
    def _():
        weight_scratch[...] = jnp.zeros_like(weight_scratch)
        bias_scratch[...] = jnp.zeros_like(bias_scratch)
        count_ref[...] = jnp.zeros_like(count_ref)
        fill_weights(head, experts, key_ref, value_router_ref, value_ref, weight_scratch)
        weight_scratch[split : split + head, :] = query_ref[...]
        weight_scratch[split + head : split + head + experts, :] = output_router_ref[...]
        bias_scratch[0:1, 0:head] = content_bias_ref[...]
        bias_scratch[1:2, 0:head] = position_bias_ref[...]

    old = step < mem_steps
    rows = jnp.where(old, memory_ref[...], inputs_ref[...]).astype(F32)
    unit, _ = unit_rows(rows)
    normed = (unit * gains_ref[0:1, :] + biases_ref[0:1, :]).astype(BF16)
    normed_ref[...] = normed
    product = dot_last(normed, weight_scratch[0:split, :])
    lane = lane_index(span)
    first = product[:, 0:LANES]
    key_piece = jnp.where(lane < head, first, 0.0).astype(BF16)

    def picks(route):
        row = lax.broadcasted_iota(jnp.int32, (LANES, span), 0) - head
        hit = (route[0:1, :] == row).astype(F32) + (route[1:2, :] == row).astype(F32)
        return hit.T

    chosen = picks(value_route_ref[...])
    gate = jax.nn.sigmoid(first) * chosen
    gate_ref[...] = gate.T[head : head + 8, :]
    total = jnp.zeros((span, LANES), F32)
    for e in range(experts):
        start = LANES * (e + 1)
        total = total + gate[:, head + e : head + e + 1] * product[:, start : start + LANES]
    values = total.astype(BF16)
    values_ref[...] = values
    current_place = lax.broadcasted_iota(jnp.int32, (1, span), 1) + (step - mem_steps) * span
    cosine, sine = angles(
        jnp.where(old, place_ref[...], current_place) + shift, coarse_ref, fine_ref
    )
    cos_low = cosine.astype(BF16)
    sin_low = sine.astype(BF16)
    key_cat_ref[:, 0:LANES] = key_piece
    key_cat_ref[:, LANES : LANES + freq] = cos_low
    key_cat_ref[:, LANES + freq :] = sin_low
    base = pl.multiple_of(step * span, span)
    key_scratch[pl.ds(base, span), 0:LANES] = key_piece
    key_scratch[pl.ds(base, span), LANES : LANES + freq] = cos_low
    key_scratch[pl.ds(base, span), LANES + freq :] = sin_low
    value_scratch[pl.ds(base, span), :] = values

    def variant(place):
        def run():
            last = dot_last(normed, weight_scratch[split:, :])
            query = jnp.where(lane < head, last, 0.0)
            content = (query + bias_scratch[0:1, :]).astype(BF16)
            biased = (query + bias_scratch[1:2, :]).astype(BF16)
            content_query_ref[...] = content
            bias_query_ref[...] = biased
            out_chosen = picks(output_route_ref[...])
            out_gate = jax.nn.sigmoid(last) * out_chosen
            count_ref[0:1, :] += jnp.sum(chosen, axis=0, keepdims=True)
            count_ref[1:2, :] += jnp.sum(out_chosen, axis=0, keepdims=True)
            rest = out_gate - out_gate.astype(BF16).astype(F32)
            extra = out_gate + pltpu.roll(rest, experts, 1)
            relative = dot_plain(biased[:, 0:head], position_ref[...])
            rel_sin = relative[:, 0:freq]
            rel_cos = relative[:, freq:]
            query_scratch[:, 0:LANES] = content
            query_scratch[:, LANES : LANES + freq] = (rel_sin * sine + rel_cos * cosine).astype(
                BF16
            )
            query_scratch[:, LANES + freq :] = (rel_cos * sine - rel_sin * cosine).astype(BF16)
            factor = head ** (-0.5) * math.log2(math.e)
            row = lax.broadcasted_iota(jnp.int32, (ROWS, ROWS), 0)
            col = lax.broadcasted_iota(jnp.int32, (ROWS, ROWS), 1)
            for part in range(span // ROWS):
                piece = slice(part * ROWS, (part + 1) * ROWS)
                seen = keys - length + place * span + (part + 1) * ROWS
                scores = dot_last(query_scratch[piece, :], key_scratch[0:seen, :])
                body = scores[:, 0 : seen - ROWS]
                tail = jnp.where(col <= row, scores[:, seen - ROWS :], -jnp.inf)
                top = factor * jnp.maximum(
                    jnp.max(body, axis=1, keepdims=True), jnp.max(tail, axis=1, keepdims=True)
                )
                body = jnp.exp2(body * factor - top)
                tail = jnp.exp2(tail * factor - top)
                share = 1.0 / (
                    jnp.sum(body, axis=1, keepdims=True) + jnp.sum(tail, axis=1, keepdims=True)
                )
                body = (body * share).astype(BF16)
                tail = (tail * share).astype(BF16)
                probs_ref[piece, 0 : seen - ROWS] = body
                probs_ref[piece, seen - ROWS : seen] = tail
                if seen < keys:
                    probs_ref[piece, seen:] = jnp.zeros((ROWS, keys - seen), BF16)
                result = dot_plain(body, value_scratch[0 : seen - ROWS, :]) + dot_plain(
                    tail, value_scratch[seen - ROWS : seen, :]
                )
                attended_ref[piece, :] = jnp.where(
                    lane[piece, :] < head, result, extra[piece, :]
                ).astype(BF16)

        return run

    for place in range(length // span):
        pl.when(step == mem_steps + place)(variant(place))


def front(
    memory,
    inputs,
    gains,
    biases,
    key_weight,
    value_weight,
    value_router,
    query_weight,
    output_router,
    position_weight,
    content_bias,
    position_bias,
    value_routes,
    output_routes,
    places,
    coarse,
    fine,
):
    mem_count, width = memory.shape
    length = inputs.shape[0]
    head = key_weight.shape[0]
    experts = value_router.shape[0]
    pos_width = coarse.shape[1]
    keys = mem_count + length
    span = 2 * ROWS
    mem_steps = mem_count // span
    old = lambda i: (jnp.minimum(i, mem_steps - 1), 0)
    new = lambda i: (jnp.maximum(i - mem_steps, 0), 0)
    every = lambda i: (i, 0)
    row = lambda size, index: pl.BlockSpec((span, size), index)
    turned = lambda index: (lambda i: index(i)[::-1])
    return pl.pallas_call(
        functools.partial(front_body, head, experts, length, 2 * mem_count),
        out_shape=(
            jax.ShapeDtypeStruct((keys, width), BF16),
            jax.ShapeDtypeStruct((keys, LANES + pos_width), BF16),
            jax.ShapeDtypeStruct((keys, LANES), BF16),
            jax.ShapeDtypeStruct((8, keys), F32),
            jax.ShapeDtypeStruct((length, LANES), BF16),
            jax.ShapeDtypeStruct((length, LANES), BF16),
            jax.ShapeDtypeStruct((8, LANES), F32),
            jax.ShapeDtypeStruct((length, keys), BF16),
            jax.ShapeDtypeStruct((length, LANES), BF16),
        ),
        grid=(keys // span,),
        in_specs=[
            row(width, old),
            row(width, new),
            whole(gains),
            whole(biases),
            whole(key_weight),
            whole(value_weight),
            whole(value_router),
            whole(query_weight),
            whole(output_router),
            whole(position_weight),
            whole(content_bias),
            whole(position_bias),
            pl.BlockSpec((value_routes.shape[0], span), turned(every)),
            pl.BlockSpec((output_routes.shape[0], span), turned(new)),
            pl.BlockSpec((1, span), turned(old)),
            whole(coarse),
            whole(fine),
        ],
        out_specs=(
            row(width, every),
            row(LANES + pos_width, every),
            row(LANES, every),
            pl.BlockSpec((8, span), turned(every)),
            row(LANES, new),
            row(LANES, new),
            fixed((8, LANES)),
            row(keys, new),
            row(LANES, new),
        ),
        scratch_shapes=[
            pltpu.VMEM((LANES * (2 + experts), width), BF16),
            pltpu.VMEM((8, LANES), F32),
            pltpu.VMEM((keys, LANES + pos_width), BF16),
            pltpu.VMEM((keys, LANES), BF16),
            pltpu.VMEM((span, LANES + pos_width), BF16),
        ],
        compiler_params=params(),
        cost_estimate=cost(30 * FLOPS_US, 30e6),
        name="front",
    )(
        memory,
        inputs,
        gains,
        biases,
        key_weight,
        value_weight,
        value_router,
        query_weight,
        output_router,
        position_weight,
        content_bias,
        position_bias,
        value_routes,
        output_routes,
        places,
        coarse,
        fine,
    )


def attend_back_body(head, heads, shift, me_ref, table_ref, *refs):
    grad_refs = refs[0:heads]
    (
        probs_ref,
        attended_ref,
        key_cat_ref,
        values_ref,
        content_ref,
        bias_ref,
        coarse_ref,
        fine_ref,
        position_ref,
        normed_ref,
        grad_keys_ref,
        grad_query_ref,
        keep_ref,
        send_ref,
        sums_ref,
        position_scratch,
        relative_scratch,
        grad_scratch,
        keys_scratch,
        weight_scratch,
        key_cat_scratch,
        normed_scratch,
        copy_sems,
    ) = refs[heads:]
    step = pl.program_id(0)
    key_copy = pltpu.make_async_copy(key_cat_ref, key_cat_scratch, copy_sems.at[0])
    normed_copy = pltpu.make_async_copy(normed_ref, normed_scratch, copy_sems.at[1])
    keys = key_cat_scratch.shape[0]
    length = pl.num_programs(0) * ROWS
    freq = coarse_ref.shape[1] // 2
    scale = head ** (-0.5)

    @pl.when(step == 0)
    def _():
        key_copy.start()
        normed_copy.start()
        keys_scratch[...] = jnp.zeros_like(keys_scratch)
        weight_scratch[...] = jnp.zeros_like(weight_scratch)
        sums_ref[...] = jnp.zeros_like(sums_ref)
        position_scratch[...] = jnp.zeros_like(position_scratch)
        position_scratch[0:head, :] = position_ref[...]
        for distance, grad_ref in enumerate(grad_refs):
            grad_scratch[jnp.bitwise_xor(me_ref[0], distance)] = grad_ref[0]

    lane = lane_index(ROWS)
    packed = grad_scratch[step]
    upstream = jnp.where(lane < head, packed, jnp.zeros_like(packed))
    place = lax.broadcasted_iota(jnp.int32, (1, ROWS), 1) + step * ROWS + shift
    cosine, sine = angles(place, coarse_ref, fine_ref)

    def variant(block):
        def run():
            seen = keys - length_static + (block + 1) * ROWS
            weights_low = probs_ref[:, 0:seen]
            weights = weights_low.astype(F32)
            grad_weights = dot_last(upstream, values_ref[0:seen, :])
            inner = jnp.sum(
                upstream.astype(F32) * attended_ref[...].astype(F32), axis=1, keepdims=True
            )
            grad_scores = (weights * (grad_weights - inner)).astype(BF16)
            keys_scratch[:, 0:seen] += dot_first(content_ref[...], grad_scores) * scale
            if block == 0:
                key_copy.wait()
                normed_copy.wait()
            grad_query = dot_plain(grad_scores, key_cat_scratch[0:seen, :]) * scale
            grad_content = grad_query[:, 0:LANES]
            grad_sin = grad_query[:, LANES : LANES + freq]
            grad_cos = grad_query[:, LANES + freq :]
            relative_scratch[:, 0:freq] = (grad_sin * sine - grad_cos * cosine).astype(BF16)
            relative_scratch[:, freq:] = (grad_sin * cosine + grad_cos * sine).astype(BF16)
            relative = relative_scratch[...]
            grad_bias = dot_last(relative, position_scratch[...])
            weight_scratch[2 * LANES :, :] += dot_first(bias_ref[...], relative)
            sums_ref[0:1, :] += jnp.sum(grad_content, axis=0, keepdims=True)
            sums_ref[1:2, :] += jnp.sum(grad_bias, axis=0, keepdims=True)
            both = jnp.where(lane < head, (grad_content + grad_bias).astype(BF16), packed)
            grad_query_ref[...] = both
            weight_scratch[LANES : 2 * LANES, :] += dot_first(
                both, normed_scratch[seen - ROWS : seen, :]
            )

        return run

    length_static = heads * ROWS
    for block in range(length_static // ROWS):
        pl.when(step == block)(variant(block))

    @pl.when(step == pl.num_programs(0) - 1)
    def _():
        grad_keys = keys_scratch[...].astype(BF16)
        grad_keys_ref[...] = grad_keys
        weight_scratch[0:LANES, :] = dot_plain(grad_keys, normed_scratch[...])
        half, chunk, _ = keep_ref.shape
        for place in range(half):
            start = pl.multiple_of(table_ref[place] * chunk, 8)
            keep_ref[place] = weight_scratch[pl.ds(start, chunk), :].astype(BF16)
            start = pl.multiple_of(table_ref[half + place] * chunk, 8)
            send_ref[place] = weight_scratch[pl.ds(start, chunk), :].astype(BF16)


def attend_back(
    me,
    table,
    grads,
    probs,
    attended,
    key_cat,
    values,
    content_query,
    bias_query,
    coarse,
    fine,
    position_weight,
    normed,
):
    length, keys = probs.shape
    head, pos_width = position_weight.shape
    width = normed.shape[1]
    count = table.shape[0]
    half = jax.ShapeDtypeStruct((count // 2, 3 * LANES // count, width), BF16)
    heads = len(grads)
    every = lambda i, *_: (i, 0)
    row = lambda size: pl.BlockSpec((ROWS, size), every)
    return pl.pallas_call(
        functools.partial(attend_back_body, head, heads, 2 * (keys - length)),
        out_shape=(
            jax.ShapeDtypeStruct((LANES, keys), BF16),
            jax.ShapeDtypeStruct((length, LANES), BF16),
            half,
            half,
            jax.ShapeDtypeStruct((8, LANES), F32),
        ),
        grid_spec=pltpu.PrefetchScalarGridSpec(
            num_scalar_prefetch=2,
            grid=(length // ROWS,),
            in_specs=[whole(grad) for grad in grads]
            + [
                row(keys),
                row(LANES),
                pl.BlockSpec(memory_space=pl.ANY),
                whole(values),
                row(LANES),
                row(LANES),
                whole(coarse),
                whole(fine),
                whole(position_weight),
                pl.BlockSpec(memory_space=pl.ANY),
            ],
            out_specs=(
                fixed((LANES, keys)),
                row(LANES),
                fixed(half.shape),
                fixed(half.shape),
                fixed((8, LANES)),
            ),
            scratch_shapes=[
                pltpu.VMEM((LANES, pos_width), BF16),
                pltpu.VMEM((ROWS, pos_width), BF16),
                pltpu.VMEM((heads, ROWS, LANES), BF16),
                pltpu.VMEM((LANES, keys), F32),
                pltpu.VMEM((3 * LANES, width), F32),
                pltpu.VMEM(key_cat.shape, BF16),
                pltpu.VMEM(normed.shape, BF16),
                pltpu.SemaphoreType.DMA((2,)),
            ],
        ),
        compiler_params=params(),
        cost_estimate=cost(17 * FLOPS_US, 25e6),
        name="attend_back",
    )(
        me,
        table,
        *grads,
        probs,
        attended,
        key_cat,
        values,
        content_query,
        bias_query,
        coarse,
        fine,
        position_weight,
        normed,
    )


def value_back_body(head, experts, heads, me_ref, table_ref, *refs):
    grad_refs = refs[0:heads]
    (
        probs_ref,
        normed_ref,
        gate_ref,
        weight_ref,
        grad_values_ref,
        logit_ref,
        keep_ref,
        send_ref,
        grad_scratch,
        packed_scratch,
        acc,
    ) = refs[heads:]
    step = pl.program_id(0)

    @pl.when(step == 0)
    def _():
        lane = lane_index(ROWS)
        for distance, grad_ref in enumerate(grad_refs):
            start = pl.multiple_of(jnp.bitwise_xor(me_ref[0], distance) * ROWS, ROWS)
            piece = grad_ref[0]
            grad_scratch[pl.ds(start, ROWS), :] = jnp.where(
                lane < head, piece, jnp.zeros_like(piece)
            )
        packed_scratch[...] = jnp.zeros_like(packed_scratch)
        acc[...] = jnp.zeros_like(acc)

    grad_values = dot_first(grad_scratch[...], probs_ref[...])
    grad_values_ref[...] = grad_values
    expert_values = dot_last(weight_ref[...], normed_ref[...])
    logits = []
    for e in range(experts):
        piece = slice(e * head, (e + 1) * head)
        gate = gate_ref[e : e + 1, :]
        packed_scratch[piece, :] = (gate * grad_values[0:head, :]).astype(BF16)
        inner = jnp.sum(expert_values[piece, :] * grad_values[0:head, :], axis=0, keepdims=True)
        logits.append(inner * gate * (1.0 - gate))
    logits.append(jnp.zeros((8 - experts, logits[0].shape[1]), F32))
    logit = jnp.concatenate(logits, axis=0)
    logit_ref[...] = logit
    packed_scratch[experts * head : experts * head + 8, :] = logit.astype(BF16)
    acc[...] += dot_plain(packed_scratch[...], normed_ref[...])

    @pl.when(step == pl.num_programs(0) - 1)
    def _():
        half, chunk, _ = keep_ref.shape
        for place in range(half):
            start = pl.multiple_of(table_ref[place] * chunk, 8)
            keep_ref[place] = acc[pl.ds(start, chunk), :].astype(BF16)
            start = pl.multiple_of(table_ref[half + place] * chunk, 8)
            send_ref[place] = acc[pl.ds(start, chunk), :].astype(BF16)


def value_back(me, table, grads, probs, normed, gates, weight, head, experts):
    heads = len(grads)
    length, keys = probs.shape
    width = normed.shape[1]
    count = table.shape[0]
    span = 2 * ROWS
    rows = experts * head + 8
    rows = rows + -rows % (8 * count)
    half = jax.ShapeDtypeStruct((count // 2, rows // count, width), BF16)
    return pl.pallas_call(
        functools.partial(value_back_body, head, experts, heads),
        out_shape=(
            jax.ShapeDtypeStruct((LANES, keys), F32),
            jax.ShapeDtypeStruct((8, keys), F32),
            half,
            half,
        ),
        grid_spec=pltpu.PrefetchScalarGridSpec(
            num_scalar_prefetch=2,
            grid=(keys // span,),
            in_specs=[whole(grad) for grad in grads]
            + [
                pl.BlockSpec((length, span), lambda i, *_: (0, i)),
                pl.BlockSpec((span, width), lambda i, *_: (i, 0)),
                pl.BlockSpec((8, span), lambda i, *_: (0, i)),
                whole(weight),
            ],
            out_specs=(
                pl.BlockSpec((LANES, span), lambda i, *_: (0, i)),
                pl.BlockSpec((8, span), lambda i, *_: (0, i)),
                fixed(half.shape),
                fixed(half.shape),
            ),
            scratch_shapes=[
                pltpu.VMEM((length, LANES), BF16),
                pltpu.VMEM((rows, span), BF16),
                pltpu.VMEM((rows, width), F32),
            ],
        ),
        compiler_params=params(),
        cost_estimate=cost(8 * FLOPS_US, 10e6),
        name="value_back",
    )(me, table, *grads, probs, normed, gates, weight)


def spread_weights(head, experts, weight_refs, scratch):
    scratch[...] = jnp.zeros_like(scratch)
    for j, weight_ref in enumerate(weight_refs):
        for e in range(experts):
            start = LANES * (experts * j + e)
            scratch[start : start + head, :] = weight_ref[e * head : (e + 1) * head, :]


def gate_spread(head, experts):
    shape = (LANES, experts * LANES)
    row = lax.broadcasted_iota(jnp.int32, shape, 0) - head
    block = lax.broadcasted_iota(jnp.int32, shape, 1) // LANES
    return ((row == block) | (row == block + experts)).astype(BF16)


def forward_body(head, experts, heads, place_ref, down_table_ref, up_table_ref, *refs):
    pair = 2
    attended_refs = [refs[part * heads : (part + 1) * heads] for part in range(pair)]
    rest = refs[pair * heads :]
    weight_refs = rest[0:heads]
    rest = rest[heads:]
    inputs_refs = rest[0:pair]
    cotangent_refs = rest[pair : 2 * pair]
    (
        up_ref,
        down_ref,
        gains_ref,
        biases_ref,
        resid_ref,
        grad_normed_ref,
        share_ref,
        down_keep_ref,
        down_send_ref,
        up_keep_ref,
        up_send_ref,
        weight_scratch,
        mixed_scratch,
        active_scratch,
        normed_scratch,
        upper_scratch,
        cotangent_scratch,
        down_acc,
        up_acc,
        up_scratch,
        down_scratch,
        weight_sems,
    ) = rest[2 * pair :]
    step = pl.program_id(0)
    final = pl.num_programs(0) - 1
    up_copy = pltpu.make_async_copy(up_ref, up_scratch, weight_sems.at[0])
    down_copy = pltpu.make_async_copy(down_ref, down_scratch, weight_sems.at[1])

    @pl.when(step == 0)
    def _():
        up_copy.start()
        down_copy.start()
        spread_weights(head, experts, weight_refs, weight_scratch)

    lane = lane_index(ROWS)
    spread = gate_spread(head, experts)
    for part in range(pair):
        piece = slice(part * ROWS, (part + 1) * ROWS)
        for j, attended_ref in enumerate(attended_refs[part]):
            packed = attended_ref[...]
            gate = dot_plain(packed, spread)
            attended = jnp.where(lane < head, packed.astype(F32), 0.0)
            for e in range(experts):
                start = LANES * (experts * j + e)
                mixed_scratch[piece, start : start + LANES] = (
                    attended * gate[:, e * LANES : (e + 1) * LANES]
                ).astype(BF16)
    pieces = [slice(part * ROWS, (part + 1) * ROWS) for part in range(pair)]
    state = [{} for _ in range(pair)]

    def mix(part):
        state[part]["mixed"] = dot_plain(mixed_scratch[pieces[part], :], weight_scratch[...])

    def grad_in(part):
        cotangent = cotangent_refs[part][...]
        cotangent_scratch[pieces[part], :] = cotangent
        state[part]["grad"] = dot_last(cotangent, down_scratch[...])

    def norm(part):
        resid = inputs_refs[part][...].astype(F32) + state[part]["mixed"]
        if part == 0:

            @pl.when(step == final)
            def _():
                resid_ref[...] = resid

        unit, _ = unit_rows(resid)
        normed = (unit * gains_ref[1:2, :] + biases_ref[1:2, :]).astype(BF16)
        normed_scratch[pieces[part], :] = normed
        state[part]["normed"] = normed

    def upper(part):
        state[part]["upper"] = dot_plain(state[part]["normed"], up_scratch[...])

    def activate(part):
        active, slope = gelu_parts(state[part]["upper"])
        active = active.astype(BF16)
        active_scratch[pieces[part], :] = active
        grad_upper = (state[part]["grad"] * slope).astype(BF16)
        upper_scratch[pieces[part], :] = grad_upper
        state[part]["active"] = active
        state[part]["grad_upper"] = grad_upper

    def leave(part):
        grad_normed_ref[part] = dot_last(state[part]["grad_upper"], up_scratch[...]).astype(BF16)
        share_ref[part] = dot_plain(state[part]["active"], down_scratch[...]).astype(BF16)

    mix(0)

    @pl.when(step == 0)
    def _():
        up_copy.wait()
        down_copy.wait()

    norm(0)
    grad_in(0)
    upper(0)
    mix(1)
    activate(0)
    norm(1)
    leave(0)
    grad_in(1)
    upper(1)
    activate(1)
    leave(1)
    down_grad = dot_first(active_scratch[...], cotangent_scratch[...])
    up_grad = dot_first(normed_scratch[...], upper_scratch[...])

    @pl.when(step == 0)
    def _():
        down_acc[...] = down_grad
        up_acc[...] = up_grad

    @pl.when(step > 0)
    def _():
        down_acc[...] += down_grad
        up_acc[...] += up_grad

    @pl.when(step == final)
    def _():
        for table_ref, acc, keep_ref, send_ref in (
            (down_table_ref, down_acc, down_keep_ref, down_send_ref),
            (up_table_ref, up_acc, up_keep_ref, up_send_ref),
        ):
            half, chunk, _ = keep_ref.shape
            for place in range(half):
                start = pl.multiple_of(table_ref[place] * chunk, chunk)
                keep_ref[place] = acc[pl.ds(start, chunk), :].astype(BF16)
                start = pl.multiple_of(table_ref[half + place] * chunk, chunk)
                send_ref[place] = acc[pl.ds(start, chunk), :].astype(BF16)


def forward_ffn(
    places,
    down_table,
    up_table,
    attended,
    weights,
    inputs,
    cotangent,
    up,
    down,
    gains,
    biases,
    experts,
):
    heads = len(attended)
    length, width = inputs.shape
    head = weights[0].shape[0] // experts
    hidden = up.shape[1]
    blocks = length // ROWS
    count = down_table.shape[0]
    chunk = hidden // count
    steps = blocks // 2
    place = lambda i, part: (steps - 1 - i) * 2 + part
    row = lambda size, part: pl.BlockSpec(
        (ROWS, size), lambda i, place_ref, *_: (place_ref[place(i, part)], 0)
    )
    relative = pl.BlockSpec((2, ROWS, width), lambda i, *_: (steps - 1 - i, 0, 0))
    half = lambda rows: jax.ShapeDtypeStruct((count // 2, rows, width), BF16)
    return pl.pallas_call(
        functools.partial(forward_body, head, experts, heads),
        out_shape=(
            jax.ShapeDtypeStruct((ROWS, width), F32),
            jax.ShapeDtypeStruct((blocks, ROWS, width), BF16),
            jax.ShapeDtypeStruct((blocks, ROWS, width), BF16),
            half(chunk),
            half(chunk),
            half(width // count),
            half(width // count),
        ),
        grid_spec=pltpu.PrefetchScalarGridSpec(
            num_scalar_prefetch=3,
            grid=(steps,),
            in_specs=[row(LANES, 0) for _ in attended]
            + [row(LANES, 1) for _ in attended]
            + [whole(weight) for weight in weights]
            + [row(width, 0), row(width, 1), row(width, 0), row(width, 1)]
            + [pl.BlockSpec(memory_space=pl.ANY), pl.BlockSpec(memory_space=pl.ANY)]
            + [whole(gains), whole(biases)],
            out_specs=(
                fixed((ROWS, width)),
                relative,
                relative,
                fixed((count // 2, chunk, width)),
                fixed((count // 2, chunk, width)),
                fixed((count // 2, width // count, hidden)),
                fixed((count // 2, width // count, hidden)),
            ),
            scratch_shapes=[
                pltpu.VMEM((heads * experts * LANES, width), BF16),
                pltpu.VMEM((2 * ROWS, heads * experts * LANES), BF16),
                pltpu.VMEM((2 * ROWS, hidden), BF16),
                pltpu.VMEM((2 * ROWS, width), BF16),
                pltpu.VMEM((2 * ROWS, hidden), BF16),
                pltpu.VMEM((2 * ROWS, width), BF16),
                pltpu.VMEM((hidden, width), F32),
                pltpu.VMEM((width, hidden), F32),
                pltpu.VMEM(up.shape, BF16),
                pltpu.VMEM(down.shape, BF16),
                pltpu.SemaphoreType.DMA((2,)),
            ],
        ),
        compiler_params=params(),
        cost_estimate=cost(28 * FLOPS_US, 30e6),
        name="forward_ffn",
    )(
        places,
        down_table,
        up_table,
        *attended,
        *attended,
        *weights,
        inputs,
        inputs,
        cotangent,
        cotangent,
        up,
        down,
        gains,
        biases,
    )


def second_norm_back_body(head, experts, heads, me_ref, *refs):
    attended_refs = refs[0:heads]
    weight_refs = refs[heads : 2 * heads]
    (
        left_ref,
        right_ref,
        resid_ref,
        cotangent_ref,
        gains_ref,
        grad_resid_ref,
        low_ref,
        packed_ref,
        sums_ref,
        weight_scratch,
        product_scratch,
    ) = refs[2 * heads :]
    spread_weights(head, experts, weight_refs, weight_scratch)
    unit, inverse = unit_rows(resid_ref[...])
    grad = left_ref[0].astype(F32) + right_ref[0].astype(F32)
    sums_ref[...] = jnp.zeros_like(sums_ref)
    sums_ref[2:3, :] = jnp.sum(grad * unit, axis=0, keepdims=True)
    sums_ref[3:4, :] = jnp.sum(grad, axis=0, keepdims=True)
    grad_resid = cotangent_ref[...].astype(F32) + norm_backward(
        grad, unit, inverse, gains_ref[1:2, :]
    )
    grad_resid_ref[...] = grad_resid
    low = grad_resid.astype(BF16)
    low_ref[0] = low
    grad_mixed = dot_last(low, weight_scratch[...])
    lane = lane_index(ROWS)
    spread = gate_spread(head, experts)
    collect = spread.T[:, 0:LANES]
    for j, attended_ref in enumerate(attended_refs):
        packed = attended_ref[...]
        gate = dot_plain(packed, spread)
        attended = jnp.where(lane < head, packed.astype(F32), 0.0)
        total = jnp.zeros((ROWS, LANES), F32)
        for e in range(experts):
            start = LANES * (experts * j + e)
            block = slice(e * LANES, (e + 1) * LANES)
            piece = grad_mixed[:, start : start + LANES]
            total = total + gate[:, block] * piece
            product_scratch[:, block] = piece * attended
        product = product_scratch[...]
        lead = product.astype(BF16)
        rest = (product - lead.astype(F32)).astype(BF16)
        logits = dot_plain(lead, collect) + dot_plain(rest, collect)
        own = packed.astype(F32)
        own = own + pltpu.roll(own, LANES - experts, 1)
        logits = logits * own * (1.0 - own)
        total = jnp.where((lane >= head) & (lane < head + experts), logits, total)
        packed_ref[j] = total.astype(BF16)


def second_norm_back(me, attended, weights, left, right, resid, cotangent, gains, experts):
    heads = len(attended)
    width = resid.shape[1]
    head = weights[0].shape[0] // experts
    own = lambda i, me_ref: (me_ref[0], 0)
    row = lambda size: pl.BlockSpec((ROWS, size), own)
    return pl.pallas_call(
        functools.partial(second_norm_back_body, head, experts, heads),
        out_shape=(
            jax.ShapeDtypeStruct((ROWS, width), F32),
            jax.ShapeDtypeStruct((1, ROWS, width), BF16),
            jax.ShapeDtypeStruct((heads, ROWS, LANES), BF16),
            jax.ShapeDtypeStruct((8, width), F32),
        ),
        grid_spec=pltpu.PrefetchScalarGridSpec(
            num_scalar_prefetch=1,
            grid=(1,),
            in_specs=[row(LANES) for _ in attended]
            + [whole(weight) for weight in weights]
            + [whole(left), whole(right), whole(resid), row(width), whole(gains)],
            out_specs=(
                fixed((ROWS, width)),
                fixed((1, ROWS, width)),
                fixed((heads, ROWS, LANES)),
                fixed((8, width)),
            ),
            scratch_shapes=[
                pltpu.VMEM((heads * experts * LANES, width), BF16),
                pltpu.VMEM((ROWS, experts * LANES), F32),
            ],
        ),
        compiler_params=params(),
        cost_estimate=cost(7 * FLOPS_US, 12e6),
        name="second_norm_back",
    )(me, *attended, *weights, left, right, resid, cotangent, gains)


def output_grad_body(
    head, experts, place_ref, table_ref, attended_ref, *refs
):
    blocks = place_ref.shape[0]
    grad_refs = refs[0:blocks]
    keep_ref, send_ref, mixed, rows, acc = refs[blocks:]
    half, chunk, _ = keep_ref.shape
    for place, grad_ref in enumerate(grad_refs):
        start = pl.multiple_of(place_ref[place] * ROWS, ROWS)
        packed = attended_ref[pl.ds(start, ROWS), :].astype(F32).T
        piece = slice(place * ROWS, (place + 1) * ROWS)
        for e in range(experts):
            gate = packed[head + e : head + e + 1, :] + packed[
                head + experts + e : head + experts + e + 1, :
            ]
            mixed[e * head : (e + 1) * head, piece] = (packed[0:head, :] * gate).astype(BF16)
        rows[piece, :] = grad_ref[0]
    mixed[experts * head :, :] = jnp.zeros_like(mixed[experts * head :, :])
    acc[...] = dot_plain(mixed[...], rows[...])
    for place in range(half):
        start = pl.multiple_of(table_ref[place] * chunk, 8)
        keep_ref[place] = acc[pl.ds(start, chunk), :].astype(BF16)
        start = pl.multiple_of(table_ref[half + place] * chunk, 8)
        send_ref[place] = acc[pl.ds(start, chunk), :].astype(BF16)


def output_grad(places, table, attended, grads, head, experts):
    count = table.shape[0]
    length = attended.shape[0]
    width = grads[0].shape[2]
    rows = experts * head
    rows = rows + -rows % (8 * count)
    chunk = rows // count
    half = jax.ShapeDtypeStruct((count // 2, chunk, width), BF16)
    return pl.pallas_call(
        functools.partial(output_grad_body, head, experts),
        out_shape=(half, half),
        grid_spec=pltpu.PrefetchScalarGridSpec(
            num_scalar_prefetch=2,
            grid=(1,),
            in_specs=[whole(attended)] + [whole(grad) for grad in grads],
            out_specs=(fixed(half.shape), fixed(half.shape)),
            scratch_shapes=[
                pltpu.VMEM((rows, length), BF16),
                pltpu.VMEM((length, width), BF16),
                pltpu.VMEM((rows, width), F32),
            ],
        ),
        compiler_params=params(),
        cost_estimate=cost(5 * FLOPS_US, 4e6),
        name="output_grad",
    )(places, table, attended, *grads)


def project_back_body(head, experts, place_ref, *refs):
    pair = 2
    groups = []
    for index in range(7):
        groups.append(refs[index * pair : (index + 1) * pair])
    grad_keys_refs, grad_values_refs, gate_refs, logit_refs, query_refs, memory_refs, inputs_refs = (
        groups
    )
    (
        key_ref,
        value_ref,
        value_router_ref,
        query_ref,
        output_router_ref,
        bias_sums_ref,
        counts_ref,
        grad_current_ref,
        sums_ref,
        extra_ref,
        weight_scratch,
        packed_scratch,
    ) = refs[7 * pair :]
    step = pl.program_id(0)
    split = LANES * (1 + experts)
    cur_steps = place_ref.shape[0] // pair
    current = step < cur_steps

    @pl.when(step == 0)
    def _():
        sums_ref[...] = jnp.zeros_like(sums_ref)
        extra_ref[...] = jnp.zeros_like(extra_ref)
        extra_ref[0:2, 0:LANES] = bias_sums_ref[0:2, :]
        extra_ref[2:4, 0:LANES] = counts_ref[0:2, :]
        weight_scratch[...] = jnp.zeros_like(weight_scratch)
        packed_scratch[...] = jnp.zeros_like(packed_scratch)
        fill_weights(head, experts, key_ref, value_router_ref, value_ref, weight_scratch)
        weight_scratch[split : split + head, :] = query_ref[...]
        weight_scratch[split + head : split + head + experts, :] = output_router_ref[...]

    for part in range(pair):
        piece = slice(part * ROWS, (part + 1) * ROWS)
        grad_values = grad_values_refs[part][0:head, :]
        packed_scratch[0:head, piece] = grad_keys_refs[part][0:head, :]
        packed_scratch[head : head + 8, piece] = logit_refs[part][...].astype(BF16)
        for e in range(experts):
            start = LANES * (e + 1)
            gate = gate_refs[part][e : e + 1, :]
            packed_scratch[start : start + head, piece] = (gate * grad_values).astype(BF16)
    grads = dot_first(packed_scratch[...], weight_scratch[0:split, :])
    for part in range(pair):
        piece = slice(part * ROWS, (part + 1) * ROWS)
        grad = grads[piece, :]
        more = dot_plain(query_refs[part][...], weight_scratch[split:, :])
        grad = grad + jnp.where(current, more, 0.0)
        rows = jnp.where(current, inputs_refs[part][...], memory_refs[part][...]).astype(F32)
        unit, _ = unit_rows(rows)
        sums_ref[0:1, :] += jnp.sum(grad * unit, axis=0, keepdims=True)
        sums_ref[1:2, :] += jnp.sum(grad, axis=0, keepdims=True)

        @pl.when(current)
        def _():
            grad_current_ref[part] = grad.astype(BF16)


def project_back(
    places,
    grad_keys,
    grad_values,
    gates,
    logits,
    grad_query,
    memory,
    inputs,
    key_weight,
    value_weight,
    value_router,
    query_weight,
    output_router,
    bias_sums,
    counts,
):
    keys = grad_keys.shape[1]
    length, width = inputs.shape
    head = key_weight.shape[0]
    experts = value_router.shape[0]
    mem_blocks = (keys - length) // ROWS
    cur_blocks = length // ROWS
    cur_steps = cur_blocks // 2
    split = LANES * (1 + experts)
    fresh = lambda i, part, place_ref: place_ref[2 * jnp.minimum(i, cur_steps - 1) + part]
    past = lambda i, part, place_ref: 2 * jnp.maximum(i - cur_steps, 0) + part
    every = lambda i, part, place_ref: jnp.where(
        i < cur_steps, fresh(i, part, place_ref) + mem_blocks, past(i, part, place_ref)
    )

    def rows(size, index):
        return [
            pl.BlockSpec((ROWS, size), lambda i, place_ref, p=part: (index(i, p, place_ref), 0))
            for part in range(2)
        ]

    def columns(size):
        return [
            pl.BlockSpec((size, ROWS), lambda i, place_ref, p=part: (0, every(i, p, place_ref)))
            for part in range(2)
        ]

    twice = lambda *arrays: [array for array in arrays for _ in range(2)]
    weights = [key_weight, value_weight, value_router, query_weight, output_router]
    return pl.pallas_call(
        functools.partial(project_back_body, head, experts),
        out_shape=(
            jax.ShapeDtypeStruct((cur_blocks, ROWS, width), BF16),
            jax.ShapeDtypeStruct((8, width), F32),
            jax.ShapeDtypeStruct((8, width), F32),
        ),
        grid_spec=pltpu.PrefetchScalarGridSpec(
            num_scalar_prefetch=1,
            grid=(keys // (2 * ROWS),),
            in_specs=columns(LANES)
            + columns(LANES)
            + columns(8)
            + columns(8)
            + rows(LANES, fresh)
            + rows(width, past)
            + rows(width, fresh)
            + [whole(weight) for weight in weights]
            + [whole(bias_sums), whole(counts)],
            out_specs=(
                pl.BlockSpec(
                    (2, ROWS, width), lambda i, *_: (jnp.minimum(i, cur_steps - 1), 0, 0)
                ),
                fixed((8, width)),
                fixed((8, width)),
            ),
            scratch_shapes=[
                pltpu.VMEM((split + LANES, width), BF16),
                pltpu.VMEM((split, 2 * ROWS), BF16),
            ],
        ),
        compiler_params=params(),
        cost_estimate=cost(12 * FLOPS_US, 15e6),
        name="project_back",
    )(
        places,
        *twice(grad_keys, grad_values, gates, logits, grad_query, memory, inputs),
        *weights,
        bias_sums,
        counts,
    )


def first_norm_back(me, left, right, inputs, grad_resid, gains):
    width = inputs.shape[1]

    def body(me_ref, left_ref, right_ref, inputs_ref, resid_ref, gains_ref, out_ref):
        unit, inverse = unit_rows(inputs_ref[...].astype(F32))
        grad = left_ref[0].astype(F32) + right_ref[0].astype(F32)
        out_ref[0] = (
            resid_ref[...] + norm_backward(grad, unit, inverse, gains_ref[0:1, :])
        ).astype(BF16)

    return pl.pallas_call(
        body,
        out_shape=jax.ShapeDtypeStruct((1, ROWS, width), BF16),
        grid_spec=pltpu.PrefetchScalarGridSpec(
            num_scalar_prefetch=1,
            grid=(1,),
            in_specs=[
                whole(left),
                whole(right),
                pl.BlockSpec((ROWS, width), lambda i, me_ref: (me_ref[0], 0)),
                whole(grad_resid),
                whole(gains),
            ],
            out_specs=fixed((1, ROWS, width)),
        ),
        compiler_params=params(),
        cost_estimate=cost(3 * FLOPS_US, 4e6),
        name="first_norm_back",
    )(me, left, right, inputs, grad_resid, gains)


def place_rows(places, pieces):
    _, rows, width = pieces[0].shape
    count = len(pieces)

    def body(place_ref, *refs):
        out_ref = refs[count]
        for place in range(count):
            start = pl.multiple_of(place_ref[place] * rows, rows)
            out_ref[pl.ds(start, rows), :] = refs[place][0]

    return pl.pallas_call(
        body,
        out_shape=jax.ShapeDtypeStruct((count * rows, width), pieces[0].dtype),
        grid_spec=pltpu.PrefetchScalarGridSpec(
            num_scalar_prefetch=1,
            grid=(1,),
            in_specs=[whole(piece) for piece in pieces],
            out_specs=fixed((count * rows, width)),
        ),
        compiler_params=params(),
        cost_estimate=cost(3 * FLOPS_US, 4e6),
        name="place_rows",
    )(places, *pieces)


def unpack_rows(table, own, got, rows_out, more=0):
    half, rows, width = own.shape
    total = 2 * half * rows
    part = width // 2

    def body(table_ref, own_ref, got_ref, out_ref, *rest):
        scratch = rest[1:] if more else rest
        rows_ref = scratch[0] if scratch else out_ref
        for place in range(half):
            start = pl.multiple_of(table_ref[place] * rows, 8)
            rows_ref[pl.ds(start, rows), :] = own_ref[place].astype(F32)
            start = pl.multiple_of(table_ref[half + place] * rows, 8)
            rows_ref[pl.ds(start, rows), :] = got_ref[place].astype(F32)
        if scratch:
            out_ref[...] = rows_ref[0:rows_out, :]
        if more:
            rest[0][...] = rows_ref[rows_out : rows_out + more, :]

    shapes = [jax.ShapeDtypeStruct((rows_out, width), F32)]
    if more:
        shapes.append(jax.ShapeDtypeStruct((more, width), F32))
    chunks = pl.BlockSpec((half, rows, part), lambda i, _: (0, 0, i))
    return pl.pallas_call(
        body,
        out_shape=tuple(shapes),
        grid_spec=pltpu.PrefetchScalarGridSpec(
            num_scalar_prefetch=1,
            grid=(2,),
            in_specs=[chunks, chunks],
            out_specs=tuple(
                pl.BlockSpec((shape.shape[0], part), lambda i, _: (0, i)) for shape in shapes
            ),
            scratch_shapes=[] if total == rows_out else [pltpu.VMEM((total, part), F32)],
        ),
        compiler_params=params(),
        cost_estimate=cost(5 * FLOPS_US, 6e6),
        name="unpack_rows",
    )(table, own, got)


def unpack_heads(table, own, got, head, experts):
    half, chunk, width = own.shape

    def body(
        table_ref,
        own_ref,
        got_ref,
        key_ref,
        query_ref,
        output_router_ref,
        position_ref,
        rows,
    ):
        for place in range(half):
            start = pl.multiple_of(table_ref[place] * chunk, 8)
            rows[pl.ds(start, chunk), :] = own_ref[place].astype(F32)
            start = pl.multiple_of(table_ref[half + place] * chunk, 8)
            rows[pl.ds(start, chunk), :] = got_ref[place].astype(F32)
        key_ref[...] = rows[0:head, :]
        query_ref[...] = rows[LANES : LANES + head, :]
        output_router_ref[...] = rows[LANES + head : LANES + head + experts, :]
        position_ref[...] = rows[2 * LANES : 2 * LANES + head, :]

    one = jax.ShapeDtypeStruct((head, width), F32)
    few = jax.ShapeDtypeStruct((experts, width), F32)
    return pl.pallas_call(
        body,
        out_shape=(one, one, few, one),
        grid_spec=pltpu.PrefetchScalarGridSpec(
            num_scalar_prefetch=1,
            grid=(1,),
            in_specs=[whole(own), whole(got)],
            out_specs=tuple(fixed(kind.shape) for kind in (one, one, few, one)),
            scratch_shapes=[pltpu.VMEM((2 * half * chunk, width), F32)],
        ),
        compiler_params=params(),
        cost_estimate=cost(3 * FLOPS_US, 3e6),
        name="unpack_heads",
    )(table, own, got)


def unpack_small(me, norms, extra, head, share):
    def body(
        me_ref,
        norms_ref,
        extra_ref,
        gains_ref,
        biases_ref,
        content_ref,
        position_ref,
        counts_ref,
    ):
        start = pl.multiple_of(me_ref[0] * share, LANES)
        gains_ref[0:1, :] = norms_ref[0:1, pl.ds(start, share)]
        gains_ref[1:2, :] = norms_ref[2:3, pl.ds(start, share)]
        biases_ref[0:1, :] = norms_ref[1:2, pl.ds(start, share)]
        biases_ref[1:2, :] = norms_ref[3:4, pl.ds(start, share)]
        content_ref[...] = extra_ref[0:1, 0:head]
        position_ref[...] = extra_ref[1:2, 0:head]
        counts_ref[...] = extra_ref[2:4, 0:LANES].astype(jnp.int32)

    shapes = (
        ((2, share), F32),
        ((2, share), F32),
        ((1, head), F32),
        ((1, head), F32),
        ((2, LANES), jnp.int32),
    )
    return pl.pallas_call(
        body,
        out_shape=tuple(jax.ShapeDtypeStruct(shape, kind) for shape, kind in shapes),
        grid_spec=pltpu.PrefetchScalarGridSpec(
            num_scalar_prefetch=1,
            grid=(1,),
            in_specs=[whole(norms), whole(extra)],
            out_specs=tuple(fixed(shape) for shape, _ in shapes),
        ),
        cost_estimate=cost(2 * FLOPS_US, 1e6),
        name="unpack_small",
    )(me, norms, extra)


def on_device(
    inputs,
    memory,
    memory_positions,
    value_routes,
    output_routes,
    norm_gains,
    norm_biases,
    query_weight,
    key_weight,
    value_weight,
    value_router,
    output_router,
    output_weight,
    position_weight,
    content_bias,
    position_bias,
    up_weight,
    down_weight,
    cotangent,
):
    length, width = inputs.shape[1:]
    mem_count = memory.shape[1]
    keys = mem_count + length
    head = query_weight.shape[1]
    experts = value_router.shape[1]
    pos_width = position_weight.shape[0]
    picks = value_routes.shape[3]
    t_index = lax.axis_index("tensor")
    me = t_index.reshape(1).astype(jnp.int32)
    t_bits = axis_bits("tensor")
    t_order = relative_order(t_bits)
    t_table = chunk_table(t_bits, "tensor")
    t_count = lax.axis_size("tensor")
    core_bit, chip_bit = t_bits
    all_bits = axis_bits("dp")
    first_bits = all_bits[:SPLITS]
    second_bits = [first_bits[1], first_bits[0]] + first_bits[2:]
    first_table = chunk_table(first_bits, "dp")
    second_table = chunk_table(second_bits, "dp")

    def bits_of(name):
        return second_bits if name in SECOND else first_bits

    def table_of(name):
        return second_table if name in SECOND else first_table

    tokens = inputs.reshape(length, width)
    upstream = cotangent.reshape(length, width)
    past = memory.reshape(mem_count, width)
    key_t = key_weight.T
    value_t = value_weight.T
    value_router_t = value_router.T
    query_t = query_weight.T
    output_router_t = output_router.T
    position_t = position_weight.T

    far_weight = swap(output_weight, "tensor", chip_bit)
    coarse = trig_tables(-2.0 * mem_count, (2 * mem_count + length) // FINE, float(FINE), pos_width)
    fine = trig_tables(0.0, FINE, 1.0, pos_width)
    (
        normed,
        key_cat,
        values,
        gates,
        content_query,
        bias_query,
        counts,
        probs,
        attended_own,
    ) = front(
        past,
        tokens,
        norm_gains,
        norm_biases,
        key_t,
        value_t,
        value_router_t,
        query_t,
        output_router_t,
        position_t,
        content_bias.reshape(1, head),
        position_bias.reshape(1, head),
        value_routes.reshape(keys, picks).T,
        output_routes.reshape(length, picks).T,
        memory_positions,
        coarse,
        fine,
    )

    totals = {}
    v = {}
    token = [attended_own]

    def tie(value):
        return after(value, *token)

    def core_sum(held, got):
        half = held.shape[0] // 2
        return add_pieces(held[:1], got[:1]), add_pieces(held[1:half], got[1:])

    def for_core(held):
        return swap(held[held.shape[0] // 2 :], "tensor", core_bit)

    far_attended = swap(attended_own, "tensor", chip_bit)
    near_attended = swap(attended_own, "tensor", core_bit)
    far_weight = after(far_weight, attended_own)
    near_weight = swap(after(output_weight, attended_own), "tensor", core_bit)
    across_weight = swap(far_weight, "tensor", core_bit)
    across_attended = swap(far_attended, "tensor", core_bit)
    attended = [attended_own, far_attended, near_attended, across_attended]
    weights = [output_weight, far_weight, near_weight, across_weight]

    def feed_forward():
        (
            v["resid"],
            v["grad_normed"],
            v["share"],
            down_keep,
            down_send,
            up_keep,
            up_send,
        ) = forward_ffn(
            tie(t_table),
            table_of("down"),
            table_of("up"),
            attended,
            weights,
            tokens,
            upstream,
            up_weight,
            down_weight,
            norm_gains,
            norm_biases,
            experts,
        )
        v["grad_normed_got"] = for_core(v["grad_normed"])
        totals["F"] = DpSum(
            [(down_keep, down_send, bits_of("down")), (up_keep, up_send, bits_of("up"))]
        )
        return down_keep

    def grad_normed_add():
        v["left"], far = core_sum(v["grad_normed"], tie(v["grad_normed_got"]))
        v["right"] = swap(far, "tensor", chip_bit)
        return far

    def share_core():
        v["share"] = tie(v["share"])
        v["share_got"] = for_core(v["share"])
        return None

    def share_add():
        v["share_left"], far = core_sum(v["share"], tie(v["share_got"]))
        v["share_right"] = swap(far, "tensor", chip_bit)
        return far

    def second_norm():
        v["grad_resid"], low_own, packed, v["sums_two"] = second_norm_back(
            tie(me),
            attended,
            weights,
            v["left"],
            v["right"],
            v["resid"],
            upstream,
            norm_gains,
            experts,
        )
        arrived = [None] * t_count
        for place, distance in enumerate(t_order):
            piece = packed[place : place + 1]
            arrived[distance] = piece if distance == 0 else swap(piece, "tensor", distance)
        v["arrived"] = arrived
        v["low"] = [
            low_own,
            swap(low_own, "tensor", chip_bit),
            swap(low_own, "tensor", core_bit),
        ]
        return low_own

    def low_across():
        far = tie(v["low"][1])
        v["low"][1] = far
        v["low"].append(swap(far, "tensor", core_bit))
        return far

    def start_pair():
        if "value_part" in v and "out_part" in v:
            totals["W"] = DpSum([v["value_part"], v["out_part"]])

    def value_grads():
        v["grad_values"], v["logits"], keep, send = value_back(
            tie(me),
            table_of("value"),
            v["arrived"],
            probs,
            normed,
            gates,
            value_t,
            head,
            experts,
        )
        v["value_part"] = (keep, send, bits_of("value"))
        start_pair()
        return v["grad_values"]

    def attention():
        v["grad_keys"], v["grad_query"], keep, send, v["bias_sums"] = attend_back(
            tie(me),
            table_of("late"),
            v["arrived"],
            probs,
            attended_own,
            key_cat,
            values,
            content_query,
            bias_query,
            coarse,
            fine,
            position_t,
            normed,
        )
        totals["L"] = DpSum([(keep, send, bits_of("late"))])
        return v["bias_sums"]

    def output_weight_grad():
        keep, send = output_grad(
            tie(t_table), table_of("out"), attended_own, v["low"], head, experts
        )
        v["out_part"] = (keep, send, bits_of("out"))
        start_pair()
        return send

    def projections():
        v["grad_current"], v["sums_one"], v["extra"] = project_back(
            tie(t_table),
            v["grad_keys"],
            v["grad_values"],
            gates,
            v["logits"],
            v["grad_query"],
            past,
            tokens,
            key_t,
            value_t,
            value_router_t,
            query_t,
            output_router_t,
            v["bias_sums"],
            counts,
        )
        v["grad_current_got"] = for_core(v["grad_current"])
        return v["extra"]

    def grad_current_add():
        v["left"], far = core_sum(v["grad_current"], tie(v["grad_current_got"]))
        v["right"] = swap(far, "tensor", chip_bit)
        return far

    def first_norm():
        own = first_norm_back(
            tie(me), v["left"], v["right"], tokens, v["grad_resid"], norm_gains
        )
        v["grad_inputs"] = [
            own,
            swap(own, "tensor", chip_bit),
            swap(own, "tensor", core_bit),
        ]
        return own

    def rows_across(name):
        far = tie(v[name][1])
        v[name][1] = far
        v[name].append(swap(far, "tensor", core_bit))
        return far

    def rows_placed(name):
        v[name] = place_rows(tie(t_table), v[name])
        return v[name]

    def output_rows():
        own = (
            v["resid"][None]
            + v["share_left"].astype(F32)
            + tie(v["share_right"]).astype(F32)
        ).astype(BF16)
        v["output"] = [
            own,
            swap(own, "tensor", chip_bit),
            swap(own, "tensor", core_bit),
        ]
        return own

    def small_sum(stage):
        if stage == 0:
            total = tie(v["sums_one"]) + v["sums_two"]
            v["small_got"] = swap(total, "tensor", core_bit)
        else:
            total = v["small"] + tie(v["small_got"])
            if stage == 1:
                v["small_got"] = swap(total, "tensor", chip_bit)
            elif stage < 2 + len(all_bits):
                if stage == 2:
                    total = jnp.concatenate([total, v["extra"]], axis=0)
                v["small_got"] = swap(total, "dp", all_bits[stage - 2])
        v["small"] = total
        return total

    def small_placed():
        for stage in range(2 + len(axis_bits("dp")[:SPLITS]), 3 + len(all_bits)):
            small_sum(stage)
        small = v["small"]
        v["small_out"] = unpack_small(
            me, small[0:8], small[8:], head, width // t_count
        )
        return v["small_out"][0]

    def sum_placed(name, rows, total, part, more=0):
        total = totals[total]
        v[name] = unpack_rows(
            tie(table_of(name)), total.keep[part], total.got[part], rows, more
        )
        return v[name][0]

    def late_placed():
        total = totals["L"]
        v["late"] = unpack_heads(
            tie(table_of("late")), total.keep[0], total.got[0], head, experts
        )
        return v["late"][2]

    tasks = {
        "ffn": feed_forward,
        "sh": share_core,
        "sha": share_add,
        "oc": lambda: rows_across("output"),
        "gi": lambda: rows_across("grad_inputs"),
        "pro": lambda: rows_placed("output"),
        "pri": lambda: rows_placed("grad_inputs"),
        "gna": grad_normed_add,
        "snb": second_norm,
        "low": low_across,
        "vb": value_grads,
        "ab": attention,
        "og": output_weight_grad,
        "pb": projections,
        "gca": grad_current_add,
        "fnb": first_norm,
        "orow": output_rows,
        "nu": small_placed,
        "Du": lambda: sum_placed("down", down_weight.shape[0], "F", 0),
        "Uu": lambda: sum_placed("up", up_weight.shape[0], "F", 1),
        "Vu": lambda: sum_placed("value", experts * head, "W", 0, experts),
        "Ou": lambda: sum_placed("out", experts * head, "W", 1),
        "Lu": late_placed,
    }
    for stage in range(5):
        tasks["n" + str(stage)] = functools.partial(small_sum, stage)
    for name in ORDER:
        if name in tasks:
            done = tasks[name]()
        else:
            done = totals[name[0]].step(*token)
        if done is not None:
            token = list(done) if isinstance(done, list) else [done]

    grad_gains, grad_biases, grad_content, grad_position, expert_counts = v["small_out"]
    grad_key_t, grad_query_t, grad_output_router, grad_position_t = v["late"]
    grad_value_t, grad_value_router = v["value"]
    return (
        v["output"].reshape(1, length, width),
        v["grad_inputs"].reshape(1, length, width),
        grad_gains,
        grad_biases,
        grad_query_t.T,
        grad_key_t.T,
        grad_value_t.T,
        grad_value_router.T,
        grad_output_router.T,
        v["out"][0],
        grad_position_t.T,
        grad_content.reshape(head),
        grad_position.reshape(head),
        v["up"][0],
        v["down"][0],
        expert_counts[:, head : head + experts],
    )


def solution(mesh):
    placed = (
        P("dp", None, None),
        P("dp", None, None),
        P("dp", None),
        P("dp", None, "tensor", None),
        P("dp", None, "tensor", None),
        P(),
        P(),
        P(None, "tensor"),
        P(None, "tensor"),
        P(None, "tensor"),
        P(None, "tensor"),
        P(None, "tensor"),
        P("tensor", None),
        P(None, "tensor"),
        P("tensor"),
        P("tensor"),
        P(None, "tensor"),
        P("tensor", None),
        P("dp", None, None),
    )
    return jax.shard_map(
        on_device,
        mesh=mesh,
        in_specs=placed,
        out_specs=(
            P("dp", None, None),
            P("dp", None, None),
            P(None, "tensor"),
            P(None, "tensor"),
            P(None, "tensor"),
            P(None, "tensor"),
            P(None, "tensor"),
            P(None, "tensor"),
            P(None, "tensor"),
            P("tensor", None),
            P(None, "tensor"),
            P("tensor"),
            P("tensor"),
            P(None, "tensor"),
            P("tensor", None),
            P(None, "tensor"),
        ),
        check_vma=False,
    )
```
